32 devices in a mesh: dp: 8 (over z, core), tp: 4 (over y, x).
Axes of the slice: x: 2, y: 2, z: 4, core: 2. Of those that a mesh axis runs over, the one named last changes fastest.
Arguments:
- block_in: bfloat16 [3, 4096, 2048], P(None, ('dp', 'tp')), may hold values from -6 to 6
- cotangent: bfloat16 [3, 4096, 2048], P(None, ('dp', 'tp')), may hold values from -6 to 6
- segments: int32 [3, 4096], replicated, may hold values from 0 to 4095, as said below
- master: float32 [20736, 2048], P('tp', 'dp')
- moment_one: float32 [20736, 2048], P('tp', 'dp'), may hold values from -6 to 6
- moment_two: float32 [20736, 2048], P('tp', 'dp'), may hold values from 1 to 1000
- vectors: float32 [22656], replicated
- vec_one: float32 [22656], replicated, may hold values from -6 to 6
- vec_two: float32 [22656], replicated, may hold values from 1 to 1000
- step_count: int32 [1], replicated, may hold values from 1 to 9
- learning_rate: float32 [1], replicated, may hold values from 0.1 to 0.4
Outputs:
- block_out: bfloat16 [3, 4096, 2048], P(None, ('dp', 'tp'))
- grad_in: bfloat16 [3, 4096, 2048], P(None, ('dp', 'tp'))
- new_master: float32 [20736, 2048], P('tp', 'dp')
- new_moment_one: float32 [20736, 2048], P('tp', 'dp')
- new_moment_two: float32 [20736, 2048], P('tp', 'dp')
- new_vectors: float32 [22656], replicated
- new_vec_one: float32 [22656], replicated
- new_vec_two: float32 [22656], replicated
The draws below stay inside these ranges and needn't reach their ends.
Inputs may be any that keep to these rules, and one draw needn't show every extreme that they name: `segments`: A token's id is the index, within its micro-batch, of its document's first token, so ids never fall along the tokens. Packed sequences begin at token 0 and at every token 1024 + k * 2048; a new document begins at each of them, so no document spans two sequences. The last token of each micro-batch is a document of its own.
All inputs are finite; a program needn't handle non-finite values.
Results may differ from the reference program's by a relative error of at most 0.015.
The reference program's roundings to bfloat16 on the way count: a program that leaves them out, or rounds other values in their place, can miss the bound.
Values may be sent and summed in bfloat16 or wider, within the bound.
No kernel may reach another device: no remote copies, remote signals or barrier semaphores. Data moves between devices by JAX's collectives and lax.ppermute only.
A program may use at most 384 MiB of HBM per device.

```python
import math
import jax
import jax.numpy as jnp
from jax import lax

D = 2048
H = 16
HD = 128
FF = 8192
TOK_DEV = 512
MB = 3
SEQ = 2048
TOKENS = 4096
ROWS_ALL = 20736
NVEC = 22656
N_TP = 4


def draw_master(key, part):
    rows_tp = ROWS_ALL // N_TP
    query_rows = H * HD // N_TP
    kv_share = 2 * HD // N_TP
    ff_rows = FF // N_TP
    position = jnp.arange(ROWS_ALL) % rows_tp
    row_scale = jnp.where(position < query_rows + kv_share, D ** (-0.5), jnp.where(position < 2 * query_rows + kv_share, (H * HD // 16) ** (-0.5), jnp.where(position < 2 * query_rows + kv_share + ff_rows, D ** (-0.5), FF ** (-0.5))))
    return jax.random.normal(key, (ROWS_ALL, D), jnp.float32) * row_scale[:, None].astype(jnp.float32)


def draw_vectors(key, part):
    position = jnp.arange(NVEC)
    gain_start = 3 * D + H * HD + HD
    is_gain = (position < D) | (position >= gain_start) & (position < gain_start + D)
    gain_key = jax.random.fold_in(key, 11)
    bias_key = jax.random.fold_in(key, 12)
    gain_vals = jax.random.uniform(gain_key, (NVEC,), jnp.float32, 0.6, 1.4)
    bias_vals = jax.random.normal(bias_key, (NVEC,), jnp.float32) * 0.3
    return jnp.where(is_gain, gain_vals, bias_vals)


def draw_segments(key, part):
    stretch_count = TOKENS // TOK_DEV
    rate_key = jax.random.fold_in(key, 1)
    start_key = jax.random.fold_in(key, 2)
    rate_bits = jax.random.randint(rate_key, (MB, stretch_count, 1), 4, SEQ.bit_length() + 1)
    coin_flips = jax.random.randint(start_key, (MB, stretch_count, TOK_DEV), 0, 1 << 20)
    starts = (coin_flips < jnp.right_shift(jnp.int32(1 << 20), rate_bits)).reshape(MB, TOKENS)
    token_pos = jnp.arange(TOKENS, dtype=jnp.int32)[None, :]
    stretch_of = token_pos // TOK_DEV
    at_stretch = token_pos % TOK_DEV == 0
    seq_begin = at_stretch & ((stretch_of + 2) % 4 == 0) | (token_pos == 0)
    starts = starts & jnp.logical_not(at_stretch) | seq_begin | (token_pos == TOKENS - 1)
    marked = jnp.where(starts, token_pos, jnp.int32(0)).astype(jnp.int32)
    return lax.cummax(marked, axis=1).astype(jnp.int32)


def shard_levels(stream_key, extent, cuts, smallest, high):
    level = 1.0
    for dim, blocks in cuts:
        steps = jax.random.uniform(jax.random.fold_in(jax.random.fold_in(stream_key, 6), dim), (blocks,), jnp.float32, smallest / len(cuts), high / len(cuts))
        level = level * jnp.repeat(jnp.exp(steps), extent[dim] // blocks).reshape((-1,) + (1,) * (len(extent) - 1 - dim))
    return level


def gaussian(rng, shape, width, limit, cuts=(), kind=jnp.bfloat16):
    entries = jax.random.normal(rng, shape, jnp.float32) * width
    if len(cuts) > 0:
        entries = shard_levels(rng, shape, cuts, -0.22, 0.18) * entries
    return jnp.clip(entries, min=-limit, max=limit).astype(kind)


def setup_inputs(seed: int = 0) -> dict:
    seeds = jax.random.split(jax.random.key(seed), 12)
    return {
        "block_in": gaussian(seeds[0], (MB, TOKENS, D), 1.0, 6.0, ((1, 32),)),
        "cotangent": gaussian(seeds[1], (MB, TOKENS, D), 1.0, 6.0, ((1, 32),)),
        "segments": draw_segments(jax.random.fold_in(seeds[11], 71), 0),
        "master": draw_master(jax.random.fold_in(seeds[11], 71), 0),
        "moment_one": gaussian(seeds[4], (ROWS_ALL, D), 1.0, 6.0, ((0, 4), (1, 8)), jnp.float32),
        "moment_two": jnp.clip(jnp.exp(math.log(1000.0) - 6.9077553 * jax.random.uniform(seeds[5], (ROWS_ALL, D), jnp.float32) ** shard_levels(seeds[5], (ROWS_ALL, D), ((0, 4), (1, 8)), -0.2, 0.2)), 1.0, 1000.0),
        "vectors": draw_vectors(jax.random.fold_in(seeds[11], 71), 0),
        "vec_one": gaussian(seeds[7], (NVEC,), 1.0, 6.0, (), jnp.float32),
        "vec_two": jnp.clip(jnp.exp(jax.random.uniform(seeds[8], (NVEC,), jnp.float32, math.log(1.0), math.log(1000.0))), 1.0, 1000.0),
        "step_count": jax.random.randint(seeds[9], (1,), 1, 10).astype(jnp.int32),
        "learning_rate": jnp.clip(jax.random.uniform(seeds[10], (1,), jnp.float32, 0.1, 0.4), 0.1, 0.4),
    }


@jax.custom_vjp
def low(v):
    return lax.optimization_barrier(v.astype(jnp.bfloat16)).astype(jnp.float32)

@jax.custom_vjp
def low_back(v):
    return v

def low_keep(v):
    return (low(v), None)

def low_pass(kept, grad):
    return (grad,)

def back_keep(v):
    return (v, None)

def back_low(kept, grad):
    return (low(grad),)
low.defvjp(low_keep, low_pass)
low_back.defvjp(back_keep, back_low)
norm_eps = 1e-05
gelu_coef = math.sqrt(2.0 / math.pi)
beta_one = 0.9
beta_two = 0.95
adam_eps = 1e-08
decay_rate = 0.1
masked_score = -1e+30
top_precision = lax.Precision.HIGHEST

def layer_norm(values, gain, shift):
    mean_row = lax.optimization_barrier(jnp.mean(values, -1, keepdims=True))
    centered = values - mean_row
    var_row = lax.optimization_barrier(jnp.mean(centered * centered, -1, keepdims=True))
    return centered * lax.rsqrt(var_row + norm_eps) * gain + shift

def gelu_tanh(values):
    inner = gelu_coef * (values + 0.044715 * values * values * values)
    return 0.5 * values * (1.0 + jnp.tanh(inner))

def matmul_rows(left, right):
    return jnp.dot(left, right.T, precision=top_precision, preferred_element_type=jnp.float32)

def split_master(weights):
    blocks = weights.reshape(N_TP, ROWS_ALL // N_TP, D)
    query_rows = H * HD // N_TP
    kv_share = 2 * HD // N_TP
    ff_rows = FF // N_TP
    bounds = [query_rows, kv_share, query_rows, ff_rows, ff_rows]
    pieces = []
    row_start = 0
    for length in bounds:
        pieces.append(blocks[:, row_start:row_start + length].reshape(N_TP * length, D))
        row_start += length
    return pieces

def vector_sizes():
    return [D, D, H * HD, HD, D, D, D, FF, D]

def split_vectors(flat):
    pieces = []
    cursor = 0
    for length in vector_sizes():
        pieces.append(flat[cursor:cursor + length])
        cursor += length
    return pieces

def attend_sequence(inputs):
    queries, keyvals, seg_ids = inputs
    key_part = keyvals[:, :HD]
    value_part = keyvals[:, HD:]
    scores = jnp.einsum('qhd,kd->hqk', queries, key_part, precision=top_precision) * (1.0 / math.sqrt(HD))
    scores = low_back(scores)
    positions = jnp.arange(SEQ)
    allowed = (seg_ids[:, None] == seg_ids[None, :]) & (positions[None, :] <= positions[:, None])
    scores = jnp.where(allowed[None], scores, masked_score)
    row_peak = lax.optimization_barrier(jnp.max(scores, -1, keepdims=True))
    exp_scores = jnp.exp(scores - row_peak)
    probs = exp_scores / lax.optimization_barrier(jnp.sum(exp_scores, -1, keepdims=True))
    probs = low(probs)
    return jnp.einsum('hqk,kd->qhd', probs, value_part, precision=top_precision)

def adam_step(weights, grads, first, second, step_count, learning_rate):
    steps_float = step_count[0].astype(jnp.float32)
    first_new = beta_one * first + (1.0 - beta_one) * grads
    second_new = beta_two * second + (1.0 - beta_two) * grads * grads
    corr_one = 1.0 - jnp.power(beta_one, steps_float)
    corr_two = 1.0 - jnp.power(beta_two, steps_float)
    update = first_new / corr_one / (jnp.sqrt(second_new / corr_two) + adam_eps)
    return (weights - learning_rate[0] * (update + decay_rate * weights), first_new, second_new)

def reference(block_in, cotangent, segments, master, moment_one, moment_two, vectors, vec_one, vec_two, step_count, learning_rate):
    seq_count = TOKENS // SEQ
    offset_rows = 2 * TOK_DEV

    def forward(master_f, vectors_f, block_f):
        w_query, w_keyval, w_out, w_up, w_down = split_master(low(master_f))
        gain_one, shift_one, bias_query, bias_value, bias_out, gain_two, shift_two, bias_up, bias_down = split_vectors(vectors_f)
        keyval_bias = jnp.concatenate([jnp.zeros((HD,), jnp.float32), bias_value])

        def one_batch(inputs):
            block_rows, seg_ids = inputs
            hidden_one = low(layer_norm(block_rows, gain_one, shift_one))
            queries = low(low_back(matmul_rows(hidden_one, w_query) + bias_query))
            keyvals = low(low_back(matmul_rows(hidden_one, w_keyval) + keyval_bias))
            rolled_q = jnp.roll(queries, -offset_rows, 0)
            rolled_kv = jnp.roll(keyvals, -offset_rows, 0)
            rolled_seg = jnp.roll(seg_ids, -offset_rows, 0)
            heads_out = lax.map(jax.checkpoint(attend_sequence), (rolled_q.reshape(seq_count, SEQ, H, HD), rolled_kv.reshape(seq_count, SEQ, 2 * HD), rolled_seg.reshape(seq_count, SEQ)))
            heads_flat = jnp.roll(heads_out.reshape(TOKENS, H * HD), offset_rows, 0)
            attended = low(low_back(heads_flat))
            residual = block_rows + low_back(jnp.dot(attended, w_out, precision=top_precision)) + bias_out
            hidden_two = low(layer_norm(residual, gain_two, shift_two))
            pre_act = low_back(matmul_rows(hidden_two, w_up) + bias_up)
            activated = low(gelu_tanh(pre_act))
            return residual + jnp.dot(activated, w_down, precision=top_precision) + bias_down
        return lax.map(jax.checkpoint(one_batch), (block_f, segments))
    outputs, pullback = jax.vjp(forward, master, vectors, block_in.astype(jnp.float32))
    grad_master, grad_vectors, grad_block = pullback(cotangent.astype(jnp.float32))
    new_master, new_moment_one, new_moment_two = adam_step(master, grad_master, moment_one, moment_two, step_count, learning_rate)
    new_vectors, new_vec_one, new_vec_two = adam_step(vectors, grad_vectors, vec_one, vec_two, step_count, learning_rate)
    return (outputs.astype(jnp.bfloat16), grad_block.astype(jnp.bfloat16), new_master, new_moment_one, new_moment_two, new_vectors, new_vec_one, new_vec_two)
```

```python
import math

import jax
import jax.numpy as jnp
from jax import lax
from jax.experimental import pallas as pl
from jax.experimental.pallas import tpu as pltpu
from jax.sharding import PartitionSpec as P

D = 2048
H = 16
HD = 128
FF = 8192
CHIP_ROWS = 1024
KEY_ROWS = 2 * CHIP_ROWS
KEY_BLOCK = 256
HEAD_GROUP = 4


norm_eps = 1e-05
gelu_coef = math.sqrt(2.0 / math.pi)
beta_one = 0.9
beta_two = 0.95
adam_eps = 1e-08
decay_rate = 0.1
masked_score = -1e30
score_scale = 1.0 / math.sqrt(HD)

bf16 = jnp.bfloat16
f32 = jnp.float32


def layer_norm_fwd(values, gain, shift):
    mean_row = jnp.mean(values, -1, keepdims=True)
    centered = values - mean_row
    var_row = jnp.mean(centered * centered, -1, keepdims=True)
    inverse = lax.rsqrt(var_row + norm_eps)
    normed = centered * inverse
    return (normed * gain + shift, normed, inverse)


def layer_norm_back(grad_norm, normed, inverse, gain):
    scaled = grad_norm * gain
    return inverse * (
        scaled
        - jnp.mean(scaled, -1, keepdims=True)
        - normed * jnp.mean(scaled * normed, -1, keepdims=True)
    )


def gelu_tanh(values):
    inner = gelu_coef * (values + 0.044715 * values * values * values)
    return 0.5 * values * (1.0 + jnp.tanh(inner))


def gelu_slope(values):
    tangent = jnp.tanh(gelu_coef * (values + 0.044715 * values * values * values))
    return 0.5 * (1.0 + tangent) + 0.5 * values * (1.0 - tangent * tangent) * gelu_coef * (
        1.0 + 3.0 * 0.044715 * values * values
    )


def rows_by_rows(left, right):
    return lax.dot_general(left, right, (((1,), (1,)), ((), ())), preferred_element_type=f32)


def cols_by_cols(left, right):
    return lax.dot_general(left, right, (((0,), (0,)), ((), ())), preferred_element_type=f32)


def plain_dot(left, right):
    return jnp.dot(left, right, preferred_element_type=f32)


def vector_sizes():
    return [D, D, H * HD, HD, D, D, D, FF, D]


def swap(value, axis, step):
    count = lax.axis_size(axis)
    return lax.ppermute(value, axis, [(source, source ^ step) for source in range(count)])


def swap_core(value):
    return swap(value, "dp", 1)


def spread(value):
    return [value] + [swap(value, "tp", m) for m in range(1, lax.axis_size("tp"))]


def collect(pieces):
    total = pieces[0].astype(f32)
    for m in range(1, len(pieces)):
        total = total + swap(pieces[m].astype(bf16), "tp", m).astype(f32)
    return total


def sum_everywhere(value):
    for axis in ("dp", "tp"):
        step = 1
        while step < lax.axis_size(axis):
            value = value + swap(value, axis, step)
            step *= 2
    return value


def attend_forward_kernel(bounds, q_ref, k_ref, vt_ref, bias_ref, out_ref, log_ref, keep_ref):
    rows = q_ref.shape[1]
    tile_heads = bias_ref.shape[2] // rows
    tiles = HEAD_GROUP // tile_heads
    width = HEAD_GROUP * rows
    batch = pl.program_id(0)
    first = bounds[batch, 0]
    last = bounds[batch, 1]
    queries = jnp.concatenate(
        [q_ref[0, :, h * HD : (h + 1) * HD] for h in range(HEAD_GROUP)], 0
    )

    def score_block(block, peak):
        start = pl.multiple_of(block * KEY_BLOCK, KEY_BLOCK)
        scores = rows_by_rows(k_ref[0, pl.ds(start, KEY_BLOCK), :], queries) * score_scale
        bias = bias_ref[0, pl.ds(start, KEY_BLOCK), :]
        scores = scores + jnp.concatenate([bias] * tiles, 1)
        keep_ref[pl.ds(start, KEY_BLOCK), :] = scores
        return jnp.maximum(peak, jnp.max(scores, 0, keepdims=True))

    peak = lax.fori_loop(first, last, score_block, jnp.full((1, width), masked_score, f32))

    def exp_block(block, total):
        start = pl.multiple_of(block * KEY_BLOCK, KEY_BLOCK)
        powers = jnp.exp(keep_ref[pl.ds(start, KEY_BLOCK), :] - peak)
        keep_ref[pl.ds(start, KEY_BLOCK), :] = powers
        return total + jnp.sum(powers, 0, keepdims=True)

    total = lax.fori_loop(first, last, exp_block, jnp.zeros((1, width), f32))
    share = 1.0 / total

    def value_block(block, acc):
        start = pl.multiple_of(block * KEY_BLOCK, KEY_BLOCK)
        probs = (keep_ref[pl.ds(start, KEY_BLOCK), :] * share).astype(bf16)
        return acc + plain_dot(vt_ref[0, :, pl.ds(start, KEY_BLOCK)], probs)

    acc = lax.fori_loop(first, last, value_block, jnp.zeros((HD, width), f32))
    for h in range(HEAD_GROUP):
        out_ref[0, :, h * HD : (h + 1) * HD] = acc[:, h * rows : (h + 1) * rows].T.astype(bf16)
    log_ref[0, 0] = peak + jnp.log(total)


def attend_backward_kernel(
    bounds,
    q_ref,
    g_ref,
    k_ref,
    kt_ref,
    v_ref,
    bias_ref,
    log_ref,
    dq_ref,
    dk_ref,
    dv_ref,
    prob_ref,
    dprob_ref,
):
    rows = q_ref.shape[1]
    tile_heads = bias_ref.shape[2] // rows
    tiles = HEAD_GROUP // tile_heads
    width = HEAD_GROUP * rows
    batch = pl.program_id(0)
    first = bounds[batch, 0]
    last = bounds[batch, 1]

    @pl.when(pl.program_id(1) == 0)
    def _():
        dk_ref[...] = jnp.zeros_like(dk_ref)
        dv_ref[...] = jnp.zeros_like(dv_ref)

    queries = jnp.concatenate(
        [q_ref[0, :, h * HD : (h + 1) * HD] for h in range(HEAD_GROUP)], 0
    )
    grads = jnp.concatenate([g_ref[0, :, h * HD : (h + 1) * HD] for h in range(HEAD_GROUP)], 0)
    log_row = log_ref[0, 0]

    def prob_block(block, delta):
        start = pl.multiple_of(block * KEY_BLOCK, KEY_BLOCK)
        scores = rows_by_rows(k_ref[0, pl.ds(start, KEY_BLOCK), :], queries) * score_scale
        bias = bias_ref[0, pl.ds(start, KEY_BLOCK), :]
        probs = jnp.exp(scores + jnp.concatenate([bias] * tiles, 1) - log_row)
        dprobs = rows_by_rows(v_ref[0, pl.ds(start, KEY_BLOCK), :], grads)
        prob_ref[pl.ds(start, KEY_BLOCK), :] = probs
        dprob_ref[pl.ds(start, KEY_BLOCK), :] = dprobs
        return delta + jnp.sum(probs * dprobs, 0, keepdims=True)

    delta = lax.fori_loop(first, last, prob_block, jnp.zeros((1, width), f32))

    def grad_block(block, acc):
        start = pl.multiple_of(block * KEY_BLOCK, KEY_BLOCK)
        probs = prob_ref[pl.ds(start, KEY_BLOCK), :]
        grad_scores = (probs * (dprob_ref[pl.ds(start, KEY_BLOCK), :] - delta)).astype(bf16)
        dk_ref[0, pl.ds(start, KEY_BLOCK), :] += plain_dot(grad_scores, queries) * score_scale
        dv_ref[0, pl.ds(start, KEY_BLOCK), :] += plain_dot(probs.astype(bf16), grads)
        return acc + plain_dot(kt_ref[0, :, pl.ds(start, KEY_BLOCK)], grad_scores)

    acc = lax.fori_loop(first, last, grad_block, jnp.zeros((HD, width), f32)) * score_scale
    for h in range(HEAD_GROUP):
        dq_ref[0, :, h * HD : (h + 1) * HD] = acc[:, h * rows : (h + 1) * rows].T.astype(bf16)


def attend_forward(queries, keys, vals_t, bias, bounds):
    batches, rows, cols = queries.shape
    groups = cols // (HEAD_GROUP * HD)
    width = HEAD_GROUP * rows
    row_spec = pl.BlockSpec((1, rows, HEAD_GROUP * HD), lambda b, g, *_: (b, 0, g))
    return pl.pallas_call(
        attend_forward_kernel,
        name="attend_forward",
        grid_spec=pltpu.PrefetchScalarGridSpec(
            num_scalar_prefetch=1,
            grid=(batches, groups),
            in_specs=[
                row_spec,
                pl.BlockSpec((1, KEY_ROWS, HD), lambda b, g, *_: (b, 0, 0)),
                pl.BlockSpec((1, HD, KEY_ROWS), lambda b, g, *_: (b, 0, 0)),
                pl.BlockSpec((1, KEY_ROWS, bias.shape[2]), lambda b, g, *_: (b, 0, 0)),
            ],
            out_specs=[
                row_spec,
                pl.BlockSpec((1, 1, 1, width), lambda b, g, *_: (b, g, 0, 0)),
            ],
            scratch_shapes=[pltpu.VMEM((KEY_ROWS, width), f32)],
        ),
        out_shape=[
            jax.ShapeDtypeStruct(queries.shape, bf16),
            jax.ShapeDtypeStruct((batches, groups, 1, width), f32),
        ],
        compiler_params=pltpu.CompilerParams(
            dimension_semantics=("arbitrary", "arbitrary"), vmem_limit_bytes=32 << 20
        ),
        cost_estimate=pl.CostEstimate(
            flops=4 * batches * rows * cols * KEY_ROWS,
            transcendentals=batches * rows * (cols // HD) * KEY_ROWS,
            bytes_accessed=batches * (4 * rows * cols + KEY_ROWS * HD * 8),
        ),
    )(bounds, queries, keys, vals_t, bias)


def attend_backward(queries, grads, keys, keys_t, vals, bias, log_sums, bounds):
    batches, rows, cols = queries.shape
    groups = cols // (HEAD_GROUP * HD)
    width = HEAD_GROUP * rows
    row_spec = pl.BlockSpec((1, rows, HEAD_GROUP * HD), lambda b, g, *_: (b, 0, g))
    key_spec = pl.BlockSpec((1, KEY_ROWS, HD), lambda b, g, *_: (b, 0, 0))
    return pl.pallas_call(
        attend_backward_kernel,
        name="attend_backward",
        grid_spec=pltpu.PrefetchScalarGridSpec(
            num_scalar_prefetch=1,
            grid=(batches, groups),
            in_specs=[
                row_spec,
                row_spec,
                key_spec,
                pl.BlockSpec((1, HD, KEY_ROWS), lambda b, g, *_: (b, 0, 0)),
                key_spec,
                pl.BlockSpec((1, KEY_ROWS, bias.shape[2]), lambda b, g, *_: (b, 0, 0)),
                pl.BlockSpec((1, 1, 1, width), lambda b, g, *_: (b, g, 0, 0)),
            ],
            out_specs=[row_spec, key_spec, key_spec],
            scratch_shapes=[
                pltpu.VMEM((KEY_ROWS, width), f32),
                pltpu.VMEM((KEY_ROWS, width), f32),
            ],
        ),
        out_shape=[
            jax.ShapeDtypeStruct(queries.shape, bf16),
            jax.ShapeDtypeStruct(keys.shape, f32),
            jax.ShapeDtypeStruct(keys.shape, f32),
        ],
        compiler_params=pltpu.CompilerParams(
            dimension_semantics=("arbitrary", "arbitrary"), vmem_limit_bytes=40 << 20
        ),
        cost_estimate=pl.CostEstimate(
            flops=10 * batches * rows * cols * KEY_ROWS,
            transcendentals=batches * rows * (cols // HD) * KEY_ROWS,
            bytes_accessed=batches * (6 * rows * cols + KEY_ROWS * HD * 20),
        ),
    )(bounds, queries, grads, keys, keys_t, vals, bias, log_sums)


def adam_step(weights, grads, first, second, step_count, learning_rate):
    steps_float = step_count[0].astype(f32)
    first_new = beta_one * first + (1.0 - beta_one) * grads
    second_new = beta_two * second + (1.0 - beta_two) * grads * grads
    corr_one = 1.0 - jnp.power(beta_one, steps_float)
    corr_two = 1.0 - jnp.power(beta_two, steps_float)
    update = first_new / corr_one / (jnp.sqrt(second_new / corr_two) + adam_eps)
    return (weights - learning_rate[0] * (update + decay_rate * weights), first_new, second_new)


def body(
    block_in,
    cotangent,
    segments,
    master,
    moment_one,
    moment_two,
    vectors,
    vec_one,
    vec_two,
    step_count,
    learning_rate,
):
    tp_size = lax.axis_size("tp")
    dp_size = lax.axis_size("dp")
    tp_index = lax.axis_index("tp")
    dp_index = lax.axis_index("dp")
    core = dp_index % 2
    chip = dp_index // 2
    batches, rows, _ = block_in.shape
    stretch = rows * tp_size
    query_rows = H * HD // tp_size
    kv_share = 2 * HD // tp_size
    ff_rows = FF // tp_size
    half = query_rows // 2
    kv_half = kv_share // 2
    row_starts = [0]
    for length in [query_rows, kv_share, query_rows, ff_rows, ff_rows]:
        row_starts.append(row_starts[-1] + length)
    parity = [[2 * i + c for i in range(dp_size // 2)] for c in range(2)]

    vec_pieces = []
    cursor = 0
    for length in vector_sizes():
        vec_pieces.append(vectors[cursor : cursor + length])
        cursor += length
    (
        gain_one,
        shift_one,
        bias_query_all,
        bias_value,
        bias_out,
        gain_two,
        shift_two,
        bias_up_all,
        bias_down,
    ) = vec_pieces
    bias_up = lax.dynamic_slice_in_dim(bias_up_all, tp_index * ff_rows, ff_rows)
    keyval_bias = jnp.concatenate([jnp.zeros((HD,), f32), bias_value])

    sides = [core, 1 - core]
    block_of = [tp_index ^ m for m in range(tp_size)]
    query_starts = [
        block_of[m] * query_rows + side * half for side in sides for m in range(tp_size)
    ]
    kv_starts = [
        block_of[m] * kv_share + side * kv_half for side in sides for m in range(tp_size)
    ]
    bias_query = jnp.concatenate(
        [lax.dynamic_slice_in_dim(bias_query_all, start, half) for start in query_starts]
    )

    def shard(first, last):
        return master[row_starts[first] : row_starts[last]].astype(bf16)

    def gather_columns(piece):
        return lax.all_gather(piece, "dp", axis=1, tiled=True)

    qkv_rows = gather_columns(shard(0, 2))
    out_shard, qkv_rows = lax.optimization_barrier((shard(2, 3), qkv_rows))
    out_rows = gather_columns(out_shard)
    up_shard, out_rows = lax.optimization_barrier((shard(3, 4), out_rows))
    w_up = gather_columns(up_shard)
    down_shard, w_up = lax.optimization_barrier((shard(4, 5), w_up))
    w_down = gather_columns(down_shard)

    def split_sides(block):
        size = block.shape[0] // 2
        return [lax.dynamic_slice_in_dim(block, side * size, size) for side in sides]

    def widen_rows(own, other):
        received = spread(own)
        crossed = swap_core(jnp.concatenate(received[1:], 0))
        return jnp.concatenate(received + [other, crossed], 0)

    kv_blocks = spread(qkv_rows[query_rows:])
    w_keyval = jnp.zeros((2 * HD, D), bf16)
    for m in range(tp_size):
        w_keyval = lax.dynamic_update_slice_in_dim(
            w_keyval, kv_blocks[m], block_of[m] * kv_share, 0
        )
    w_query = widen_rows(*split_sides(qkv_rows[:query_rows]))
    w_out = widen_rows(*split_sides(out_rows))

    block_rows = block_in.astype(f32).reshape(batches * rows, D)
    ln_one, normed_one, inverse_one = layer_norm_fwd(block_rows, gain_one, shift_one)
    hidden_one = ln_one.astype(bf16)
    kv_local = (rows_by_rows(hidden_one, w_keyval) + keyval_bias).astype(bf16)
    kv_local = kv_local.reshape(batches, 1, rows, 2 * HD)
    kv_stretch = jnp.zeros((batches, tp_size, rows, 2 * HD), bf16)
    for m, piece in enumerate(spread(kv_local)):
        kv_stretch = lax.dynamic_update_slice_in_dim(kv_stretch, piece, block_of[m], 1)
    kv_stretch = kv_stretch.reshape(batches, 1, stretch, 2 * HD)

    def both_sides(own, other):
        pair = jnp.zeros((batches, 2, stretch, 2 * HD), bf16)
        pair = lax.dynamic_update_slice_in_dim(pair, own, core, 1)
        return lax.dynamic_update_slice_in_dim(pair, other, 1 - core, 1)

    to_next = [(d, d + 2) for d in range(dp_size - 2) if (d // 2) % 2 == 1]
    to_last = [(target, source) for source, target in to_next]
    kv_before = lax.ppermute(kv_stretch, "dp", to_next)
    kv_here = both_sides(kv_stretch, swap_core(kv_stretch))
    kv_before = both_sides(kv_before, swap_core(kv_before))
    keyvals = jnp.concatenate([kv_before, kv_here], 1).reshape(batches, KEY_ROWS, 2 * HD)
    keys = keyvals[:, :, :HD]
    vals = keyvals[:, :, HD:]
    keys_t = keys.transpose(0, 2, 1)
    vals_t = vals.transpose(0, 2, 1)

    own_first = dp_index * stretch + tp_index * rows
    seg_own = lax.dynamic_slice_in_dim(segments, own_first, rows, 1)
    seg_padded = jnp.pad(segments, ((0, 0), (CHIP_ROWS, 0)), constant_values=-1)
    seg_keys = lax.dynamic_slice_in_dim(seg_padded, chip * CHIP_ROWS, KEY_ROWS, 1)
    key_base = (chip - 1) * CHIP_ROWS
    key_place = key_base + jnp.arange(KEY_ROWS)
    tile_heads = max(1, 128 // rows)
    own_place = own_first + jnp.arange(rows)
    allowed = (seg_keys[:, :, None] == seg_own[:, None, :]) & (
        key_place[None, :, None] <= own_place[None, None, :]
    )
    bias = jnp.where(jnp.tile(allowed, (1, 1, tile_heads)), 0.0, masked_score).astype(f32)
    last_block = jnp.broadcast_to(
        (own_first - key_base + rows + KEY_BLOCK - 1) // KEY_BLOCK, (batches,)
    )
    first_block = jnp.maximum(seg_own[:, 0] - key_base, 0) // KEY_BLOCK
    bounds = jnp.stack([first_block, last_block], 1).astype(jnp.int32)

    queries = (rows_by_rows(hidden_one, w_query) + bias_query).astype(bf16)
    queries = queries.reshape(batches, rows, H * HD)
    attended, log_sums = attend_forward(queries, keys, vals_t, bias, bounds)
    attended = attended.reshape(batches * rows, H * HD)
    residual = block_rows + plain_dot(attended, w_out) + bias_out
    ln_two, normed_two, inverse_two = layer_norm_fwd(residual, gain_two, shift_two)
    hidden_two = ln_two.astype(bf16)

    outputs = []
    wide_hidden = []
    wide_cot = []
    wide_act = []
    wide_pre_grad = []
    grad_two_parts = []
    for b in range(batches):
        own = slice(b * rows, (b + 1) * rows)
        hidden_all = jnp.concatenate(spread(hidden_two[own]), 0)
        cot_all = jnp.concatenate(spread(cotangent[b]), 0)
        pre_act = rows_by_rows(hidden_all, w_up) + bias_up
        activated = gelu_tanh(pre_act).astype(bf16)
        grad_pre = (rows_by_rows(cot_all, w_down) * gelu_slope(pre_act)).astype(bf16)
        grad_hidden = plain_dot(grad_pre, w_up)
        grad_two_parts.append(
            collect([grad_hidden[m * rows : (m + 1) * rows] for m in range(tp_size)])
        )
        product = plain_dot(activated, w_down)
        summed = collect([product[m * rows : (m + 1) * rows] for m in range(tp_size)])
        outputs.append((residual[own] + summed + bias_down).astype(bf16))
        wide_hidden.append(hidden_all)
        wide_cot.append(cot_all)
        wide_act.append(activated)
        wide_pre_grad.append(grad_pre)

    grad_down = cols_by_cols(jnp.concatenate(wide_act, 0), jnp.concatenate(wide_cot, 0))
    grad_up = cols_by_cols(jnp.concatenate(wide_pre_grad, 0), jnp.concatenate(wide_hidden, 0))
    grad_bias_up = sum(jnp.sum(part.astype(f32), 0) for part in wide_pre_grad)

    def scatter_columns(full):
        return lax.psum_scatter(full, "dp", scatter_dimension=1, tiled=True)

    shard_down = scatter_columns(grad_down.astype(bf16)).astype(f32)
    shard_up = scatter_columns(grad_up.astype(bf16)).astype(f32)

    cot_rows = cotangent.astype(f32).reshape(batches * rows, D)
    grad_bias_down = jnp.sum(cot_rows, 0)
    grad_hidden_two = jnp.concatenate(grad_two_parts, 0)
    grad_resid = cot_rows + layer_norm_back(grad_hidden_two, normed_two, inverse_two, gain_two)
    grad_gain_two = jnp.sum(grad_hidden_two * normed_two, 0)
    grad_shift_two = jnp.sum(grad_hidden_two, 0)
    grad_att = grad_resid.astype(bf16)
    grad_bias_out = jnp.sum(grad_resid, 0)
    grad_heads = rows_by_rows(grad_att, w_out).astype(bf16).reshape(batches, rows, H * HD)
    grad_query, grad_key, grad_val = attend_backward(
        queries, grad_heads, keys, keys_t, vals, bias, log_sums, bounds
    )
    grad_query = grad_query.reshape(batches * rows, H * HD)
    grad_bias_query = jnp.sum(grad_query.astype(f32), 0)

    kv_grads = jnp.concatenate([grad_key, grad_val], 2)
    kv_grads = kv_grads.reshape(batches, 2, 2, stretch, 2 * HD)
    kv_kept = lax.dynamic_slice_in_dim(kv_grads, core, 1, 2)
    kv_sent = lax.dynamic_slice_in_dim(kv_grads, 1 - core, 1, 2).astype(bf16)
    kv_kept = kv_kept + swap_core(kv_sent).astype(f32)
    kv_kept = kv_kept.reshape(batches, 2, tp_size, rows, 2 * HD)
    kv_total = kv_kept[:, 1] + lax.ppermute(kv_kept[:, 0].astype(bf16), "dp", to_last).astype(f32)
    grad_kv = collect([lax.dynamic_slice_in_dim(kv_total, at, 1, 1) for at in block_of])
    grad_kv = grad_kv.astype(bf16).reshape(batches * rows, 2 * HD)
    grad_bias_value = jnp.sum(grad_kv[:, HD:].astype(f32), 0)

    grad_hidden_one = plain_dot(grad_query, w_query) + plain_dot(grad_kv, w_keyval)
    grad_rows = grad_resid + layer_norm_back(grad_hidden_one, normed_one, inverse_one, gain_one)
    grad_gain_one = jnp.sum(grad_hidden_one * normed_one, 0)
    grad_shift_one = jnp.sum(grad_hidden_one, 0)
    input_grads = grad_rows.astype(bf16).reshape(batches, rows, D)

    def reduce_blocks(own, other):
        own = own + swap_core(other.astype(bf16)).astype(f32)
        size = own.shape[0] // tp_size
        return collect([own[m * size : (m + 1) * size] for m in range(tp_size)])

    cols_half = H * HD // 2
    part_out = reduce_blocks(
        cols_by_cols(attended[:, :cols_half], grad_att),
        cols_by_cols(attended[:, cols_half:], grad_att),
    )
    part_query = reduce_blocks(
        cols_by_cols(grad_query[:, :cols_half], hidden_one),
        cols_by_cols(grad_query[:, cols_half:], hidden_one),
    )
    grad_w_keyval = cols_by_cols(grad_kv, hidden_one)
    kv_rows = [lax.dynamic_slice_in_dim(grad_w_keyval, start, kv_half) for start in kv_starts]
    part_keyval = reduce_blocks(
        jnp.concatenate(kv_rows[:tp_size], 0), jnp.concatenate(kv_rows[tp_size:], 0)
    )
    part_all = jnp.concatenate([part_query, part_keyval, part_out], 0).astype(bf16)
    part_all = lax.psum_scatter(
        part_all, "dp", scatter_dimension=1, axis_index_groups=parity, tiled=True
    )
    width = part_all.shape[1] // 2
    mine = lax.dynamic_slice_in_dim(part_all, core * width, width, 1)
    theirs = swap_core(lax.dynamic_slice_in_dim(part_all, (1 - core) * width, width, 1))
    low_half = jnp.where(core == 0, mine, theirs)
    high_half = jnp.where(core == 0, theirs, mine)
    pieces = []
    at = 0
    for size in (half, kv_half, half):
        pieces += [low_half[at : at + size], high_half[at : at + size]]
        at += size
    shard_attention = jnp.concatenate(pieces, 0).astype(f32)

    whole_bias_query = jnp.zeros((H * HD,), f32)
    for index, start in enumerate(query_starts):
        whole_bias_query = lax.dynamic_update_slice_in_dim(
            whole_bias_query, grad_bias_query[index * half : (index + 1) * half], start, 0
        )
    whole_bias_up = lax.dynamic_update_slice_in_dim(
        jnp.zeros((FF,), f32), grad_bias_up, tp_index * ff_rows, 0
    )
    vec_grads = jnp.concatenate(
        [
            grad_gain_one,
            grad_shift_one,
            whole_bias_query,
            grad_bias_value,
            grad_bias_out,
            grad_gain_two,
            grad_shift_two,
            whole_bias_up,
            grad_bias_down,
        ]
    )
    vec_total = sum_everywhere(vec_grads.reshape(-1, 128)).reshape(-1)
    new_vectors, new_vec_one, new_vec_two = adam_step(
        vectors, vec_total, vec_one, vec_two, step_count, learning_rate
    )
    updated = []
    for first, last, grads in (
        (0, 3, shard_attention),
        (3, 4, shard_up),
        (4, 5, shard_down),
    ):
        at = slice(row_starts[first], row_starts[last])
        updated.append(
            adam_step(
                master[at], grads, moment_one[at], moment_two[at], step_count, learning_rate
            )
        )
    new_master, new_moment_one, new_moment_two = (
        jnp.concatenate(parts, 0) for parts in zip(*updated)
    )
    return (
        jnp.stack(outputs),
        input_grads,
        new_master,
        new_moment_one,
        new_moment_two,
        new_vectors,
        new_vec_one,
        new_vec_two,
    )


def solution(mesh):
    in_specs = (
        P(None, ("dp", "tp"), None),
        P(None, ("dp", "tp"), None),
        P(),
        P("tp", "dp"),
        P("tp", "dp"),
        P("tp", "dp"),
        P(),
        P(),
        P(),
        P(),
        P(),
    )
    out_specs = (
        P(None, ("dp", "tp"), None),
        P(None, ("dp", "tp"), None),
        P("tp", "dp"),
        P("tp", "dp"),
        P("tp", "dp"),
        P(),
        P(),
        P(),
    )
    return jax.shard_map(body, mesh=mesh, in_specs=in_specs, out_specs=out_specs, check_vma=False)
```

```python
import functools
import math

import jax
import jax.numpy as jnp
from jax import lax
from jax.experimental import pallas as pl
from jax.experimental.pallas import tpu as pltpu
from jax.sharding import PartitionSpec as P

D = 2048
H = 16
HD = 128
FF = 8192
CHIP_ROWS = 1024
KEY_ROWS = 2 * CHIP_ROWS
KEY_BLOCK = 256
HEAD_GROUP = 4


norm_eps = 1e-05
gelu_coef = math.sqrt(2.0 / math.pi)
beta_one = 0.9
beta_two = 0.95
adam_eps = 1e-08
decay_rate = 0.1
masked_score = -1e30
score_scale = 1.0 / math.sqrt(HD)

bf16 = jnp.bfloat16
f32 = jnp.float32

cheap = pl.CostEstimate(flops=1 << 20, transcendentals=0, bytes_accessed=1 << 20)


def layer_norm_fwd(values, gain, shift):
    mean_row = jnp.mean(values, -1, keepdims=True)
    centered = values - mean_row
    var_row = jnp.mean(centered * centered, -1, keepdims=True)
    inverse = lax.rsqrt(var_row + norm_eps)
    normed = centered * inverse
    return (normed * gain + shift, normed, inverse)


def layer_norm_back(grad_norm, normed, inverse, gain):
    scaled = grad_norm * gain
    return inverse * (
        scaled
        - jnp.mean(scaled, -1, keepdims=True)
        - normed * jnp.mean(scaled * normed, -1, keepdims=True)
    )


def gelu_tanh(values):
    inner = gelu_coef * (values + 0.044715 * values * values * values)
    return 0.5 * values * (1.0 + jnp.tanh(inner))


def gelu_slope(values):
    tangent = jnp.tanh(gelu_coef * (values + 0.044715 * values * values * values))
    return 0.5 * (1.0 + tangent) + 0.5 * values * (1.0 - tangent * tangent) * gelu_coef * (
        1.0 + 3.0 * 0.044715 * values * values
    )


def rows_by_rows(left, right):
    return lax.dot_general(left, right, (((1,), (1,)), ((), ())), preferred_element_type=f32)


def cols_by_cols(left, right):
    return lax.dot_general(left, right, (((0,), (0,)), ((), ())), preferred_element_type=f32)


def plain_dot(left, right):
    return jnp.dot(left, right, preferred_element_type=f32)


def vector_sizes():
    return [D, D, H * HD, HD, D, D, D, FF, D]


def swap(value, axis, step):
    count = lax.axis_size(axis)
    return lax.ppermute(value, axis, [(source, source ^ step) for source in range(count)])


def swap_core(value):
    return swap(value, "dp", 1)


def spread_directly(value):
    return [value] + [swap(value, "tp", m) for m in range(1, lax.axis_size("tp"))]


def cut(value):
    at = value.shape[-2] // 2
    return (value[..., :at, :], value[..., at:, :])


def spread(value):
    if lax.axis_size("tp") != 4:
        return spread_directly(value)
    first = swap(value, "tp", 1)
    second = swap(value, "tp", 2)
    far_top = swap(cut(first)[0], "tp", 2)
    far_low = swap(cut(second)[1], "tp", 1)
    return [value, first, second, jnp.concatenate([far_top, far_low], -2)]


def deliver(pieces):
    return [pieces[0]] + [swap(pieces[m].astype(bf16), "tp", m) for m in range(1, len(pieces))]


def total_of(pieces):
    total = pieces[0].astype(f32)
    for piece in pieces[1:]:
        total = total + piece.astype(f32)
    return total


def after(value, *others):
    return lax.optimization_barrier((value,) + others)[0]


def sum_everywhere(value):
    for axis in ("dp", "tp"):
        step = 1
        while step < lax.axis_size(axis):
            value = value + swap(value, axis, step)
            step *= 2
    return value


def attend_forward_kernel(bounds, q_ref, k_ref, vt_ref, bias_ref, out_ref, log_ref, keep_ref):
    rows = q_ref.shape[1]
    tile_heads = bias_ref.shape[2] // rows
    tiles = HEAD_GROUP // tile_heads
    width = HEAD_GROUP * rows
    batch = pl.program_id(0)
    first = bounds[batch, 0]
    last = bounds[batch, 1]
    queries = jnp.concatenate(
        [q_ref[0, :, h * HD : (h + 1) * HD] for h in range(HEAD_GROUP)], 0
    )

    def score_block(block, peak):
        start = pl.multiple_of(block * KEY_BLOCK, KEY_BLOCK)
        scores = rows_by_rows(k_ref[0, pl.ds(start, KEY_BLOCK), :], queries) * score_scale
        bias = bias_ref[0, pl.ds(start, KEY_BLOCK), :]
        scores = scores + jnp.concatenate([bias] * tiles, 1)
        keep_ref[pl.ds(start, KEY_BLOCK), :] = scores
        return jnp.maximum(peak, jnp.max(scores, 0, keepdims=True))

    peak = lax.fori_loop(first, last, score_block, jnp.full((1, width), masked_score, f32))

    def exp_block(block, total):
        start = pl.multiple_of(block * KEY_BLOCK, KEY_BLOCK)
        powers = jnp.exp(keep_ref[pl.ds(start, KEY_BLOCK), :] - peak)
        keep_ref[pl.ds(start, KEY_BLOCK), :] = powers
        return total + jnp.sum(powers, 0, keepdims=True)

    total = lax.fori_loop(first, last, exp_block, jnp.zeros((1, width), f32))
    share = 1.0 / total

    def value_block(block, acc):
        start = pl.multiple_of(block * KEY_BLOCK, KEY_BLOCK)
        probs = (keep_ref[pl.ds(start, KEY_BLOCK), :] * share).astype(bf16)
        return acc + plain_dot(vt_ref[0, :, pl.ds(start, KEY_BLOCK)], probs)

    acc = lax.fori_loop(first, last, value_block, jnp.zeros((HD, width), f32))
    for h in range(HEAD_GROUP):
        out_ref[0, :, h * HD : (h + 1) * HD] = acc[:, h * rows : (h + 1) * rows].T.astype(bf16)
    log_ref[0, 0] = peak + jnp.log(total)


def attend_backward_kernel(
    bounds,
    q_ref,
    g_ref,
    k_ref,
    kt_ref,
    v_ref,
    bias_ref,
    log_ref,
    dq_ref,
    dk_ref,
    dv_ref,
    prob_ref,
    dprob_ref,
):
    rows = q_ref.shape[1]
    tile_heads = bias_ref.shape[2] // rows
    tiles = HEAD_GROUP // tile_heads
    width = HEAD_GROUP * rows
    batch = pl.program_id(0)
    first = bounds[batch, 0]
    last = bounds[batch, 1]

    @pl.when(pl.program_id(1) == 0)
    def _():
        dk_ref[...] = jnp.zeros_like(dk_ref)
        dv_ref[...] = jnp.zeros_like(dv_ref)

    queries = jnp.concatenate(
        [q_ref[0, :, h * HD : (h + 1) * HD] for h in range(HEAD_GROUP)], 0
    )
    grads = jnp.concatenate([g_ref[0, :, h * HD : (h + 1) * HD] for h in range(HEAD_GROUP)], 0)
    log_row = log_ref[0, 0]

    def prob_block(block, delta):
        start = pl.multiple_of(block * KEY_BLOCK, KEY_BLOCK)
        scores = rows_by_rows(k_ref[0, pl.ds(start, KEY_BLOCK), :], queries) * score_scale
        bias = bias_ref[0, pl.ds(start, KEY_BLOCK), :]
        probs = jnp.exp(scores + jnp.concatenate([bias] * tiles, 1) - log_row)
        dprobs = rows_by_rows(v_ref[0, pl.ds(start, KEY_BLOCK), :], grads)
        prob_ref[pl.ds(start, KEY_BLOCK), :] = probs
        dprob_ref[pl.ds(start, KEY_BLOCK), :] = dprobs
        return delta + jnp.sum(probs * dprobs, 0, keepdims=True)

    delta = lax.fori_loop(first, last, prob_block, jnp.zeros((1, width), f32))

    def grad_block(block, acc):
        start = pl.multiple_of(block * KEY_BLOCK, KEY_BLOCK)
        probs = prob_ref[pl.ds(start, KEY_BLOCK), :]
        grad_scores = (probs * (dprob_ref[pl.ds(start, KEY_BLOCK), :] - delta)).astype(bf16)
        dk_ref[0, pl.ds(start, KEY_BLOCK), :] += plain_dot(grad_scores, queries) * score_scale
        dv_ref[0, pl.ds(start, KEY_BLOCK), :] += plain_dot(probs.astype(bf16), grads)
        return acc + plain_dot(kt_ref[0, :, pl.ds(start, KEY_BLOCK)], grad_scores)

    acc = lax.fori_loop(first, last, grad_block, jnp.zeros((HD, width), f32)) * score_scale
    for h in range(HEAD_GROUP):
        dq_ref[0, :, h * HD : (h + 1) * HD] = acc[:, h * rows : (h + 1) * rows].T.astype(bf16)


def attend_forward(queries, keys, vals_t, bias, bounds):
    batches, rows, cols = queries.shape
    groups = cols // (HEAD_GROUP * HD)
    width = HEAD_GROUP * rows
    row_spec = pl.BlockSpec((1, rows, HEAD_GROUP * HD), lambda b, g, *_: (b, 0, g))
    return pl.pallas_call(
        attend_forward_kernel,
        name="attend_forward",
        grid_spec=pltpu.PrefetchScalarGridSpec(
            num_scalar_prefetch=1,
            grid=(batches, groups),
            in_specs=[
                row_spec,
                pl.BlockSpec((1, KEY_ROWS, HD), lambda b, g, *_: (b, 0, 0)),
                pl.BlockSpec((1, HD, KEY_ROWS), lambda b, g, *_: (b, 0, 0)),
                pl.BlockSpec((1, KEY_ROWS, bias.shape[2]), lambda b, g, *_: (b, 0, 0)),
            ],
            out_specs=[
                row_spec,
                pl.BlockSpec((1, 1, 1, width), lambda b, g, *_: (b, g, 0, 0)),
            ],
            scratch_shapes=[pltpu.VMEM((KEY_ROWS, width), f32)],
        ),
        out_shape=[
            jax.ShapeDtypeStruct(queries.shape, bf16),
            jax.ShapeDtypeStruct((batches, groups, 1, width), f32),
        ],
        compiler_params=pltpu.CompilerParams(
            dimension_semantics=("arbitrary", "arbitrary"), vmem_limit_bytes=32 << 20
        ),
        cost_estimate=cheap,
    )(bounds, queries, keys, vals_t, bias)


def attend_backward(queries, grads, keys, keys_t, vals, bias, log_sums, bounds):
    batches, rows, cols = queries.shape
    groups = cols // (HEAD_GROUP * HD)
    width = HEAD_GROUP * rows
    row_spec = pl.BlockSpec((1, rows, HEAD_GROUP * HD), lambda b, g, *_: (b, 0, g))
    key_spec = pl.BlockSpec((1, KEY_ROWS, HD), lambda b, g, *_: (b, 0, 0))
    return pl.pallas_call(
        attend_backward_kernel,
        name="attend_backward",
        grid_spec=pltpu.PrefetchScalarGridSpec(
            num_scalar_prefetch=1,
            grid=(batches, groups),
            in_specs=[
                row_spec,
                row_spec,
                key_spec,
                pl.BlockSpec((1, HD, KEY_ROWS), lambda b, g, *_: (b, 0, 0)),
                key_spec,
                pl.BlockSpec((1, KEY_ROWS, bias.shape[2]), lambda b, g, *_: (b, 0, 0)),
                pl.BlockSpec((1, 1, 1, width), lambda b, g, *_: (b, g, 0, 0)),
            ],
            out_specs=[row_spec, key_spec, key_spec],
            scratch_shapes=[
                pltpu.VMEM((KEY_ROWS, width), f32),
                pltpu.VMEM((KEY_ROWS, width), f32),
            ],
        ),
        out_shape=[
            jax.ShapeDtypeStruct(queries.shape, bf16),
            jax.ShapeDtypeStruct(keys.shape, f32),
            jax.ShapeDtypeStruct(keys.shape, f32),
        ],
        compiler_params=pltpu.CompilerParams(
            dimension_semantics=("arbitrary", "arbitrary"), vmem_limit_bytes=40 << 20
        ),
        cost_estimate=cheap,
    )(bounds, queries, grads, keys, keys_t, vals, bias, log_sums)


def gelu_parts(values):
    square = values * values
    return jnp.tanh(values * (gelu_coef + (gelu_coef * 0.044715) * square)), square


def ffn_up_kernel(*refs):
    count = len(refs) - 4
    hidden_refs = refs[:count]
    weight_ref, bias_ref, pre_ref, act_ref = refs[count:]
    rows = hidden_refs[0].shape[0]
    for m in range(count):
        at = pl.ds(m * rows, rows)
        values = rows_by_rows(hidden_refs[m][...], weight_ref[...]) + bias_ref[...]
        pre_ref[at, :] = values
        tangent, _ = gelu_parts(values)
        act_ref[at, :] = (0.5 * values * (1.0 + tangent)).astype(bf16)


def ffn_back_kernel(*refs, count):
    weight_ref = refs[count]
    pre_refs, (grad_ref, sum_ref) = refs[count + 1 : -2], refs[-2:]
    cot_refs = refs[:count]
    rows = cot_refs[0].shape[0]
    total = jnp.zeros(sum_ref.shape, f32)
    for m in range(count):
        at = pl.ds(m * rows, rows)
        values = piece_of(pre_refs, m, rows)
        tangent, square = gelu_parts(values)
        slope = 0.5 * (1.0 + tangent) + (0.5 * gelu_coef) * values * (1.0 - tangent * tangent) * (
            1.0 + (3.0 * 0.044715) * square
        )
        grad = (rows_by_rows(cot_refs[m][...], weight_ref[...]) * slope).astype(bf16)
        grad_ref[at, :] = grad
        total = total + jnp.sum(grad.astype(f32), 0, keepdims=True)
    sum_ref[...] = total


def piece_of(refs, index, rows):
    at = index * rows
    for ref in refs:
        if at < ref.shape[0]:
            return ref[pl.ds(at, rows), :]
        at -= ref.shape[0]


def ffn_product_kernel(*refs, lefts):
    right_ref, out_refs = refs[lefts], refs[lefts + 1 :]
    for m, out_ref in enumerate(out_refs):
        left = piece_of(refs[:lefts], m, out_ref.shape[0])
        out_ref[...] = plain_dot(left, right_ref[...]).astype(bf16)


def ffn_weight_kernel(*refs, lefts):
    right_refs, out_ref = refs[lefts:-1], refs[-1]
    rows = right_refs[0].shape[0]
    total = None
    for m, right_ref in enumerate(right_refs):
        part = cols_by_cols(piece_of(refs[:lefts], m, rows), right_ref[...])
        total = part if total is None else total + part
    out_ref[...] = total.astype(bf16)


def ffn_params():
    return pltpu.CompilerParams(
        dimension_semantics=("arbitrary",), vmem_limit_bytes=56 << 20
    )


def whole_specs(pieces):
    return [pl.BlockSpec(piece.shape, lambda i: (0, 0)) for piece in pieces]


def ffn_up(pieces, weights, bias, tile=256):
    units, width = weights.shape
    rows = len(pieces) * pieces[0].shape[0]
    out_spec = pl.BlockSpec((rows, tile), lambda i: (0, i))
    return pl.pallas_call(
        ffn_up_kernel,
        name="ffn_up",
        grid=(units // tile,),
        in_specs=whole_specs(pieces)
        + [
            pl.BlockSpec((tile, width), lambda i: (i, 0)),
            pl.BlockSpec((1, tile), lambda i: (0, i)),
        ],
        out_specs=[out_spec, out_spec],
        out_shape=[
            jax.ShapeDtypeStruct((rows, units), f32),
            jax.ShapeDtypeStruct((rows, units), bf16),
        ],
        compiler_params=ffn_params(),
        cost_estimate=cheap,
    )(*pieces, weights, bias.reshape(1, units))


def ffn_back(pieces, weights, pre_acts, tile=256):
    units, width = weights.shape
    rows = len(pieces) * pieces[0].shape[0]
    out_spec = pl.BlockSpec((rows, tile), lambda i: (0, i))
    sum_spec = pl.BlockSpec((1, tile), lambda i: (0, i))
    return pl.pallas_call(
        functools.partial(ffn_back_kernel, count=len(pieces)),
        name="ffn_back",
        grid=(units // tile,),
        in_specs=whole_specs(pieces)
        + [pl.BlockSpec((tile, width), lambda i: (i, 0))]
        + [pl.BlockSpec((part.shape[0], tile), lambda i: (0, i)) for part in pre_acts],
        out_specs=[out_spec, sum_spec],
        out_shape=[
            jax.ShapeDtypeStruct((rows, units), bf16),
            jax.ShapeDtypeStruct((1, units), f32),
        ],
        compiler_params=ffn_params(),
        cost_estimate=cheap,
    )(*pieces, weights, *pre_acts)


def ffn_product(lefts, right, count, tile=256):
    units, width = right.shape
    piece = sum(left.shape[0] for left in lefts) // count
    return pl.pallas_call(
        functools.partial(ffn_product_kernel, lefts=len(lefts)),
        name="ffn_product",
        grid=(width // tile,),
        in_specs=whole_specs(lefts) + [pl.BlockSpec((units, tile), lambda i: (0, i))],
        out_specs=[pl.BlockSpec((piece, tile), lambda i: (0, i))] * count,
        out_shape=[jax.ShapeDtypeStruct((piece, width), bf16)] * count,
        compiler_params=ffn_params(),
        cost_estimate=cheap,
    )(*lefts, right)


def ffn_weight(lefts, pieces, tile=256):
    units = lefts[0].shape[1]
    width = pieces[0].shape[1]
    return pl.pallas_call(
        functools.partial(ffn_weight_kernel, lefts=len(lefts)),
        name="ffn_weight",
        grid=(units // tile,),
        in_specs=[pl.BlockSpec((left.shape[0], tile), lambda i: (0, i)) for left in lefts]
        + whole_specs(pieces),
        out_specs=pl.BlockSpec((tile, width), lambda i: (i, 0)),
        out_shape=jax.ShapeDtypeStruct((units, width), bf16),
        compiler_params=ffn_params(),
        cost_estimate=cheap,
    )(*lefts, *pieces)


def adam_step(weights, grads, first, second, step_count, learning_rate):
    steps_float = step_count[0].astype(f32)
    first_new = beta_one * first + (1.0 - beta_one) * grads
    second_new = beta_two * second + (1.0 - beta_two) * grads * grads
    corr_one = 1.0 - jnp.power(beta_one, steps_float)
    corr_two = 1.0 - jnp.power(beta_two, steps_float)
    update = first_new / corr_one / (jnp.sqrt(second_new / corr_two) + adam_eps)
    return (weights - learning_rate[0] * (update + decay_rate * weights), first_new, second_new)


def adam_kernel(scalars, weights, grads, first, second, *refs):
    new_weights, new_first, new_second = refs[-3:]
    rate = scalars[0]
    grad = grads[...].astype(f32)
    first_new = beta_one * first[...] + (1.0 - beta_one) * grad
    second_new = beta_two * second[...] + (1.0 - beta_two) * grad * grad
    update = first_new / scalars[1] / (jnp.sqrt(second_new / scalars[2]) + adam_eps)
    new_weights[...] = weights[...] - rate * (update + decay_rate * weights[...])
    new_first[...] = first_new
    new_second[...] = second_new


def adam_rows(scalars, weights, grads, first, second, start, block, filled):
    count, width = grads.shape

    def placed(i, *_):
        return (pl.multiple_of(start + i * block, 8), 0)

    whole = pl.BlockSpec((pl.Element(block), pl.Element(width)), placed)
    piece = pl.BlockSpec((block, width), lambda i, *_: (i, 0))
    return pl.pallas_call(
        adam_kernel,
        name="adam_rows",
        grid_spec=pltpu.PrefetchScalarGridSpec(
            num_scalar_prefetch=1,
            grid=(count // block,),
            in_specs=[whole, piece, whole, whole]
            + [pl.BlockSpec(memory_space=pl.ANY)] * len(filled),
            out_specs=[whole] * 3,
        ),
        out_shape=[jax.ShapeDtypeStruct(weights.shape, f32)] * 3,
        input_output_aliases={5 + i: i for i in range(len(filled))},
        compiler_params=pltpu.CompilerParams(
            dimension_semantics=("arbitrary",), vmem_limit_bytes=56 << 20
        ),
        cost_estimate=cheap,
    )(scalars, weights, grads, first, second, *filled)


def body(
    block_in,
    cotangent,
    segments,
    master,
    moment_one,
    moment_two,
    vectors,
    vec_one,
    vec_two,
    step_count,
    learning_rate,
):
    tp_size = lax.axis_size("tp")
    dp_size = lax.axis_size("dp")
    tp_index = lax.axis_index("tp")
    dp_index = lax.axis_index("dp")
    core = dp_index % 2
    chip = dp_index // 2
    batches, rows, _ = block_in.shape
    stretch = rows * tp_size
    query_rows = H * HD // tp_size
    kv_share = 2 * HD // tp_size
    ff_rows = FF // tp_size
    half = query_rows // 2
    kv_half = kv_share // 2
    row_starts = [0]
    for length in [query_rows, kv_share, query_rows, ff_rows, ff_rows]:
        row_starts.append(row_starts[-1] + length)
    parity = [[2 * i + c for i in range(dp_size // 2)] for c in range(2)]

    vec_pieces = []
    cursor = 0
    for length in vector_sizes():
        vec_pieces.append(vectors[cursor : cursor + length])
        cursor += length
    (
        gain_one,
        shift_one,
        bias_query_all,
        bias_value,
        bias_out,
        gain_two,
        shift_two,
        bias_up_all,
        bias_down,
    ) = vec_pieces
    bias_up = lax.dynamic_slice_in_dim(bias_up_all, tp_index * ff_rows, ff_rows)
    keyval_bias = jnp.concatenate([jnp.zeros((HD,), f32), bias_value])

    sides = [core, 1 - core]
    block_of = [tp_index ^ m for m in range(tp_size)]
    query_starts = [
        block_of[m] * query_rows + side * half for side in sides for m in range(tp_size)
    ]
    kv_starts = [
        block_of[m] * kv_share + side * kv_half for side in sides for m in range(tp_size)
    ]
    bias_query = jnp.concatenate(
        [lax.dynamic_slice_in_dim(bias_query_all, start, half) for start in query_starts]
    )

    def shard(first, last):
        return master[row_starts[first] : row_starts[last]].astype(bf16)

    def gather_columns(piece):
        return lax.all_gather(piece, "dp", axis=1, tiled=True)

    kv_rows = gather_columns(shard(1, 2))
    query_rows_all = gather_columns(shard(0, 1))
    out_rows = gather_columns(shard(2, 3))
    w_up = gather_columns(shard(3, 4))
    w_down = gather_columns(shard(4, 5))
    def split_sides(block):
        size = block.shape[0] // 2
        return [lax.dynamic_slice_in_dim(block, side * size, size) for side in sides]

    def widen_rows(received, other):
        crossed = swap_core(jnp.concatenate(received[1:], 0))
        return jnp.concatenate(received + [other, crossed], 0)

    w_keyval = jnp.zeros((2 * HD, D), bf16)
    for m, piece in enumerate(spread_directly(kv_rows)):
        w_keyval = lax.dynamic_update_slice_in_dim(w_keyval, piece, block_of[m] * kv_share, 0)
    query_own, query_other = split_sides(query_rows_all)
    query_got = spread_directly(query_own)
    w_query = widen_rows(query_got, query_other)

    block_rows = block_in.astype(f32).reshape(batches * rows, D)
    ln_one, normed_one, inverse_one = layer_norm_fwd(block_rows, gain_one, shift_one)
    hidden_one = ln_one.astype(bf16)
    kv_local = (rows_by_rows(hidden_one, w_keyval) + keyval_bias).astype(bf16)
    kv_local = kv_local.reshape(1, batches, 1, rows, 2 * HD)
    to_next = [(d, d + 2) for d in range(dp_size - 2) if (d // 2) % 2 == 1]
    to_last = [(target, source) for source, target in to_next]
    kv_pair = jnp.concatenate([lax.ppermute(kv_local, "dp", to_next), kv_local], 0)
    kv_stretch = jnp.zeros((2, batches, tp_size, rows, 2 * HD), bf16)
    kv_pieces = spread_directly(after(kv_pair, *query_got))
    out_own, out_other = split_sides(after(out_rows, *kv_pieces))
    out_got = spread_directly(out_own)
    w_out = widen_rows(out_got, out_other)
    early = max(1, batches - 1)
    cot_early = cotangent[:early].reshape(early * rows, D)
    cot_early = spread_directly(after(cot_early, *out_got))
    for m, piece in enumerate(kv_pieces):
        kv_stretch = lax.dynamic_update_slice_in_dim(kv_stretch, piece, block_of[m], 2)
    kv_stretch = kv_stretch.reshape(2, batches, stretch, 2 * HD).transpose(1, 0, 2, 3)
    kv_stretch = kv_stretch.reshape(batches, 2, 1, stretch, 2 * HD)
    keyvals = jnp.zeros((batches, 2, 2, stretch, 2 * HD), bf16)
    keyvals = lax.dynamic_update_slice_in_dim(keyvals, kv_stretch, core, 2)
    keyvals = lax.dynamic_update_slice_in_dim(keyvals, swap_core(kv_stretch), 1 - core, 2)
    keyvals = keyvals.reshape(batches, KEY_ROWS, 2 * HD)
    keys = keyvals[:, :, :HD]
    vals = keyvals[:, :, HD:]
    keys_t = keys.transpose(0, 2, 1)
    vals_t = vals.transpose(0, 2, 1)

    own_first = dp_index * stretch + tp_index * rows
    seg_own = lax.dynamic_slice_in_dim(segments, own_first, rows, 1)
    seg_padded = jnp.pad(segments, ((0, 0), (CHIP_ROWS, 0)), constant_values=-1)
    seg_keys = lax.dynamic_slice_in_dim(seg_padded, chip * CHIP_ROWS, KEY_ROWS, 1)
    key_base = (chip - 1) * CHIP_ROWS
    key_place = key_base + jnp.arange(KEY_ROWS)
    tile_heads = max(1, 128 // rows)
    own_place = own_first + jnp.arange(rows)
    allowed = (seg_keys[:, :, None] == seg_own[:, None, :]) & (
        key_place[None, :, None] <= own_place[None, None, :]
    )
    bias = jnp.where(jnp.tile(allowed, (1, 1, tile_heads)), 0.0, masked_score).astype(f32)
    last_block = jnp.broadcast_to(
        (own_first - key_base + rows + KEY_BLOCK - 1) // KEY_BLOCK, (batches,)
    )
    first_block = jnp.maximum(seg_own[:, 0] - key_base, 0) // KEY_BLOCK
    bounds = jnp.stack([first_block, last_block], 1).astype(jnp.int32)

    queries = (rows_by_rows(hidden_one, w_query) + bias_query).astype(bf16)
    queries = queries.reshape(batches, rows, H * HD)
    attended, log_sums = attend_forward(queries, keys, vals_t, bias, bounds)
    attended = attended.reshape(batches * rows, H * HD)
    residual = block_rows + plain_dot(attended, w_out) + bias_out
    ln_two, normed_two, inverse_two = layer_norm_fwd(residual, gain_two, shift_two)
    hidden_two = ln_two.astype(bf16)

    hidden_got = spread(hidden_two)
    cot_late = cotangent[early:].reshape((batches - early) * rows, D)
    cot_late = spread_directly(after(cot_late, *hidden_got))

    def scatter_columns(full):
        return lax.psum_scatter(full, "dp", scatter_dimension=1, tiled=True)

    near = tp_size - 1
    ups = [ffn_up(part, w_up, bias_up) for part in (hidden_got[:near], hidden_got[near:])]
    pre_act = [up[0] for up in ups]
    activated = [up[1] for up in ups]
    product = ffn_product(activated, w_down, tp_size)
    received = deliver(product)
    cot_late = after(cot_late, product)
    cot_got = [jnp.concatenate(pair, 0) for pair in zip(cot_early, cot_late)]
    grad_down = ffn_weight(activated, cot_got)
    grad_pre, grad_bias_up = ffn_back(after(cot_got, grad_down), w_down, pre_act)
    grad_bias_up = grad_bias_up[0]
    grad_hidden = ffn_product([grad_pre], w_up, tp_size)
    shard_down = scatter_columns(after(grad_down, *grad_hidden, *received))
    grad_hidden_parts = deliver(grad_hidden)
    grad_up = ffn_weight([after(grad_pre, *grad_hidden)], hidden_got)
    shard_up = scatter_columns(after(grad_up, *grad_hidden_parts))
    grad_hidden_two = total_of(after(grad_hidden_parts, grad_up))

    cot_rows = cotangent.astype(f32).reshape(batches * rows, D)
    grad_bias_down = jnp.sum(cot_rows, 0)
    grad_resid = cot_rows + layer_norm_back(grad_hidden_two, normed_two, inverse_two, gain_two)
    grad_gain_two = jnp.sum(grad_hidden_two * normed_two, 0)
    grad_shift_two = jnp.sum(grad_hidden_two, 0)
    grad_att = grad_resid.astype(bf16)
    grad_bias_out = jnp.sum(grad_resid, 0)
    cols_half = H * HD // 2
    out_grad_own = cols_by_cols(attended[:, :cols_half], grad_att)
    out_grad_other = cols_by_cols(attended[:, cols_half:], grad_att).astype(bf16)
    grad_heads = rows_by_rows(grad_att, w_out).astype(bf16).reshape(batches, rows, H * HD)

    def reduce_core(own, other):
        own = (own + swap_core(other.astype(bf16)).astype(f32)).astype(bf16)
        size = own.shape[0] // tp_size
        return [own[m * size : (m + 1) * size] for m in range(tp_size)]

    out_pieces = reduce_core(out_grad_own, out_grad_other)
    grad_heads = after(grad_heads, *out_pieces)
    out_pieces = deliver(out_pieces)
    grad_query, grad_key, grad_val = attend_backward(
        queries, grad_heads, keys, keys_t, vals, bias, log_sums, bounds
    )
    grad_query, received = lax.optimization_barrier((grad_query, received))
    result = residual + total_of(received) + bias_down
    outputs = result.astype(bf16).reshape(batches, rows, D)
    grad_query = grad_query.reshape(batches * rows, H * HD)
    grad_bias_query = jnp.sum(grad_query.astype(f32), 0)

    query_grad_other = ffn_weight([grad_query[:, cols_half:]], [hidden_one])
    query_pieces = reduce_core(
        cols_by_cols(grad_query[:, :cols_half], hidden_one), query_grad_other
    )
    out_pieces, shard_up, shard_down = lax.optimization_barrier((out_pieces, shard_up, shard_down))
    part_out = part_out_sum = total_of(out_pieces).astype(bf16)

    def scatter_chips(part):
        return lax.psum_scatter(
            part, "dp", scatter_dimension=1, axis_index_groups=parity, tiled=True
        )

    part_out = scatter_chips(part_out)
    query_got = deliver(query_pieces)
    grad_query = after(grad_query, *query_pieces)

    kv_grads = jnp.concatenate([grad_key, grad_val], 2)
    kv_grads = kv_grads.reshape(batches, 2, 2, stretch, 2 * HD)
    kv_kept = lax.dynamic_slice_in_dim(kv_grads, core, 1, 2)
    kv_sent = lax.dynamic_slice_in_dim(kv_grads, 1 - core, 1, 2).astype(bf16)
    kv_kept = kv_kept + swap_core(kv_sent).astype(f32)
    kv_kept = after(kv_kept, *out_pieces, query_grad_other)
    kv_kept = kv_kept.reshape(batches, 2, tp_size, rows, 2 * HD)
    kv_total = total_of(
        deliver([lax.dynamic_slice_in_dim(kv_kept, at, 1, 2) for at in block_of])
    )
    grad_kv = kv_total[:, 1] + lax.ppermute(
        kv_total[:, 0].astype(bf16), "dp", to_last
    ).astype(f32)
    grad_kv = grad_kv.astype(bf16).reshape(batches * rows, 2 * HD)
    grad_bias_value = jnp.sum(grad_kv[:, HD:].astype(f32), 0)

    grad_hidden_one = plain_dot(grad_query, w_query) + plain_dot(grad_kv, w_keyval)
    grad_rows = grad_resid + layer_norm_back(grad_hidden_one, normed_one, inverse_one, gain_one)
    grad_gain_one = jnp.sum(grad_hidden_one * normed_one, 0)
    grad_shift_one = jnp.sum(grad_hidden_one, 0)
    input_grads = grad_rows.astype(bf16).reshape(batches, rows, D)

    grad_w_keyval = cols_by_cols(after(grad_kv, part_out_sum), hidden_one)
    kv_rows = [lax.dynamic_slice_in_dim(grad_w_keyval, start, kv_half) for start in kv_starts]
    kv_parts = reduce_core(
        jnp.concatenate(kv_rows[:tp_size], 0), jnp.concatenate(kv_rows[tp_size:], 0)
    )
    query_got, kv_parts = lax.optimization_barrier((query_got, kv_parts))
    part_keyval = total_of(deliver(kv_parts))
    part_query = total_of(query_got)
    part_all = jnp.concatenate([part_query, part_keyval], 0).astype(bf16)
    part_all = scatter_chips(after(part_all, part_out))
    part_all = jnp.concatenate([part_all, part_out], 0)
    width = part_all.shape[1] // 2
    mine = lax.dynamic_slice_in_dim(part_all, core * width, width, 1)
    theirs = swap_core(lax.dynamic_slice_in_dim(part_all, (1 - core) * width, width, 1))
    low_half = jnp.where(core == 0, mine, theirs)
    high_half = jnp.where(core == 0, theirs, mine)
    pieces = []
    at = 0
    for size in (half, kv_half, half):
        pieces += [low_half[at : at + size], high_half[at : at + size]]
        at += size
    shard_attention = jnp.concatenate(pieces, 0)

    whole_bias_query = jnp.zeros((H * HD,), f32)
    for index, start in enumerate(query_starts):
        whole_bias_query = lax.dynamic_update_slice_in_dim(
            whole_bias_query, grad_bias_query[index * half : (index + 1) * half], start, 0
        )
    whole_bias_up = lax.dynamic_update_slice_in_dim(
        jnp.zeros((FF,), f32), grad_bias_up, tp_index * ff_rows, 0
    )
    vec_grads = jnp.concatenate(
        [
            grad_gain_one,
            grad_shift_one,
            whole_bias_query,
            grad_bias_value,
            grad_bias_out,
            grad_gain_two,
            grad_shift_two,
            whole_bias_up,
            grad_bias_down,
        ]
    )
    vec_total = sum_everywhere(vec_grads.reshape(-1, 128)).reshape(-1)
    new_vectors, new_vec_one, new_vec_two = adam_step(
        vectors, vec_total, vec_one, vec_two, step_count, learning_rate
    )
    steps_float = step_count[0].astype(f32)
    scalars = jnp.stack(
        [
            learning_rate[0],
            1.0 - jnp.power(beta_one, steps_float),
            1.0 - jnp.power(beta_two, steps_float),
        ]
    )
    state = ()
    for start, grads in (
        (row_starts[4], shard_down),
        (row_starts[3], shard_up),
        (0, shard_attention),
    ):
        block = grads.shape[0] // 2
        if start == 0:
            grads = after(grads, *state)
        state = adam_rows(scalars, master, grads, moment_one, moment_two, start, block, state)
    new_master, new_moment_one, new_moment_two = state
    return (
        outputs,
        input_grads,
        new_master,
        new_moment_one,
        new_moment_two,
        new_vectors,
        new_vec_one,
        new_vec_two,
    )


def solution(mesh):
    in_specs = (
        P(None, ("dp", "tp"), None),
        P(None, ("dp", "tp"), None),
        P(),
        P("tp", "dp"),
        P("tp", "dp"),
        P("tp", "dp"),
        P(),
        P(),
        P(),
        P(),
        P(),
    )
    out_specs = (
        P(None, ("dp", "tp"), None),
        P(None, ("dp", "tp"), None),
        P("tp", "dp"),
        P("tp", "dp"),
        P("tp", "dp"),
        P(),
        P(),
        P(),
    )
    return jax.shard_map(body, mesh=mesh, in_specs=in_specs, out_specs=out_specs, check_vma=False)
```

```python
import functools
import math

import jax
import jax.numpy as jnp
from jax import lax
from jax.experimental import pallas as pl
from jax.experimental.pallas import tpu as pltpu
from jax.sharding import PartitionSpec as P

D = 2048
H = 16
HD = 128
FF = 8192
CHIP_ROWS = 1024
KEY_ROWS = 2 * CHIP_ROWS
KEY_BLOCK = 256
HEAD_GROUP = 4


norm_eps = 1e-05
gelu_coef = math.sqrt(2.0 / math.pi)
beta_one = 0.9
beta_two = 0.95
adam_eps = 1e-08
decay_rate = 0.1
masked_score = -1e30
score_scale = 1.0 / math.sqrt(HD)

bf16 = jnp.bfloat16
f32 = jnp.float32

cheap = pl.CostEstimate(flops=1 << 20, transcendentals=0, bytes_accessed=1 << 20)


def layer_norm_fwd(values, gain, shift):
    mean_row = jnp.mean(values, -1, keepdims=True)
    centered = values - mean_row
    var_row = jnp.mean(centered * centered, -1, keepdims=True)
    inverse = lax.rsqrt(var_row + norm_eps)
    normed = centered * inverse
    return (normed * gain + shift, normed, inverse)


def layer_norm_back(grad_norm, normed, inverse, gain):
    scaled = grad_norm * gain
    return inverse * (
        scaled
        - jnp.mean(scaled, -1, keepdims=True)
        - normed * jnp.mean(scaled * normed, -1, keepdims=True)
    )


def gelu_tanh(values):
    inner = gelu_coef * (values + 0.044715 * values * values * values)
    return 0.5 * values * (1.0 + jnp.tanh(inner))


def gelu_slope(values):
    tangent = jnp.tanh(gelu_coef * (values + 0.044715 * values * values * values))
    return 0.5 * (1.0 + tangent) + 0.5 * values * (1.0 - tangent * tangent) * gelu_coef * (
        1.0 + 3.0 * 0.044715 * values * values
    )


def rows_by_rows(left, right):
    return lax.dot_general(left, right, (((1,), (1,)), ((), ())), preferred_element_type=f32)


def cols_by_cols(left, right):
    return lax.dot_general(left, right, (((0,), (0,)), ((), ())), preferred_element_type=f32)


def plain_dot(left, right):
    return jnp.dot(left, right, preferred_element_type=f32)


def vector_sizes():
    return [D, D, H * HD, HD, D, D, D, FF, D]


def swap(value, axis, step):
    count = lax.axis_size(axis)
    return lax.ppermute(value, axis, [(source, source ^ step) for source in range(count)])


def swap_core(value):
    return swap(value, "dp", 1)


def spread_directly(value):
    return [value] + [swap(value, "tp", m) for m in range(1, lax.axis_size("tp"))]


def cut(value):
    at = value.shape[-2] // 2
    return (value[..., :at, :], value[..., at:, :])


def spread(value):
    if lax.axis_size("tp") != 4:
        return spread_directly(value)
    first = swap(value, "tp", 1)
    second = swap(value, "tp", 2)
    far_top = swap(cut(first)[0], "tp", 2)
    far_low = swap(cut(second)[1], "tp", 1)
    return [value, first, second, far_top, far_low]


def deliver(pieces):
    return [pieces[0]] + [swap(pieces[m].astype(bf16), "tp", m) for m in range(1, len(pieces))]


def far_cuts(count, rows):
    return [rows] * count if count != 4 else [rows] + [rows // 2] * 6


def row_halves(value):
    at = value.shape[0] // 2
    return (slice(0, at), slice(at, 2 * at))


def deliver_halves(pieces):
    if len(pieces) != 7:
        own, *others = deliver(pieces)
        return (own, *([piece[part] for piece in others] for part in row_halves(own)))
    own, one_top, one_low, two_top, two_low, far_top, far_low = pieces
    for_two = swap(far_top, "tp", 1)
    for_one = swap(far_low, "tp", 2)
    got_one_top = swap(one_top, "tp", 1)
    got_two_low = swap(two_low, "tp", 2)
    got_one_low = swap((one_low.astype(f32) + for_one.astype(f32)).astype(bf16), "tp", 1)
    got_two_top = swap((two_top.astype(f32) + for_two.astype(f32)).astype(bf16), "tp", 2)
    return (own, [got_one_top, got_two_top], [got_one_low, got_two_low])


def total_of(pieces):
    total = pieces[0].astype(f32)
    for piece in pieces[1:]:
        total = total + piece.astype(f32)
    return total


def after(value, *others):
    return lax.optimization_barrier((value,) + others)[0]


def sum_everywhere(value):
    for axis in ("dp", "tp"):
        step = 1
        while step < lax.axis_size(axis):
            value = value + swap(value, axis, step)
            step *= 2
    return value


def attend_forward_kernel(bounds, q_ref, k_ref, vt_ref, bias_ref, out_ref, log_ref, keep_ref):
    rows = q_ref.shape[1]
    tile_heads = bias_ref.shape[2] // rows
    tiles = HEAD_GROUP // tile_heads
    width = HEAD_GROUP * rows
    batch = pl.program_id(0)
    first = bounds[batch, 0]
    last = bounds[batch, 1]
    queries = jnp.concatenate(
        [q_ref[0, :, h * HD : (h + 1) * HD] for h in range(HEAD_GROUP)], 0
    )

    def score_block(block, peak):
        start = pl.multiple_of(block * KEY_BLOCK, KEY_BLOCK)
        scores = rows_by_rows(k_ref[0, pl.ds(start, KEY_BLOCK), :], queries) * score_scale
        bias = bias_ref[0, pl.ds(start, KEY_BLOCK), :]
        scores = scores + jnp.concatenate([bias] * tiles, 1)
        keep_ref[pl.ds(start, KEY_BLOCK), :] = scores
        return jnp.maximum(peak, jnp.max(scores, 0, keepdims=True))

    peak = lax.fori_loop(first, last, score_block, jnp.full((1, width), masked_score, f32))

    def exp_block(block, total):
        start = pl.multiple_of(block * KEY_BLOCK, KEY_BLOCK)
        powers = jnp.exp(keep_ref[pl.ds(start, KEY_BLOCK), :] - peak)
        keep_ref[pl.ds(start, KEY_BLOCK), :] = powers
        return total + jnp.sum(powers, 0, keepdims=True)

    total = lax.fori_loop(first, last, exp_block, jnp.zeros((1, width), f32))
    share = 1.0 / total

    def value_block(block, acc):
        start = pl.multiple_of(block * KEY_BLOCK, KEY_BLOCK)
        probs = (keep_ref[pl.ds(start, KEY_BLOCK), :] * share).astype(bf16)
        return acc + plain_dot(vt_ref[0, :, pl.ds(start, KEY_BLOCK)], probs)

    acc = lax.fori_loop(first, last, value_block, jnp.zeros((HD, width), f32))
    for h in range(HEAD_GROUP):
        out_ref[0, :, h * HD : (h + 1) * HD] = acc[:, h * rows : (h + 1) * rows].T.astype(bf16)
    log_ref[0, 0] = peak + jnp.log(total)


def attend_backward_kernel(
    bounds,
    q_ref,
    g_ref,
    k_ref,
    kt_ref,
    v_ref,
    bias_ref,
    log_ref,
    dq_ref,
    dk_ref,
    dv_ref,
    prob_ref,
    dprob_ref,
):
    rows = q_ref.shape[1]
    tile_heads = bias_ref.shape[2] // rows
    tiles = HEAD_GROUP // tile_heads
    width = HEAD_GROUP * rows
    batch = pl.program_id(0)
    first = bounds[batch, 0]
    last = bounds[batch, 1]

    @pl.when(pl.program_id(1) == 0)
    def _():
        dk_ref[...] = jnp.zeros_like(dk_ref)
        dv_ref[...] = jnp.zeros_like(dv_ref)

    queries = jnp.concatenate(
        [q_ref[0, :, h * HD : (h + 1) * HD] for h in range(HEAD_GROUP)], 0
    )
    grads = jnp.concatenate([g_ref[0, :, h * HD : (h + 1) * HD] for h in range(HEAD_GROUP)], 0)
    log_row = log_ref[0, 0]

    def prob_block(block, delta):
        start = pl.multiple_of(block * KEY_BLOCK, KEY_BLOCK)
        scores = rows_by_rows(k_ref[0, pl.ds(start, KEY_BLOCK), :], queries) * score_scale
        bias = bias_ref[0, pl.ds(start, KEY_BLOCK), :]
        probs = jnp.exp(scores + jnp.concatenate([bias] * tiles, 1) - log_row)
        dprobs = rows_by_rows(v_ref[0, pl.ds(start, KEY_BLOCK), :], grads)
        prob_ref[pl.ds(start, KEY_BLOCK), :] = probs
        dprob_ref[pl.ds(start, KEY_BLOCK), :] = dprobs
        return delta + jnp.sum(probs * dprobs, 0, keepdims=True)

    delta = lax.fori_loop(first, last, prob_block, jnp.zeros((1, width), f32))

    def grad_block(block, acc):
        start = pl.multiple_of(block * KEY_BLOCK, KEY_BLOCK)
        probs = prob_ref[pl.ds(start, KEY_BLOCK), :]
        grad_scores = (probs * (dprob_ref[pl.ds(start, KEY_BLOCK), :] - delta)).astype(bf16)
        dk_ref[0, pl.ds(start, KEY_BLOCK), :] += plain_dot(grad_scores, queries) * score_scale
        dv_ref[0, pl.ds(start, KEY_BLOCK), :] += plain_dot(probs.astype(bf16), grads)
        return acc + plain_dot(kt_ref[0, :, pl.ds(start, KEY_BLOCK)], grad_scores)

    acc = lax.fori_loop(first, last, grad_block, jnp.zeros((HD, width), f32)) * score_scale
    for h in range(HEAD_GROUP):
        dq_ref[0, :, h * HD : (h + 1) * HD] = acc[:, h * rows : (h + 1) * rows].T.astype(bf16)


def attend_forward(queries, keys, vals_t, bias, bounds):
    batches, rows, cols = queries.shape
    groups = cols // (HEAD_GROUP * HD)
    width = HEAD_GROUP * rows
    row_spec = pl.BlockSpec((1, rows, HEAD_GROUP * HD), lambda b, g, *_: (b, 0, g))
    return pl.pallas_call(
        attend_forward_kernel,
        name="attend_forward",
        grid_spec=pltpu.PrefetchScalarGridSpec(
            num_scalar_prefetch=1,
            grid=(batches, groups),
            in_specs=[
                row_spec,
                pl.BlockSpec((1, KEY_ROWS, HD), lambda b, g, *_: (b, 0, 0)),
                pl.BlockSpec((1, HD, KEY_ROWS), lambda b, g, *_: (b, 0, 0)),
                pl.BlockSpec((1, KEY_ROWS, bias.shape[2]), lambda b, g, *_: (b, 0, 0)),
            ],
            out_specs=[
                row_spec,
                pl.BlockSpec((1, 1, 1, width), lambda b, g, *_: (b, g, 0, 0)),
            ],
            scratch_shapes=[pltpu.VMEM((KEY_ROWS, width), f32)],
        ),
        out_shape=[
            jax.ShapeDtypeStruct(queries.shape, bf16),
            jax.ShapeDtypeStruct((batches, groups, 1, width), f32),
        ],
        compiler_params=pltpu.CompilerParams(
            dimension_semantics=("arbitrary", "arbitrary"), vmem_limit_bytes=32 << 20
        ),
        cost_estimate=cheap,
    )(bounds, queries, keys, vals_t, bias)


def attend_backward(queries, grads, keys, keys_t, vals, bias, log_sums, bounds):
    batches, rows, cols = queries.shape
    groups = cols // (HEAD_GROUP * HD)
    width = HEAD_GROUP * rows
    row_spec = pl.BlockSpec((1, rows, HEAD_GROUP * HD), lambda b, g, *_: (b, 0, g))
    key_spec = pl.BlockSpec((1, KEY_ROWS, HD), lambda b, g, *_: (b, 0, 0))
    return pl.pallas_call(
        attend_backward_kernel,
        name="attend_backward",
        grid_spec=pltpu.PrefetchScalarGridSpec(
            num_scalar_prefetch=1,
            grid=(batches, groups),
            in_specs=[
                row_spec,
                row_spec,
                key_spec,
                pl.BlockSpec((1, HD, KEY_ROWS), lambda b, g, *_: (b, 0, 0)),
                key_spec,
                pl.BlockSpec((1, KEY_ROWS, bias.shape[2]), lambda b, g, *_: (b, 0, 0)),
                pl.BlockSpec((1, 1, 1, width), lambda b, g, *_: (b, g, 0, 0)),
            ],
            out_specs=[row_spec, key_spec, key_spec],
            scratch_shapes=[
                pltpu.VMEM((KEY_ROWS, width), f32),
                pltpu.VMEM((KEY_ROWS, width), f32),
            ],
        ),
        out_shape=[
            jax.ShapeDtypeStruct(queries.shape, bf16),
            jax.ShapeDtypeStruct(keys.shape, f32),
            jax.ShapeDtypeStruct(keys.shape, f32),
        ],
        compiler_params=pltpu.CompilerParams(
            dimension_semantics=("arbitrary", "arbitrary"), vmem_limit_bytes=40 << 20
        ),
        cost_estimate=cheap,
    )(bounds, queries, grads, keys, keys_t, vals, bias, log_sums)


def gelu_parts(values):
    square = values * values
    return jnp.tanh(values * (gelu_coef + (gelu_coef * 0.044715) * square)), square


def rows_at(refs, at, rows):
    for ref in refs:
        if at < ref.shape[0]:
            return ref[pl.ds(at, rows), :]
        at -= ref.shape[0]


def spans(refs):
    at = 0
    for ref in refs:
        yield ref, at, ref.shape[0]
        at += ref.shape[0]


def ffn_up_kernel(*refs):
    hidden_refs, (weight_ref, bias_ref, pre_ref, act_ref) = refs[:-4], refs[-4:]
    for hidden_ref, at, rows in spans(hidden_refs):
        values = rows_by_rows(hidden_ref[...], weight_ref[...]) + bias_ref[...]
        pre_ref[pl.ds(at, rows), :] = values
        tangent, _ = gelu_parts(values)
        act_ref[pl.ds(at, rows), :] = (0.5 * values * (1.0 + tangent)).astype(bf16)


def ffn_back_kernel(*refs, count):
    cot_refs, weight_ref = refs[:count], refs[count]
    pre_refs, (grad_ref, sum_ref) = refs[count + 1 : -2], refs[-2:]
    total = jnp.zeros(sum_ref.shape, f32)
    for cot_ref, at, rows in spans(cot_refs):
        values = rows_at(pre_refs, at, rows)
        tangent, square = gelu_parts(values)
        slope = 0.5 * (1.0 + tangent) + (0.5 * gelu_coef) * values * (1.0 - tangent * tangent) * (
            1.0 + (3.0 * 0.044715) * square
        )
        grad = (rows_by_rows(cot_ref[...], weight_ref[...]) * slope).astype(bf16)
        grad_ref[pl.ds(at, rows), :] = grad
        total = total + jnp.sum(grad.astype(f32), 0, keepdims=True)
    sum_ref[...] = total


def ffn_product_kernel(*refs, lefts):
    right_ref, out_refs = refs[lefts], refs[lefts + 1 :]
    for out_ref, at, rows in spans(out_refs):
        left = rows_at(refs[:lefts], at, rows)
        out_ref[...] = plain_dot(left, right_ref[...]).astype(bf16)


def ffn_weight_kernel(*refs, lefts):
    right_refs, out_ref = refs[lefts:-1], refs[-1]
    total = None
    for right_ref, at, rows in spans(right_refs):
        part = cols_by_cols(rows_at(refs[:lefts], at, rows), right_ref[...])
        total = part if total is None else total + part
    out_ref[...] = total.astype(bf16)


def ffn_params():
    return pltpu.CompilerParams(
        dimension_semantics=("arbitrary",), vmem_limit_bytes=56 << 20
    )


def whole_specs(pieces):
    return [pl.BlockSpec(piece.shape, lambda i: (0, 0)) for piece in pieces]


def ffn_up(pieces, weights, bias, tile=256):
    units, width = weights.shape
    rows = sum(piece.shape[0] for piece in pieces)
    out_spec = pl.BlockSpec((rows, tile), lambda i: (0, i))
    return pl.pallas_call(
        ffn_up_kernel,
        name="ffn_up",
        grid=(units // tile,),
        in_specs=whole_specs(pieces)
        + [
            pl.BlockSpec((tile, width), lambda i: (i, 0)),
            pl.BlockSpec((1, tile), lambda i: (0, i)),
        ],
        out_specs=[out_spec, out_spec],
        out_shape=[
            jax.ShapeDtypeStruct((rows, units), f32),
            jax.ShapeDtypeStruct((rows, units), bf16),
        ],
        compiler_params=ffn_params(),
        cost_estimate=cheap,
    )(*pieces, weights, bias.reshape(1, units))


def ffn_back(pieces, weights, pre_acts, tile=256):
    units, width = weights.shape
    rows = sum(piece.shape[0] for piece in pieces)
    out_spec = pl.BlockSpec((rows, tile), lambda i: (0, i))
    sum_spec = pl.BlockSpec((1, tile), lambda i: (0, i))
    return pl.pallas_call(
        functools.partial(ffn_back_kernel, count=len(pieces)),
        name="ffn_back",
        grid=(units // tile,),
        in_specs=whole_specs(pieces)
        + [pl.BlockSpec((tile, width), lambda i: (i, 0))]
        + [pl.BlockSpec((part.shape[0], tile), lambda i: (0, i)) for part in pre_acts],
        out_specs=[out_spec, sum_spec],
        out_shape=[
            jax.ShapeDtypeStruct((rows, units), bf16),
            jax.ShapeDtypeStruct((1, units), f32),
        ],
        compiler_params=ffn_params(),
        cost_estimate=cheap,
    )(*pieces, weights, *pre_acts)


def ffn_product(lefts, right, sizes, tile=256):
    units, width = right.shape
    return pl.pallas_call(
        functools.partial(ffn_product_kernel, lefts=len(lefts)),
        name="ffn_product",
        grid=(width // tile,),
        in_specs=whole_specs(lefts) + [pl.BlockSpec((units, tile), lambda i: (0, i))],
        out_specs=[pl.BlockSpec((size, tile), lambda i: (0, i)) for size in sizes],
        out_shape=[jax.ShapeDtypeStruct((size, width), bf16) for size in sizes],
        compiler_params=ffn_params(),
        cost_estimate=cheap,
    )(*lefts, right)


def ffn_weight(lefts, pieces, tile=256, first=0):
    units = lefts[0].shape[1] - first
    skip = first // tile
    width = pieces[0].shape[1]
    return pl.pallas_call(
        functools.partial(ffn_weight_kernel, lefts=len(lefts)),
        name="ffn_weight",
        grid=(units // tile,),
        in_specs=[pl.BlockSpec((left.shape[0], tile), lambda i: (0, i + skip)) for left in lefts]
        + whole_specs(pieces),
        out_specs=pl.BlockSpec((tile, width), lambda i: (i, 0)),
        out_shape=jax.ShapeDtypeStruct((units, width), bf16),
        compiler_params=ffn_params(),
        cost_estimate=cheap,
    )(*lefts, *pieces)


def weight_pieces_kernel(left_ref, right_ref, add_ref, *out_refs):
    total = cols_by_cols(left_ref[...], right_ref[...]) + add_ref[...].astype(f32)
    for m, out_ref in enumerate(out_refs):

        @pl.when(pl.program_id(0) == m)
        def _():
            out_ref[...] = total.astype(bf16)


def weight_pieces(left, right, addend, count):
    rows, width = right.shape
    tile = addend.shape[0] // count
    return pl.pallas_call(
        weight_pieces_kernel,
        name="weight_pieces",
        grid=(count,),
        in_specs=[pl.BlockSpec((rows, tile), lambda i: (0, i))]
        + whole_specs([right])
        + [pl.BlockSpec((tile, width), lambda i: (i, 0))],
        out_specs=[pl.BlockSpec((tile, width), lambda i: (0, 0))] * count,
        out_shape=[jax.ShapeDtypeStruct((tile, width), bf16)] * count,
        compiler_params=ffn_params(),
        cost_estimate=cheap,
    )(left, right, addend)


def onto_rows_kernel(*refs):
    left_ref, bias_ref, piece_refs, out_ref = refs[0], refs[1], refs[2:-1], refs[-1]
    for m, piece_ref in enumerate(piece_refs):

        @pl.when(pl.program_id(0) == m)
        def _():
            out_ref[...] = (rows_by_rows(left_ref[...], piece_ref[...]) + bias_ref[...]).astype(bf16)


def onto_rows(left, pieces, bias):
    tile = pieces[0].shape[0]
    width = tile * len(pieces)
    return pl.pallas_call(
        onto_rows_kernel,
        name="onto_rows",
        grid=(len(pieces),),
        in_specs=whole_specs([left])
        + [pl.BlockSpec((1, tile), lambda i: (0, i))]
        + whole_specs(pieces),
        out_specs=pl.BlockSpec((left.shape[0], tile), lambda i: (0, i)),
        out_shape=jax.ShapeDtypeStruct((left.shape[0], width), bf16),
        compiler_params=ffn_params(),
        cost_estimate=cheap,
    )(left, bias.reshape(1, width), *pieces)


def onto_columns_kernel(*refs, lefts):
    piece_refs, out_ref = refs[lefts:-1], refs[-1]
    total = None
    at, index = 0, 0
    for piece_ref in piece_refs:
        size = piece_ref.shape[0]
        if at == refs[index].shape[1]:
            at, index = 0, index + 1
        part = plain_dot(refs[index][:, at : at + size], piece_ref[...])
        total = part if total is None else total + part
        at += size
    out_ref[...] = total


def onto_columns(lefts, pieces, tile=512):
    rows, width = lefts[0].shape[0], pieces[0].shape[1]
    return pl.pallas_call(
        functools.partial(onto_columns_kernel, lefts=len(lefts)),
        name="onto_columns",
        grid=(width // tile,),
        in_specs=whole_specs(lefts)
        + [pl.BlockSpec((piece.shape[0], tile), lambda i: (0, i)) for piece in pieces],
        out_specs=pl.BlockSpec((rows, tile), lambda i: (0, i)),
        out_shape=jax.ShapeDtypeStruct((rows, width), f32),
        compiler_params=ffn_params(),
        cost_estimate=cheap,
    )(*lefts, *pieces)


def place_keys_kernel(starts, *refs):
    piece_refs, (key_ref, key_t_ref, val_ref, val_t_ref) = refs[:-4], refs[-4:]
    rows = piece_refs[0].shape[2]
    for index, piece_ref in enumerate(piece_refs):
        for which in range(2):
            at = pl.ds(pl.multiple_of(which * CHIP_ROWS + starts[index], rows), rows)
            key_ref[0, at, :] = piece_ref[which, 0, :, :HD]
            val_ref[0, at, :] = piece_ref[which, 0, :, HD:]
    for first in range(0, KEY_ROWS, 128):
        at = slice(first, first + 128)
        key_t_ref[0, :, at] = key_ref[0, at, :].T
        val_t_ref[0, :, at] = val_ref[0, at, :].T


def place_keys(starts, pieces):
    batches, rows = pieces[0].shape[1:3]
    tall = pl.BlockSpec((1, KEY_ROWS, HD), lambda b, *_: (b, 0, 0))
    wide = pl.BlockSpec((1, HD, KEY_ROWS), lambda b, *_: (b, 0, 0))
    return pl.pallas_call(
        place_keys_kernel,
        name="place_keys",
        grid_spec=pltpu.PrefetchScalarGridSpec(
            num_scalar_prefetch=1,
            grid=(batches,),
            in_specs=[pl.BlockSpec((2, 1, rows, 2 * HD), lambda b, *_: (0, b, 0, 0))] * len(pieces),
            out_specs=[tall, wide, tall, wide],
        ),
        out_shape=[
            jax.ShapeDtypeStruct((batches, KEY_ROWS, HD), bf16),
            jax.ShapeDtypeStruct((batches, HD, KEY_ROWS), bf16),
        ]
        * 2,
        compiler_params=ffn_params(),
        cost_estimate=cheap,
    )(starts, *pieces)


def norm_back_kernel(*refs, count):
    own_ref, cot_ref, normed_ref, inverse_ref, gain_ref = refs[:5]
    top_refs, low_refs = refs[5 : 5 + count], refs[5 + count : 5 + 2 * count]
    resid_ref, low_resid_ref, sum_ref = refs[5 + 2 * count :]
    is_top = pl.program_id(0) < 2
    grad = own_ref[...].astype(f32)
    for top_ref, low_ref in zip(top_refs, low_refs):
        grad = grad + jnp.where(is_top, top_ref[...], low_ref[...]).astype(f32)
    normed = normed_ref[...]
    resid = cot_ref[...].astype(f32) + layer_norm_back(
        grad, normed, inverse_ref[...], gain_ref[...]
    )
    resid_ref[...] = resid
    low_resid_ref[...] = resid.astype(bf16)
    sums = [jnp.sum(part, 0, keepdims=True) for part in (grad * normed, grad, resid)]

    @pl.when(pl.program_id(0) == 0)
    def _():
        sum_ref[...] = jnp.zeros_like(sum_ref)

    for index, part in enumerate(sums):
        sum_ref[index : index + 1, :] += part


def norm_back(own, tops, lows, cot, normed, inverse, gain):
    rows, width = own.shape
    block = rows // 4
    by_block = pl.BlockSpec((block, width), lambda i: (i, 0))
    return pl.pallas_call(
        functools.partial(norm_back_kernel, count=len(tops)),
        name="norm_back",
        grid=(4,),
        in_specs=[
            by_block,
            by_block,
            by_block,
            pl.BlockSpec((block, 1), lambda i: (i, 0)),
            pl.BlockSpec((1, width), lambda i: (0, 0)),
        ]
        + [pl.BlockSpec((block, width), lambda i: (jnp.minimum(i, 1), 0))] * len(tops)
        + [pl.BlockSpec((block, width), lambda i: (jnp.maximum(i - 2, 0), 0))] * len(lows),
        out_specs=[by_block, by_block, pl.BlockSpec((8, width), lambda i: (0, 0))],
        out_shape=[
            jax.ShapeDtypeStruct((rows, width), f32),
            jax.ShapeDtypeStruct((rows, width), bf16),
            jax.ShapeDtypeStruct((8, width), f32),
        ],
        compiler_params=ffn_params(),
        cost_estimate=cheap,
    )(own, cot, normed, inverse, gain.reshape(1, width), *tops, *lows)


def adam_step(weights, grads, first, second, step_count, learning_rate):
    steps_float = step_count[0].astype(f32)
    first_new = beta_one * first + (1.0 - beta_one) * grads
    second_new = beta_two * second + (1.0 - beta_two) * grads * grads
    corr_one = 1.0 - jnp.power(beta_one, steps_float)
    corr_two = 1.0 - jnp.power(beta_two, steps_float)
    update = first_new / corr_one / (jnp.sqrt(second_new / corr_two) + adam_eps)
    return (weights - learning_rate[0] * (update + decay_rate * weights), first_new, second_new)


def adam_kernel(scalars, weights, grads, first, second, *refs):
    new_weights, new_first, new_second = refs[-3:]
    rate = scalars[0]
    grad = grads[...].astype(f32)
    first_new = beta_one * first[...] + (1.0 - beta_one) * grad
    second_new = beta_two * second[...] + (1.0 - beta_two) * grad * grad
    update = first_new / scalars[1] / (jnp.sqrt(second_new / scalars[2]) + adam_eps)
    new_weights[...] = weights[...] - rate * (update + decay_rate * weights[...])
    new_first[...] = first_new
    new_second[...] = second_new


def adam_rows(scalars, weights, grads, first, second, start, block, filled):
    count, width = grads.shape

    def placed(i, *_):
        return (pl.multiple_of(start + i * block, 8), 0)

    whole = pl.BlockSpec((pl.Element(block), pl.Element(width)), placed)
    piece = pl.BlockSpec((block, width), lambda i, *_: (i, 0))
    return pl.pallas_call(
        adam_kernel,
        name="adam_rows",
        grid_spec=pltpu.PrefetchScalarGridSpec(
            num_scalar_prefetch=1,
            grid=(count // block,),
            in_specs=[whole, piece, whole, whole]
            + [pl.BlockSpec(memory_space=pl.ANY)] * len(filled),
            out_specs=[whole] * 3,
        ),
        out_shape=[jax.ShapeDtypeStruct(weights.shape, f32)] * 3,
        input_output_aliases={5 + i: i for i in range(len(filled))},
        compiler_params=pltpu.CompilerParams(
            dimension_semantics=("arbitrary",), vmem_limit_bytes=56 << 20
        ),
        cost_estimate=cheap,
    )(scalars, weights, grads, first, second, *filled)


def body(
    block_in,
    cotangent,
    segments,
    master,
    moment_one,
    moment_two,
    vectors,
    vec_one,
    vec_two,
    step_count,
    learning_rate,
):
    tp_size = lax.axis_size("tp")
    dp_size = lax.axis_size("dp")
    tp_index = lax.axis_index("tp")
    dp_index = lax.axis_index("dp")
    core = dp_index % 2
    chip = dp_index // 2
    batches, rows, _ = block_in.shape
    stretch = rows * tp_size
    query_rows = H * HD // tp_size
    kv_share = 2 * HD // tp_size
    ff_rows = FF // tp_size
    half = query_rows // 2
    kv_half = kv_share // 2
    row_starts = [0]
    for length in [query_rows, kv_share, query_rows, ff_rows, ff_rows]:
        row_starts.append(row_starts[-1] + length)
    parity = [[2 * i + c for i in range(dp_size // 2)] for c in range(2)]

    vec_pieces = []
    cursor = 0
    for length in vector_sizes():
        vec_pieces.append(vectors[cursor : cursor + length])
        cursor += length
    (
        gain_one,
        shift_one,
        bias_query_all,
        bias_value,
        bias_out,
        gain_two,
        shift_two,
        bias_up_all,
        bias_down,
    ) = vec_pieces
    bias_up = lax.dynamic_slice_in_dim(bias_up_all, tp_index * ff_rows, ff_rows)
    keyval_bias = jnp.concatenate([jnp.zeros((HD,), f32), bias_value])

    sides = [core, 1 - core]
    block_of = [tp_index ^ m for m in range(tp_size)]
    query_starts = [
        block_of[m] * query_rows + side * half for side in sides for m in range(tp_size)
    ]
    kv_starts = [
        block_of[m] * kv_share + side * kv_half for side in sides for m in range(tp_size)
    ]
    bias_query = jnp.concatenate(
        [lax.dynamic_slice_in_dim(bias_query_all, start, half) for start in query_starts]
    )

    def shard(first, last):
        return master[row_starts[first] : row_starts[last]].astype(bf16)

    def gather_columns(piece):
        return lax.all_gather(piece, "dp", axis=1, tiled=True)

    kv_rows = gather_columns(shard(1, 2))
    query_rows_all = gather_columns(shard(0, 1))
    out_rows = gather_columns(shard(2, 3))
    w_up = gather_columns(shard(3, 4))
    w_down = gather_columns(shard(4, 5))
    def split_sides(block):
        size = block.shape[0] // 2
        return [lax.dynamic_slice_in_dim(block, side * size, size) for side in sides]

    def widen_rows(received, other):
        return received + [other] + [swap_core(piece) for piece in received[1:]]

    w_keyval = jnp.zeros((2 * HD, D), bf16)
    for m, piece in enumerate(spread_directly(kv_rows)):
        w_keyval = lax.dynamic_update_slice_in_dim(w_keyval, piece, block_of[m] * kv_share, 0)
    query_own, query_other = split_sides(query_rows_all)
    query_got = spread_directly(query_own)
    w_query = widen_rows(query_got, query_other)

    block_rows = block_in.astype(f32).reshape(batches * rows, D)
    ln_one, normed_one, inverse_one = layer_norm_fwd(block_rows, gain_one, shift_one)
    hidden_one = ln_one.astype(bf16)
    kv_local = (rows_by_rows(hidden_one, w_keyval) + keyval_bias).astype(bf16)
    kv_local = kv_local.reshape(1, batches, rows, 2 * HD)
    to_next = [(d, d + 2) for d in range(dp_size - 2) if (d // 2) % 2 == 1]
    to_last = [(target, source) for source, target in to_next]
    kv_pair = jnp.concatenate([lax.ppermute(kv_local, "dp", to_next), kv_local], 0)
    kv_pieces = spread_directly(after(kv_pair, *query_got))
    out_own, out_other = split_sides(out_rows)
    out_got = spread_directly(after(out_own, *kv_pieces))
    key_starts = jnp.stack([side * stretch + at * rows for side in sides for at in block_of])
    keys, keys_t, vals, vals_t = place_keys(
        key_starts.astype(jnp.int32), kv_pieces + [swap_core(piece) for piece in kv_pieces]
    )

    own_first = dp_index * stretch + tp_index * rows
    seg_own = lax.dynamic_slice_in_dim(segments, own_first, rows, 1)
    seg_padded = jnp.pad(segments, ((0, 0), (CHIP_ROWS, 0)), constant_values=-1)
    seg_keys = lax.dynamic_slice_in_dim(seg_padded, chip * CHIP_ROWS, KEY_ROWS, 1)
    key_base = (chip - 1) * CHIP_ROWS
    key_place = key_base + jnp.arange(KEY_ROWS)
    tile_heads = max(1, 128 // rows)
    own_place = own_first + jnp.arange(rows)
    allowed = (seg_keys[:, :, None] == seg_own[:, None, :]) & (
        key_place[None, :, None] <= own_place[None, None, :]
    )
    bias = jnp.where(jnp.tile(allowed, (1, 1, tile_heads)), 0.0, masked_score).astype(f32)
    last_block = jnp.broadcast_to(
        (own_first - key_base + rows + KEY_BLOCK - 1) // KEY_BLOCK, (batches,)
    )
    first_block = jnp.maximum(seg_own[:, 0] - key_base, 0) // KEY_BLOCK
    bounds = jnp.stack([first_block, last_block], 1).astype(jnp.int32)

    queries = onto_rows(hidden_one, w_query, bias_query)
    queries = queries.reshape(batches, rows, H * HD)
    attended, log_sums = attend_forward(queries, keys, vals_t, bias, bounds)
    attended = attended.reshape(batches * rows, H * HD)
    w_out = widen_rows(after(out_got, attended), out_other)
    residual = block_rows + onto_columns([attended], w_out) + bias_out
    ln_two, normed_two, inverse_two = layer_norm_fwd(residual, gain_two, shift_two)
    hidden_two = ln_two.astype(bf16)

    hidden_got = spread(hidden_two)
    cot_got = spread_directly(after(cotangent.reshape(batches * rows, D), *hidden_got))

    def scatter_columns(full):
        return lax.psum_scatter(full, "dp", scatter_dimension=1, tiled=True)

    pre_act, activated = ffn_up(hidden_got, w_up, bias_up)
    product = ffn_product([activated], w_down, [batches * rows] * tp_size)
    received = deliver(product)
    cot_got = after(cot_got, product)
    grad_down = ffn_weight([activated], cot_got)
    grad_pre, grad_bias_up = ffn_back(after(cot_got, grad_down), w_down, [pre_act])
    grad_bias_up = grad_bias_up[0]
    grad_hidden = ffn_product([grad_pre], w_up, far_cuts(tp_size, batches * rows))
    shard_down = scatter_columns(after(grad_down, *grad_hidden, *received))
    grad_two_own, grad_two_tops, grad_two_lows = deliver_halves(grad_hidden)
    grad_up = ffn_weight([after(grad_pre, *grad_hidden)], hidden_got)
    shard_up = scatter_columns(after(grad_up, *grad_two_tops, *grad_two_lows))

    cot_rows = cotangent.reshape(batches * rows, D)
    grad_bias_down = jnp.sum(cot_rows.astype(f32), 0)
    grad_resid, grad_att, norm_sums = norm_back(
        after(grad_two_own, grad_up),
        grad_two_tops,
        grad_two_lows,
        cot_rows,
        normed_two,
        inverse_two,
        gain_two,
    )
    grad_gain_two, grad_shift_two, grad_bias_out = norm_sums[0], norm_sums[1], norm_sums[2]
    cols_half = H * HD // 2

    def halves_of(left, right):
        return (cols_by_cols(left[:, :cols_half], right), cols_by_cols(left[:, cols_half:], right))

    def reduce_core(own, other):
        own = (own + other.astype(f32)).astype(bf16)
        size = own.shape[0] // tp_size
        return [own[m * size : (m + 1) * size] for m in range(tp_size)]

    out_grad_own, out_grad_other = halves_of(attended, grad_att)
    out_grad_other = out_grad_other.astype(bf16)
    out_pieces = reduce_core(out_grad_own, swap_core(out_grad_other))
    grad_heads = onto_rows(after(grad_att, *out_pieces), w_out, jnp.zeros((H * HD,), f32))
    grad_heads = grad_heads.reshape(batches, rows, H * HD)
    out_pieces = deliver(out_pieces)
    grad_query, grad_key, grad_val = attend_backward(
        queries, grad_heads, keys, keys_t, vals, bias, log_sums, bounds
    )
    grad_query, received = lax.optimization_barrier((grad_query, received))
    result = residual + total_of(received) + bias_down
    outputs = result.astype(bf16).reshape(batches, rows, D)
    grad_query = grad_query.reshape(batches * rows, H * HD)

    query_grad_other = ffn_weight([after(grad_query, *out_pieces)], [hidden_one], first=cols_half)
    query_pieces = weight_pieces(grad_query, hidden_one, swap_core(query_grad_other), tp_size)
    part_out = part_out_sum = total_of(after(out_pieces, *query_pieces)).astype(bf16)

    def scatter_chips(part):
        return lax.psum_scatter(
            part, "dp", scatter_dimension=1, axis_index_groups=parity, tiled=True
        )

    query_got = deliver(query_pieces)
    grad_query = after(grad_query, *query_pieces)
    grad_bias_query = jnp.sum(grad_query.astype(f32), 0)

    kv_grads = jnp.concatenate([grad_key, grad_val], 2)
    kv_grads = kv_grads.reshape(batches, 2, 2, stretch, 2 * HD)
    kv_kept = lax.dynamic_slice_in_dim(kv_grads, core, 1, 2)
    kv_sent = lax.dynamic_slice_in_dim(kv_grads, 1 - core, 1, 2).astype(bf16)
    kv_kept = kv_kept + swap_core(kv_sent).astype(f32)
    kv_kept = after(kv_kept, *out_pieces, query_grad_other)
    kv_kept = kv_kept.reshape(batches, 2, tp_size, rows, 2 * HD)
    kv_got = deliver([lax.dynamic_slice_in_dim(kv_kept, at, 1, 2) for at in block_of])
    kv_total = total_of(after(kv_got, *query_pieces))
    part_out, shard_up, shard_down, kv_total, _ = lax.optimization_barrier(
        (part_out, shard_up, shard_down, kv_total, query_pieces)
    )
    part_out = scatter_chips(part_out)
    grad_kv = kv_total[:, 1] + lax.ppermute(
        kv_total[:, 0].astype(bf16), "dp", to_last
    ).astype(f32)
    grad_kv = grad_kv.astype(bf16).reshape(batches * rows, 2 * HD)
    grad_bias_value = jnp.sum(grad_kv[:, HD:].astype(f32), 0)

    steps_float = step_count[0].astype(f32)
    scalars = jnp.stack(
        [
            learning_rate[0],
            1.0 - jnp.power(beta_one, steps_float),
            1.0 - jnp.power(beta_two, steps_float),
        ]
    )

    def update_rows(grads, start, filled):
        block = grads.shape[0] // 2
        return adam_rows(scalars, master, grads, moment_one, moment_two, start, block, filled)

    state = update_rows(shard_down, row_starts[4], ())
    state = update_rows(shard_up, row_starts[3], state)
    grad_kv = after(grad_kv, *state)
    grad_hidden_one = onto_columns([grad_query, grad_kv], w_query + [w_keyval])
    grad_rows = grad_resid + layer_norm_back(grad_hidden_one, normed_one, inverse_one, gain_one)
    grad_gain_one = jnp.sum(grad_hidden_one * normed_one, 0)
    grad_shift_one = jnp.sum(grad_hidden_one, 0)
    input_grads = grad_rows.astype(bf16).reshape(batches, rows, D)

    grad_w_keyval = cols_by_cols(after(grad_kv, part_out_sum), hidden_one)
    kv_rows = [lax.dynamic_slice_in_dim(grad_w_keyval, start, kv_half) for start in kv_starts]
    kv_parts = reduce_core(
        jnp.concatenate(kv_rows[:tp_size], 0),
        swap_core(jnp.concatenate(kv_rows[tp_size:], 0).astype(bf16)),
    )
    query_got, kv_parts = lax.optimization_barrier((query_got, kv_parts))
    part_keyval = total_of(deliver(kv_parts))
    part_query = total_of(query_got)
    part_all = jnp.concatenate([part_query, part_keyval], 0).astype(bf16)
    part_all = scatter_chips(after(part_all, part_out))
    part_all = jnp.concatenate([part_all, part_out], 0)
    width = part_all.shape[1] // 2
    mine = lax.dynamic_slice_in_dim(part_all, core * width, width, 1)
    theirs = swap_core(lax.dynamic_slice_in_dim(part_all, (1 - core) * width, width, 1))
    low_half = jnp.where(core == 0, mine, theirs)
    high_half = jnp.where(core == 0, theirs, mine)
    pieces = []
    at = 0
    for size in (half, kv_half, half):
        pieces += [low_half[at : at + size], high_half[at : at + size]]
        at += size
    shard_attention = jnp.concatenate(pieces, 0)

    whole_bias_query = jnp.zeros((H * HD,), f32)
    for index, start in enumerate(query_starts):
        whole_bias_query = lax.dynamic_update_slice_in_dim(
            whole_bias_query, grad_bias_query[index * half : (index + 1) * half], start, 0
        )
    whole_bias_up = lax.dynamic_update_slice_in_dim(
        jnp.zeros((FF,), f32), grad_bias_up, tp_index * ff_rows, 0
    )
    vec_grads = jnp.concatenate(
        [
            grad_gain_one,
            grad_shift_one,
            whole_bias_query,
            grad_bias_value,
            grad_bias_out,
            grad_gain_two,
            grad_shift_two,
            whole_bias_up,
            grad_bias_down,
        ]
    )
    vec_total = sum_everywhere(vec_grads.reshape(-1, 128)).reshape(-1)
    new_vectors, new_vec_one, new_vec_two = adam_step(
        vectors, vec_total, vec_one, vec_two, step_count, learning_rate
    )
    new_state = update_rows(shard_attention, 0, state)
    new_master, new_moment_one, new_moment_two = new_state
    return (
        outputs,
        input_grads,
        new_master,
        new_moment_one,
        new_moment_two,
        new_vectors,
        new_vec_one,
        new_vec_two,
    )


def solution(mesh):
    in_specs = (
        P(None, ("dp", "tp"), None),
        P(None, ("dp", "tp"), None),
        P(),
        P("tp", "dp"),
        P("tp", "dp"),
        P("tp", "dp"),
        P(),
        P(),
        P(),
        P(),
        P(),
    )
    out_specs = (
        P(None, ("dp", "tp"), None),
        P(None, ("dp", "tp"), None),
        P("tp", "dp"),
        P("tp", "dp"),
        P("tp", "dp"),
        P(),
        P(),
        P(),
    )
    return jax.shard_map(body, mesh=mesh, in_specs=in_specs, out_specs=out_specs, check_vma=False)
```

```python
import functools
import math

import jax
import jax.numpy as jnp
from jax import lax
from jax.experimental import pallas as pl
from jax.experimental.pallas import tpu as pltpu
from jax.sharding import PartitionSpec as P

D = 2048
H = 16
HD = 128
FF = 8192
CHIP_ROWS = 1024
KEY_ROWS = 2 * CHIP_ROWS
KEY_BLOCK = 256
HEAD_GROUP = 4


norm_eps = 1e-05
gelu_coef = math.sqrt(2.0 / math.pi)
beta_one = 0.9
beta_two = 0.95
adam_eps = 1e-08
decay_rate = 0.1
masked_score = -1e30
score_scale = 1.0 / math.sqrt(HD)

bf16 = jnp.bfloat16
f32 = jnp.float32

cheap = pl.CostEstimate(flops=1 << 20, transcendentals=0, bytes_accessed=1 << 20)


def layer_norm_fwd(values, gain, shift):
    mean_row = jnp.mean(values, -1, keepdims=True)
    centered = values - mean_row
    var_row = jnp.mean(centered * centered, -1, keepdims=True)
    inverse = lax.rsqrt(var_row + norm_eps)
    normed = centered * inverse
    return (normed * gain + shift, normed, inverse)


def layer_norm_back(grad_norm, normed, inverse, gain):
    scaled = grad_norm * gain
    return inverse * (
        scaled
        - jnp.mean(scaled, -1, keepdims=True)
        - normed * jnp.mean(scaled * normed, -1, keepdims=True)
    )


def gelu_tanh(values):
    inner = gelu_coef * (values + 0.044715 * values * values * values)
    return 0.5 * values * (1.0 + jnp.tanh(inner))


def gelu_slope(values):
    tangent = jnp.tanh(gelu_coef * (values + 0.044715 * values * values * values))
    return 0.5 * (1.0 + tangent) + 0.5 * values * (1.0 - tangent * tangent) * gelu_coef * (
        1.0 + 3.0 * 0.044715 * values * values
    )


def rows_by_rows(left, right):
    return lax.dot_general(left, right, (((1,), (1,)), ((), ())), preferred_element_type=f32)


def cols_by_cols(left, right):
    return lax.dot_general(left, right, (((0,), (0,)), ((), ())), preferred_element_type=f32)


def plain_dot(left, right):
    return jnp.dot(left, right, preferred_element_type=f32)


def vector_sizes():
    return [D, D, H * HD, HD, D, D, D, FF, D]


def swap(value, axis, step):
    count = lax.axis_size(axis)
    return lax.ppermute(value, axis, [(source, source ^ step) for source in range(count)])


def swap_core(value):
    return swap(value, "dp", 1)


def spread_directly(value):
    return [value] + [swap(value, "tp", m) for m in range(1, lax.axis_size("tp"))]


def cut(value):
    at = value.shape[-2] // 2
    return (value[..., :at, :], value[..., at:, :])


def spread(value):
    if lax.axis_size("tp") != 4:
        return spread_directly(value)
    first = swap(value, "tp", 1)
    second = swap(value, "tp", 2)
    far_top = swap(cut(first)[0], "tp", 2)
    far_low = swap(cut(second)[1], "tp", 1)
    return [value, first, second, far_top, far_low]


def deliver(pieces):
    return [pieces[0]] + [swap(pieces[m].astype(bf16), "tp", m) for m in range(1, len(pieces))]


def far_cuts(count, rows):
    return [rows] * count if count != 4 else [rows] + [rows // 2] * 6


def row_halves(value):
    at = value.shape[0] // 2
    return (slice(0, at), slice(at, 2 * at))


def deliver_halves(pieces):
    if len(pieces) != 7:
        own, *others = deliver(pieces)
        return (own, *([piece[part] for piece in others] for part in row_halves(own)))
    own, one_top, one_low, two_top, two_low, far_top, far_low = pieces
    for_two = swap(far_top, "tp", 1)
    for_one = swap(far_low, "tp", 2)
    got_one_top = swap(one_top, "tp", 1)
    got_two_low = swap(two_low, "tp", 2)
    got_one_low = swap((one_low.astype(f32) + for_one.astype(f32)).astype(bf16), "tp", 1)
    got_two_top = swap((two_top.astype(f32) + for_two.astype(f32)).astype(bf16), "tp", 2)
    return (own, [got_one_top, got_two_top], [got_one_low, got_two_low])


def total_of(pieces):
    total = pieces[0].astype(f32)
    for piece in pieces[1:]:
        total = total + piece.astype(f32)
    return total


def after(value, *others):
    return lax.optimization_barrier((value,) + others)[0]


def sum_everywhere(value):
    for axis in ("dp", "tp"):
        step = 1
        while step < lax.axis_size(axis):
            value = value + swap(value, axis, step)
            step *= 2
    return value


def attend_forward_kernel(bounds, q_ref, k_ref, vt_ref, bias_ref, out_ref, log_ref, keep_ref):
    rows = q_ref.shape[1]
    tile_heads = bias_ref.shape[2] // rows
    tiles = HEAD_GROUP // tile_heads
    width = HEAD_GROUP * rows
    batch = pl.program_id(0)
    first = bounds[batch, 0]
    last = bounds[batch, 1]
    queries = jnp.concatenate(
        [q_ref[0, :, h * HD : (h + 1) * HD] for h in range(HEAD_GROUP)], 0
    )

    def score_block(block, peak):
        start = pl.multiple_of(block * KEY_BLOCK, KEY_BLOCK)
        scores = rows_by_rows(k_ref[0, pl.ds(start, KEY_BLOCK), :], queries) * score_scale
        bias = bias_ref[0, pl.ds(start, KEY_BLOCK), :]
        scores = scores + jnp.concatenate([bias] * tiles, 1)
        keep_ref[pl.ds(start, KEY_BLOCK), :] = scores
        return jnp.maximum(peak, jnp.max(scores, 0, keepdims=True))

    peak = lax.fori_loop(first, last, score_block, jnp.full((1, width), masked_score, f32))

    def exp_block(block, total):
        start = pl.multiple_of(block * KEY_BLOCK, KEY_BLOCK)
        powers = jnp.exp(keep_ref[pl.ds(start, KEY_BLOCK), :] - peak)
        keep_ref[pl.ds(start, KEY_BLOCK), :] = powers
        return total + jnp.sum(powers, 0, keepdims=True)

    total = lax.fori_loop(first, last, exp_block, jnp.zeros((1, width), f32))
    share = 1.0 / total

    def value_block(block, acc):
        start = pl.multiple_of(block * KEY_BLOCK, KEY_BLOCK)
        probs = (keep_ref[pl.ds(start, KEY_BLOCK), :] * share).astype(bf16)
        return acc + plain_dot(vt_ref[0, :, pl.ds(start, KEY_BLOCK)], probs)

    acc = lax.fori_loop(first, last, value_block, jnp.zeros((HD, width), f32))
    for h in range(HEAD_GROUP):
        out_ref[0, :, h * HD : (h + 1) * HD] = acc[:, h * rows : (h + 1) * rows].T.astype(bf16)
    log_ref[0, 0] = peak + jnp.log(total)


def attend_backward_kernel(
    bounds,
    q_ref,
    g_ref,
    k_ref,
    kt_ref,
    v_ref,
    bias_ref,
    log_ref,
    dq_ref,
    dkv_ref,
    prob_ref,
    dprob_ref,
):
    rows = q_ref.shape[1]
    tile_heads = bias_ref.shape[2] // rows
    tiles = HEAD_GROUP // tile_heads
    width = HEAD_GROUP * rows
    batch = pl.program_id(0)
    first = bounds[batch, 0]
    last = bounds[batch, 1]

    @pl.when(pl.program_id(1) == 0)
    def _():
        dkv_ref[...] = jnp.zeros_like(dkv_ref)

    queries = jnp.concatenate(
        [q_ref[0, :, h * HD : (h + 1) * HD] for h in range(HEAD_GROUP)], 0
    )
    grads = jnp.concatenate([g_ref[0, :, h * HD : (h + 1) * HD] for h in range(HEAD_GROUP)], 0)
    log_row = log_ref[0, 0]

    def prob_block(block, delta):
        start = pl.multiple_of(block * KEY_BLOCK, KEY_BLOCK)
        scores = rows_by_rows(k_ref[0, pl.ds(start, KEY_BLOCK), :], queries) * score_scale
        bias = bias_ref[0, pl.ds(start, KEY_BLOCK), :]
        probs = jnp.exp(scores + jnp.concatenate([bias] * tiles, 1) - log_row)
        dprobs = rows_by_rows(v_ref[0, pl.ds(start, KEY_BLOCK), :], grads)
        prob_ref[pl.ds(start, KEY_BLOCK), :] = probs
        dprob_ref[pl.ds(start, KEY_BLOCK), :] = dprobs
        return delta + jnp.sum(probs * dprobs, 0, keepdims=True)

    delta = lax.fori_loop(first, last, prob_block, jnp.zeros((1, width), f32))

    def grad_block(block, acc):
        start = pl.multiple_of(block * KEY_BLOCK, KEY_BLOCK)
        probs = prob_ref[pl.ds(start, KEY_BLOCK), :]
        grad_scores = (probs * (dprob_ref[pl.ds(start, KEY_BLOCK), :] - delta)).astype(bf16)
        at = pl.ds(start, KEY_BLOCK)
        dkv_ref[0, at, :HD] += plain_dot(grad_scores, queries) * score_scale
        dkv_ref[0, at, HD:] += plain_dot(probs.astype(bf16), grads)
        return acc + plain_dot(kt_ref[0, :, pl.ds(start, KEY_BLOCK)], grad_scores)

    acc = lax.fori_loop(first, last, grad_block, jnp.zeros((HD, width), f32)) * score_scale
    for h in range(HEAD_GROUP):
        dq_ref[0, :, h * HD : (h + 1) * HD] = acc[:, h * rows : (h + 1) * rows].T.astype(bf16)


def attend_forward(queries, keys, vals_t, bias, bounds):
    batches, rows, cols = queries.shape
    groups = cols // (HEAD_GROUP * HD)
    width = HEAD_GROUP * rows
    row_spec = pl.BlockSpec((1, rows, HEAD_GROUP * HD), lambda b, g, *_: (b, 0, g))
    return pl.pallas_call(
        attend_forward_kernel,
        name="attend_forward",
        grid_spec=pltpu.PrefetchScalarGridSpec(
            num_scalar_prefetch=1,
            grid=(batches, groups),
            in_specs=[
                row_spec,
                pl.BlockSpec((1, KEY_ROWS, HD), lambda b, g, *_: (b, 0, 0)),
                pl.BlockSpec((1, HD, KEY_ROWS), lambda b, g, *_: (b, 0, 0)),
                pl.BlockSpec((1, KEY_ROWS, bias.shape[2]), lambda b, g, *_: (b, 0, 0)),
            ],
            out_specs=[
                row_spec,
                pl.BlockSpec((1, 1, 1, width), lambda b, g, *_: (b, g, 0, 0)),
            ],
            scratch_shapes=[pltpu.VMEM((KEY_ROWS, width), f32)],
        ),
        out_shape=[
            jax.ShapeDtypeStruct(queries.shape, bf16),
            jax.ShapeDtypeStruct((batches, groups, 1, width), f32),
        ],
        compiler_params=pltpu.CompilerParams(
            dimension_semantics=("arbitrary", "arbitrary"), vmem_limit_bytes=32 << 20
        ),
        cost_estimate=cheap,
    )(bounds, queries, keys, vals_t, bias)


def attend_backward(queries, grads, keys, keys_t, vals, bias, log_sums, bounds):
    batches, rows, cols = queries.shape
    groups = cols // (HEAD_GROUP * HD)
    width = HEAD_GROUP * rows
    row_spec = pl.BlockSpec((1, rows, HEAD_GROUP * HD), lambda b, g, *_: (b, 0, g))
    key_spec = pl.BlockSpec((1, KEY_ROWS, HD), lambda b, g, *_: (b, 0, 0))
    return pl.pallas_call(
        attend_backward_kernel,
        name="attend_backward",
        grid_spec=pltpu.PrefetchScalarGridSpec(
            num_scalar_prefetch=1,
            grid=(batches, groups),
            in_specs=[
                row_spec,
                row_spec,
                key_spec,
                pl.BlockSpec((1, HD, KEY_ROWS), lambda b, g, *_: (b, 0, 0)),
                key_spec,
                pl.BlockSpec((1, KEY_ROWS, bias.shape[2]), lambda b, g, *_: (b, 0, 0)),
                pl.BlockSpec((1, 1, 1, width), lambda b, g, *_: (b, g, 0, 0)),
            ],
            out_specs=[
                row_spec,
                pl.BlockSpec((1, KEY_ROWS, 2 * HD), lambda b, g, *_: (b, 0, 0)),
            ],
            scratch_shapes=[
                pltpu.VMEM((KEY_ROWS, width), f32),
                pltpu.VMEM((KEY_ROWS, width), f32),
            ],
        ),
        out_shape=[
            jax.ShapeDtypeStruct(queries.shape, bf16),
            jax.ShapeDtypeStruct((batches, KEY_ROWS, 2 * HD), f32),
        ],
        compiler_params=pltpu.CompilerParams(
            dimension_semantics=("arbitrary", "arbitrary"), vmem_limit_bytes=40 << 20
        ),
        cost_estimate=cheap,
    )(bounds, queries, grads, keys, keys_t, vals, bias, log_sums)


def gelu_parts(values):
    square = values * values
    return jnp.tanh(values * (gelu_coef + (gelu_coef * 0.044715) * square)), square


def rows_at(refs, at, rows):
    for ref in refs:
        if at < ref.shape[0]:
            return ref[pl.ds(at, rows), :]
        at -= ref.shape[0]


def spans(refs):
    at = 0
    for ref in refs:
        yield ref, at, ref.shape[0]
        at += ref.shape[0]


def ffn_up_kernel(*refs):
    hidden_refs, (weight_ref, bias_ref, pre_ref, act_ref) = refs[:-4], refs[-4:]
    for hidden_ref, at, rows in spans(hidden_refs):
        values = rows_by_rows(hidden_ref[...], weight_ref[...]) + bias_ref[...]
        pre_ref[pl.ds(at, rows), :] = values
        tangent, _ = gelu_parts(values)
        act_ref[pl.ds(at, rows), :] = (0.5 * values * (1.0 + tangent)).astype(bf16)


def ffn_back_kernel(*refs, count):
    cot_refs, weight_ref = refs[:count], refs[count]
    pre_refs, (grad_ref, sum_ref) = refs[count + 1 : -2], refs[-2:]
    total = jnp.zeros(sum_ref.shape, f32)
    for cot_ref, at, rows in spans(cot_refs):
        values = rows_at(pre_refs, at, rows)
        tangent, square = gelu_parts(values)
        slope = 0.5 * (1.0 + tangent) + (0.5 * gelu_coef) * values * (1.0 - tangent * tangent) * (
            1.0 + (3.0 * 0.044715) * square
        )
        grad = (rows_by_rows(cot_ref[...], weight_ref[...]) * slope).astype(bf16)
        grad_ref[pl.ds(at, rows), :] = grad
        total = total + jnp.sum(grad.astype(f32), 0, keepdims=True)
    sum_ref[...] = total


def ffn_product_kernel(*refs, lefts):
    right_ref, out_refs = refs[lefts], refs[lefts + 1 :]
    for out_ref, at, rows in spans(out_refs):
        left = rows_at(refs[:lefts], at, rows)
        out_ref[...] = plain_dot(left, right_ref[...]).astype(bf16)


def ffn_weight_kernel(*refs, lefts):
    right_refs, out_ref = refs[lefts:-1], refs[-1]
    total = None
    for right_ref, at, rows in spans(right_refs):
        part = cols_by_cols(rows_at(refs[:lefts], at, rows), right_ref[...])
        total = part if total is None else total + part
    out_ref[...] = total.astype(bf16)


def ffn_params():
    return pltpu.CompilerParams(
        dimension_semantics=("arbitrary",), vmem_limit_bytes=56 << 20
    )


def whole_specs(pieces):
    return [pl.BlockSpec(piece.shape, lambda i: (0, 0)) for piece in pieces]


def ffn_up(pieces, weights, bias, tile=256):
    units, width = weights.shape
    rows = sum(piece.shape[0] for piece in pieces)
    out_spec = pl.BlockSpec((rows, tile), lambda i: (0, i))
    return pl.pallas_call(
        ffn_up_kernel,
        name="ffn_up",
        grid=(units // tile,),
        in_specs=whole_specs(pieces)
        + [
            pl.BlockSpec((tile, width), lambda i: (i, 0)),
            pl.BlockSpec((1, tile), lambda i: (0, i)),
        ],
        out_specs=[out_spec, out_spec],
        out_shape=[
            jax.ShapeDtypeStruct((rows, units), f32),
            jax.ShapeDtypeStruct((rows, units), bf16),
        ],
        compiler_params=ffn_params(),
        cost_estimate=cheap,
    )(*pieces, weights, bias.reshape(1, units))


def ffn_back(pieces, weights, pre_acts, tile=256):
    units, width = weights.shape
    rows = sum(piece.shape[0] for piece in pieces)
    out_spec = pl.BlockSpec((rows, tile), lambda i: (0, i))
    sum_spec = pl.BlockSpec((1, tile), lambda i: (0, i))
    return pl.pallas_call(
        functools.partial(ffn_back_kernel, count=len(pieces)),
        name="ffn_back",
        grid=(units // tile,),
        in_specs=whole_specs(pieces)
        + [pl.BlockSpec((tile, width), lambda i: (i, 0))]
        + [pl.BlockSpec((part.shape[0], tile), lambda i: (0, i)) for part in pre_acts],
        out_specs=[out_spec, sum_spec],
        out_shape=[
            jax.ShapeDtypeStruct((rows, units), bf16),
            jax.ShapeDtypeStruct((1, units), f32),
        ],
        compiler_params=ffn_params(),
        cost_estimate=cheap,
    )(*pieces, weights, *pre_acts)


def ffn_product(lefts, right, sizes, tile=256):
    units, width = right.shape
    return pl.pallas_call(
        functools.partial(ffn_product_kernel, lefts=len(lefts)),
        name="ffn_product",
        grid=(width // tile,),
        in_specs=whole_specs(lefts) + [pl.BlockSpec((units, tile), lambda i: (0, i))],
        out_specs=[pl.BlockSpec((size, tile), lambda i: (0, i)) for size in sizes],
        out_shape=[jax.ShapeDtypeStruct((size, width), bf16) for size in sizes],
        compiler_params=ffn_params(),
        cost_estimate=cheap,
    )(*lefts, right)


def ffn_weight(lefts, pieces, tile=256, first=0):
    units = lefts[0].shape[1] - first
    skip = first // tile
    width = pieces[0].shape[1]
    return pl.pallas_call(
        functools.partial(ffn_weight_kernel, lefts=len(lefts)),
        name="ffn_weight",
        grid=(units // tile,),
        in_specs=[pl.BlockSpec((left.shape[0], tile), lambda i: (0, i + skip)) for left in lefts]
        + whole_specs(pieces),
        out_specs=pl.BlockSpec((tile, width), lambda i: (i, 0)),
        out_shape=jax.ShapeDtypeStruct((units, width), bf16),
        compiler_params=ffn_params(),
        cost_estimate=cheap,
    )(*lefts, *pieces)


def weight_pieces_kernel(left_ref, right_ref, add_ref, *out_refs):
    total = cols_by_cols(left_ref[...], right_ref[...]) + add_ref[...].astype(f32)
    for m, out_ref in enumerate(out_refs):

        @pl.when(pl.program_id(0) == m)
        def _():
            out_ref[...] = total.astype(bf16)


def weight_pieces(left, right, addend, count):
    rows, width = right.shape
    tile = addend.shape[0] // count
    return pl.pallas_call(
        weight_pieces_kernel,
        name="weight_pieces",
        grid=(count,),
        in_specs=[pl.BlockSpec((rows, tile), lambda i: (0, i))]
        + whole_specs([right])
        + [pl.BlockSpec((tile, width), lambda i: (i, 0))],
        out_specs=[pl.BlockSpec((tile, width), lambda i: (0, 0))] * count,
        out_shape=[jax.ShapeDtypeStruct((tile, width), bf16)] * count,
        compiler_params=ffn_params(),
        cost_estimate=cheap,
    )(left, right, addend)


def onto_rows_kernel(*refs, group):
    left_ref, bias_ref, piece_refs, out_ref = refs[0], refs[1], refs[2:-1], refs[-1]
    tile = piece_refs[0].shape[0]
    for first in range(0, len(piece_refs), group):

        @pl.when(pl.program_id(0) == first // group)
        def _():
            for m, piece_ref in enumerate(piece_refs[first : first + group]):
                at = slice(m * tile, (m + 1) * tile)
                product = rows_by_rows(left_ref[...], piece_ref[...])
                out_ref[:, at] = (product + bias_ref[:, at]).astype(bf16)


def onto_rows(left, pieces, bias, group=4):
    tile = pieces[0].shape[0] * group
    width = pieces[0].shape[0] * len(pieces)
    return pl.pallas_call(
        functools.partial(onto_rows_kernel, group=group),
        name="onto_rows",
        grid=(len(pieces) // group,),
        in_specs=whole_specs([left])
        + [pl.BlockSpec((1, tile), lambda i: (0, i))]
        + whole_specs(pieces),
        out_specs=pl.BlockSpec((left.shape[0], tile), lambda i: (0, i)),
        out_shape=jax.ShapeDtypeStruct((left.shape[0], width), bf16),
        compiler_params=ffn_params(),
        cost_estimate=cheap,
    )(left, bias.reshape(1, width), *pieces)


def onto_columns_kernel(*refs, lefts):
    piece_refs, out_ref = refs[lefts:-1], refs[-1]
    total = None
    at, index = 0, 0
    for piece_ref in piece_refs:
        size = piece_ref.shape[0]
        if at == refs[index].shape[1]:
            at, index = 0, index + 1
        part = plain_dot(refs[index][:, at : at + size], piece_ref[...])
        total = part if total is None else total + part
        at += size
    out_ref[...] = total


def onto_columns(lefts, pieces, tile=512):
    rows, width = lefts[0].shape[0], pieces[0].shape[1]
    return pl.pallas_call(
        functools.partial(onto_columns_kernel, lefts=len(lefts)),
        name="onto_columns",
        grid=(width // tile,),
        in_specs=whole_specs(lefts)
        + [pl.BlockSpec((piece.shape[0], tile), lambda i: (0, i)) for piece in pieces],
        out_specs=pl.BlockSpec((rows, tile), lambda i: (0, i)),
        out_shape=jax.ShapeDtypeStruct((rows, width), f32),
        compiler_params=ffn_params(),
        cost_estimate=cheap,
    )(*lefts, *pieces)


def place_keys_kernel(starts, *refs):
    piece_refs, (key_ref, key_t_ref, val_ref, val_t_ref) = refs[:-4], refs[-4:]
    rows = piece_refs[0].shape[2]
    for index, piece_ref in enumerate(piece_refs):
        for which in range(2):
            at = pl.ds(pl.multiple_of(which * CHIP_ROWS + starts[index], rows), rows)
            key_ref[0, at, :] = piece_ref[which, 0, :, :HD]
            val_ref[0, at, :] = piece_ref[which, 0, :, HD:]
    for first in range(0, KEY_ROWS, 128):
        at = slice(first, first + 128)
        key_t_ref[0, :, at] = key_ref[0, at, :].T
        val_t_ref[0, :, at] = val_ref[0, at, :].T


def place_keys(starts, pieces):
    batches, rows = pieces[0].shape[1:3]
    tall = pl.BlockSpec((1, KEY_ROWS, HD), lambda b, *_: (b, 0, 0))
    wide = pl.BlockSpec((1, HD, KEY_ROWS), lambda b, *_: (b, 0, 0))
    return pl.pallas_call(
        place_keys_kernel,
        name="place_keys",
        grid_spec=pltpu.PrefetchScalarGridSpec(
            num_scalar_prefetch=1,
            grid=(batches,),
            in_specs=[pl.BlockSpec((2, 1, rows, 2 * HD), lambda b, *_: (0, b, 0, 0))] * len(pieces),
            out_specs=[tall, wide, tall, wide],
        ),
        out_shape=[
            jax.ShapeDtypeStruct((batches, KEY_ROWS, HD), bf16),
            jax.ShapeDtypeStruct((batches, HD, KEY_ROWS), bf16),
        ]
        * 2,
        compiler_params=ffn_params(),
        cost_estimate=cheap,
    )(starts, *pieces)


def norm_back_kernel(*refs, count):
    own_ref, cot_ref, normed_ref, inverse_ref, gain_ref = refs[:5]
    top_refs, low_refs = refs[5 : 5 + count], refs[5 + count : 5 + 2 * count]
    resid_ref, low_resid_ref, sum_ref = refs[5 + 2 * count :]
    is_top = pl.program_id(0) < 2
    grad = own_ref[...].astype(f32)
    for top_ref, low_ref in zip(top_refs, low_refs):
        grad = grad + jnp.where(is_top, top_ref[...], low_ref[...]).astype(f32)
    normed = normed_ref[...]
    resid = cot_ref[...].astype(f32) + layer_norm_back(
        grad, normed, inverse_ref[...], gain_ref[...]
    )
    resid_ref[...] = resid
    low_resid_ref[...] = resid.astype(bf16)
    sums = [jnp.sum(part, 0, keepdims=True) for part in (grad * normed, grad, resid)]

    @pl.when(pl.program_id(0) == 0)
    def _():
        sum_ref[...] = jnp.zeros_like(sum_ref)

    for index, part in enumerate(sums):
        sum_ref[index : index + 1, :] += part


def norm_back(own, tops, lows, cot, normed, inverse, gain):
    rows, width = own.shape
    block = rows // 4
    by_block = pl.BlockSpec((block, width), lambda i: (i, 0))
    return pl.pallas_call(
        functools.partial(norm_back_kernel, count=len(tops)),
        name="norm_back",
        grid=(4,),
        in_specs=[
            by_block,
            by_block,
            by_block,
            pl.BlockSpec((block, 1), lambda i: (i, 0)),
            pl.BlockSpec((1, width), lambda i: (0, 0)),
        ]
        + [pl.BlockSpec((block, width), lambda i: (jnp.minimum(i, 1), 0))] * len(tops)
        + [pl.BlockSpec((block, width), lambda i: (jnp.maximum(i - 2, 0), 0))] * len(lows),
        out_specs=[by_block, by_block, pl.BlockSpec((8, width), lambda i: (0, 0))],
        out_shape=[
            jax.ShapeDtypeStruct((rows, width), f32),
            jax.ShapeDtypeStruct((rows, width), bf16),
            jax.ShapeDtypeStruct((8, width), f32),
        ],
        compiler_params=ffn_params(),
        cost_estimate=cheap,
    )(own, cot, normed, inverse, gain.reshape(1, width), *tops, *lows)


def adam_step(weights, grads, first, second, step_count, learning_rate):
    steps_float = step_count[0].astype(f32)
    first_new = beta_one * first + (1.0 - beta_one) * grads
    second_new = beta_two * second + (1.0 - beta_two) * grads * grads
    corr_one = 1.0 - jnp.power(beta_one, steps_float)
    corr_two = 1.0 - jnp.power(beta_two, steps_float)
    update = first_new / corr_one / (jnp.sqrt(second_new / corr_two) + adam_eps)
    return (weights - learning_rate[0] * (update + decay_rate * weights), first_new, second_new)


def adam_kernel(scalars, weights, grads, first, second, *refs):
    new_weights, new_first, new_second = refs[-3:]
    rate = scalars[0]
    grad = grads[...].astype(f32)
    first_new = beta_one * first[...] + (1.0 - beta_one) * grad
    second_new = beta_two * second[...] + (1.0 - beta_two) * grad * grad
    update = first_new / scalars[1] / (jnp.sqrt(second_new / scalars[2]) + adam_eps)
    new_weights[...] = weights[...] - rate * (update + decay_rate * weights[...])
    new_first[...] = first_new
    new_second[...] = second_new


def adam_rows(scalars, weights, grads, first, second, start, block, filled):
    count, width = grads.shape

    def placed(i, *_):
        return (pl.multiple_of(start + i * block, 8), 0)

    whole = pl.BlockSpec((pl.Element(block), pl.Element(width)), placed)
    piece = pl.BlockSpec((block, width), lambda i, *_: (i, 0))
    return pl.pallas_call(
        adam_kernel,
        name="adam_rows",
        grid_spec=pltpu.PrefetchScalarGridSpec(
            num_scalar_prefetch=1,
            grid=(count // block,),
            in_specs=[whole, piece, whole, whole]
            + [pl.BlockSpec(memory_space=pl.ANY)] * len(filled),
            out_specs=[whole] * 3,
        ),
        out_shape=[jax.ShapeDtypeStruct(weights.shape, f32)] * 3,
        input_output_aliases={5 + i: i for i in range(len(filled))},
        compiler_params=pltpu.CompilerParams(
            dimension_semantics=("arbitrary",), vmem_limit_bytes=56 << 20
        ),
        cost_estimate=cheap,
    )(scalars, weights, grads, first, second, *filled)


def body(
    block_in,
    cotangent,
    segments,
    master,
    moment_one,
    moment_two,
    vectors,
    vec_one,
    vec_two,
    step_count,
    learning_rate,
):
    tp_size = lax.axis_size("tp")
    dp_size = lax.axis_size("dp")
    tp_index = lax.axis_index("tp")
    dp_index = lax.axis_index("dp")
    core = dp_index % 2
    chip = dp_index // 2
    batches, rows, _ = block_in.shape
    stretch = rows * tp_size
    query_rows = H * HD // tp_size
    kv_share = 2 * HD // tp_size
    ff_rows = FF // tp_size
    half = query_rows // 2
    kv_half = kv_share // 2
    row_starts = [0]
    for length in [query_rows, kv_share, query_rows, ff_rows, ff_rows]:
        row_starts.append(row_starts[-1] + length)
    parity = [[2 * i + c for i in range(dp_size // 2)] for c in range(2)]

    vec_pieces = []
    cursor = 0
    for length in vector_sizes():
        vec_pieces.append(vectors[cursor : cursor + length])
        cursor += length
    (
        gain_one,
        shift_one,
        bias_query_all,
        bias_value,
        bias_out,
        gain_two,
        shift_two,
        bias_up_all,
        bias_down,
    ) = vec_pieces
    bias_up = lax.dynamic_slice_in_dim(bias_up_all, tp_index * ff_rows, ff_rows)
    keyval_bias = jnp.concatenate([jnp.zeros((HD,), f32), bias_value])

    sides = [core, 1 - core]
    block_of = [tp_index ^ m for m in range(tp_size)]
    query_starts = [
        block_of[m] * query_rows + side * half for side in sides for m in range(tp_size)
    ]
    kv_starts = [
        block_of[m] * kv_share + side * kv_half for side in sides for m in range(tp_size)
    ]
    bias_query = jnp.concatenate(
        [lax.dynamic_slice_in_dim(bias_query_all, start, half) for start in query_starts]
    )

    def shard(first, last):
        return master[row_starts[first] : row_starts[last]].astype(bf16)

    def gather_columns(piece):
        return lax.all_gather(piece, "dp", axis=1, tiled=True)

    kv_rows = gather_columns(shard(1, 2))
    query_rows_all = gather_columns(shard(0, 1))
    out_rows = gather_columns(shard(2, 3))
    w_up = gather_columns(shard(3, 4))
    w_down = gather_columns(shard(4, 5))
    def split_sides(block):
        size = block.shape[0] // 2
        return [lax.dynamic_slice_in_dim(block, side * size, size) for side in sides]

    def widen_rows(received, other):
        return received + [other] + [swap_core(piece) for piece in received[1:]]

    w_keyval = jnp.zeros((2 * HD, D), bf16)
    for m, piece in enumerate(spread_directly(kv_rows)):
        w_keyval = lax.dynamic_update_slice_in_dim(w_keyval, piece, block_of[m] * kv_share, 0)
    query_own, query_other = split_sides(query_rows_all)
    query_got = spread_directly(query_own)
    w_query = widen_rows(query_got, query_other)

    block_rows = block_in.astype(f32).reshape(batches * rows, D)
    ln_one, normed_one, inverse_one = layer_norm_fwd(block_rows, gain_one, shift_one)
    hidden_one = ln_one.astype(bf16)
    kv_local = (rows_by_rows(hidden_one, w_keyval) + keyval_bias).astype(bf16)
    kv_local = kv_local.reshape(1, batches, rows, 2 * HD)
    to_next = [(d, d + 2) for d in range(dp_size - 2) if (d // 2) % 2 == 1]
    to_last = [(target, source) for source, target in to_next]
    kv_pair = jnp.concatenate([lax.ppermute(kv_local, "dp", to_next), kv_local], 0)
    kv_pieces = spread_directly(after(kv_pair, *query_got))
    out_own, out_other = split_sides(out_rows)
    out_got = spread_directly(after(out_own, *kv_pieces))
    key_starts = jnp.stack([side * stretch + at * rows for side in sides for at in block_of])
    keys, keys_t, vals, vals_t = place_keys(
        key_starts.astype(jnp.int32), kv_pieces + [swap_core(piece) for piece in kv_pieces]
    )

    own_first = dp_index * stretch + tp_index * rows
    seg_own = lax.dynamic_slice_in_dim(segments, own_first, rows, 1)
    seg_padded = jnp.pad(segments, ((0, 0), (CHIP_ROWS, 0)), constant_values=-1)
    seg_keys = lax.dynamic_slice_in_dim(seg_padded, chip * CHIP_ROWS, KEY_ROWS, 1)
    key_base = (chip - 1) * CHIP_ROWS
    key_place = key_base + jnp.arange(KEY_ROWS)
    tile_heads = max(1, 128 // rows)
    own_place = own_first + jnp.arange(rows)
    allowed = (seg_keys[:, :, None] == seg_own[:, None, :]) & (
        key_place[None, :, None] <= own_place[None, None, :]
    )
    bias = jnp.where(jnp.tile(allowed, (1, 1, tile_heads)), 0.0, masked_score).astype(f32)
    last_block = jnp.broadcast_to(
        (own_first - key_base + rows + KEY_BLOCK - 1) // KEY_BLOCK, (batches,)
    )
    first_block = jnp.maximum(seg_own[:, 0] - key_base, 0) // KEY_BLOCK
    bounds = jnp.stack([first_block, last_block], 1).astype(jnp.int32)

    queries = onto_rows(hidden_one, w_query, bias_query)
    queries = queries.reshape(batches, rows, H * HD)
    attended, log_sums = attend_forward(queries, keys, vals_t, bias, bounds)
    attended = attended.reshape(batches * rows, H * HD)
    w_out = widen_rows(after(out_got, attended), out_other)
    residual = block_rows + onto_columns([attended], w_out) + bias_out
    ln_two, normed_two, inverse_two = layer_norm_fwd(residual, gain_two, shift_two)
    hidden_two = ln_two.astype(bf16)

    hidden_got = spread(hidden_two)
    cot_got = spread_directly(after(cotangent.reshape(batches * rows, D), *hidden_got))

    def scatter_columns(full):
        return lax.psum_scatter(full, "dp", scatter_dimension=1, tiled=True)

    pre_act, activated = ffn_up(hidden_got, w_up, bias_up)
    product = ffn_product([activated], w_down, [batches * rows] * tp_size)
    received = deliver(product)
    cot_got = after(cot_got, product)
    grad_down = ffn_weight([activated], cot_got)
    grad_pre, grad_bias_up = ffn_back(after(cot_got, grad_down), w_down, [pre_act])
    grad_bias_up = grad_bias_up[0]
    grad_hidden = ffn_product([grad_pre], w_up, far_cuts(tp_size, batches * rows))
    shard_down = scatter_columns(after(grad_down, *grad_hidden, *received))
    grad_two_own, grad_two_tops, grad_two_lows = deliver_halves(grad_hidden)
    grad_up = ffn_weight([after(grad_pre, *grad_hidden)], hidden_got)
    shard_up = scatter_columns(after(grad_up, *grad_two_tops, *grad_two_lows))

    cot_rows = cotangent.reshape(batches * rows, D)
    grad_bias_down = jnp.sum(cot_rows.astype(f32), 0)
    grad_resid, grad_att, norm_sums = norm_back(
        after(grad_two_own, grad_up),
        grad_two_tops,
        grad_two_lows,
        cot_rows,
        normed_two,
        inverse_two,
        gain_two,
    )
    grad_gain_two, grad_shift_two, grad_bias_out = norm_sums[0], norm_sums[1], norm_sums[2]
    cols_half = H * HD // 2

    def halves_of(left, right):
        return (cols_by_cols(left[:, :cols_half], right), cols_by_cols(left[:, cols_half:], right))

    def reduce_core(own, other):
        own = (own + other.astype(f32)).astype(bf16)
        size = own.shape[0] // tp_size
        return [own[m * size : (m + 1) * size] for m in range(tp_size)]

    out_grad_own, out_grad_other = halves_of(attended, grad_att)
    out_grad_other = out_grad_other.astype(bf16)
    result = residual + total_of(after(received, out_grad_other)) + bias_down
    outputs = result.astype(bf16).reshape(batches, rows, D)
    out_pieces = reduce_core(out_grad_own, after(swap_core(out_grad_other), outputs))
    grad_heads = onto_rows(after(grad_att, *out_pieces), w_out, jnp.zeros((H * HD,), f32))
    grad_heads = grad_heads.reshape(batches, rows, H * HD)
    out_pieces = deliver(out_pieces)
    grad_query, kv_grads = attend_backward(
        queries, grad_heads, keys, keys_t, vals, bias, log_sums, bounds
    )
    grad_query = grad_query.reshape(batches * rows, H * HD)

    query_grad_other = ffn_weight([after(grad_query, *out_pieces)], [hidden_one], first=cols_half)
    query_pieces = weight_pieces(grad_query, hidden_one, swap_core(query_grad_other), tp_size)
    part_out = part_out_sum = total_of(after(out_pieces, *query_pieces)).astype(bf16)

    def scatter_chips(part):
        return lax.psum_scatter(
            part, "dp", scatter_dimension=1, axis_index_groups=parity, tiled=True
        )

    query_got = deliver(query_pieces)
    grad_query = after(grad_query, *query_pieces)
    grad_bias_query = jnp.sum(grad_query.astype(f32), 0)

    kv_grads = kv_grads.reshape(batches, 2, 2, stretch, 2 * HD)
    kv_kept = lax.dynamic_slice_in_dim(kv_grads, core, 1, 2)
    kv_sent = lax.dynamic_slice_in_dim(kv_grads, 1 - core, 1, 2).astype(bf16)
    kv_kept = kv_kept + swap_core(kv_sent).astype(f32)
    kv_kept = after(kv_kept, *out_pieces, query_grad_other)
    kv_kept = kv_kept.reshape(batches, 2, tp_size, rows, 2 * HD)
    kv_got = deliver([lax.dynamic_slice_in_dim(kv_kept, at, 1, 2) for at in block_of])
    kv_total = total_of(after(kv_got, *query_pieces))
    steps_float = step_count[0].astype(f32)
    scalars = jnp.stack(
        [
            learning_rate[0],
            1.0 - jnp.power(beta_one, steps_float),
            1.0 - jnp.power(beta_two, steps_float),
        ]
    )

    def update_rows(grads, start, filled):
        block = grads.shape[0] // 2
        return adam_rows(scalars, master, grads, moment_one, moment_two, start, block, filled)

    state = update_rows(after(shard_down, *query_pieces), row_starts[4], ())
    part_out, shard_up, kv_total, _, _ = lax.optimization_barrier(
        (part_out, shard_up, kv_total, query_pieces, state)
    )
    part_out = scatter_chips(part_out)
    grad_kv = kv_total[:, 1] + lax.ppermute(
        kv_total[:, 0].astype(bf16), "dp", to_last
    ).astype(f32)
    grad_kv = grad_kv.astype(bf16).reshape(batches * rows, 2 * HD)
    grad_bias_value = jnp.sum(grad_kv[:, HD:].astype(f32), 0)

    grad_w_keyval = cols_by_cols(after(grad_kv, part_out_sum), hidden_one)
    kv_rows = [lax.dynamic_slice_in_dim(grad_w_keyval, start, kv_half) for start in kv_starts]
    kv_parts = reduce_core(
        jnp.concatenate(kv_rows[:tp_size], 0),
        swap_core(jnp.concatenate(kv_rows[tp_size:], 0).astype(bf16)),
    )
    grad_kv = after(grad_kv, *kv_parts)
    kv_parts = deliver(kv_parts)
    grad_hidden_one = onto_columns([grad_query, grad_kv], w_query + [w_keyval])
    grad_rows = grad_resid + layer_norm_back(grad_hidden_one, normed_one, inverse_one, gain_one)
    grad_gain_one = jnp.sum(grad_hidden_one * normed_one, 0)
    grad_shift_one = jnp.sum(grad_hidden_one, 0)
    input_grads = grad_rows.astype(bf16).reshape(batches, rows, D)

    query_got = after(query_got, grad_hidden_one)
    part_keyval = total_of(after(kv_parts, *query_got))
    part_query = total_of(query_got)
    part_all = jnp.concatenate([part_query, part_keyval], 0).astype(bf16)
    state = update_rows(after(shard_up, part_all), row_starts[3], state)
    part_all = after(scatter_chips(after(part_all, part_out)), *state)
    part_all = jnp.concatenate([part_all, part_out], 0)
    width = part_all.shape[1] // 2
    mine = lax.dynamic_slice_in_dim(part_all, core * width, width, 1)
    theirs = swap_core(lax.dynamic_slice_in_dim(part_all, (1 - core) * width, width, 1))
    low_half = jnp.where(core == 0, mine, theirs)
    high_half = jnp.where(core == 0, theirs, mine)
    pieces = []
    at = 0
    for size in (half, kv_half, half):
        pieces += [low_half[at : at + size], high_half[at : at + size]]
        at += size
    shard_attention = jnp.concatenate(pieces, 0)

    whole_bias_query = jnp.zeros((H * HD,), f32)
    for index, start in enumerate(query_starts):
        whole_bias_query = lax.dynamic_update_slice_in_dim(
            whole_bias_query, grad_bias_query[index * half : (index + 1) * half], start, 0
        )
    whole_bias_up = lax.dynamic_update_slice_in_dim(
        jnp.zeros((FF,), f32), grad_bias_up, tp_index * ff_rows, 0
    )
    vec_grads = jnp.concatenate(
        [
            grad_gain_one,
            grad_shift_one,
            whole_bias_query,
            grad_bias_value,
            grad_bias_out,
            grad_gain_two,
            grad_shift_two,
            whole_bias_up,
            grad_bias_down,
        ]
    )
    vec_total = sum_everywhere(vec_grads.reshape(-1, 128)).reshape(-1)
    new_vectors, new_vec_one, new_vec_two = adam_step(
        vectors, vec_total, vec_one, vec_two, step_count, learning_rate
    )
    new_state = update_rows(shard_attention, 0, state)
    new_master, new_moment_one, new_moment_two = new_state
    return (
        outputs,
        input_grads,
        new_master,
        new_moment_one,
        new_moment_two,
        new_vectors,
        new_vec_one,
        new_vec_two,
    )


def solution(mesh):
    in_specs = (
        P(None, ("dp", "tp"), None),
        P(None, ("dp", "tp"), None),
        P(),
        P("tp", "dp"),
        P("tp", "dp"),
        P("tp", "dp"),
        P(),
        P(),
        P(),
        P(),
        P(),
    )
    out_specs = (
        P(None, ("dp", "tp"), None),
        P(None, ("dp", "tp"), None),
        P("tp", "dp"),
        P("tp", "dp"),
        P("tp", "dp"),
        P(),
        P(),
        P(),
    )
    return jax.shard_map(body, mesh=mesh, in_specs=in_specs, out_specs=out_specs, check_vma=False)
```

```python
import functools
import math

import jax
import jax.numpy as jnp
from jax import lax
from jax.experimental import pallas as pl
from jax.experimental.pallas import tpu as pltpu
from jax.sharding import PartitionSpec as P

D = 2048
H = 16
HD = 128
FF = 8192
CHIP_ROWS = 1024
KEY_ROWS = 2 * CHIP_ROWS
KEY_BLOCK = 512
HEAD_GROUP = 4


norm_eps = 1e-05
gelu_coef = math.sqrt(2.0 / math.pi)
beta_one = 0.9
beta_two = 0.95
adam_eps = 1e-08
decay_rate = 0.1
masked_score = -1e30
score_scale = 1.0 / math.sqrt(HD)

bf16 = jnp.bfloat16
f32 = jnp.float32

cheap = pl.CostEstimate(flops=1 << 20, transcendentals=0, bytes_accessed=1 << 20)


def layer_norm_fwd(values, gain, shift):
    mean_row = jnp.mean(values, -1, keepdims=True)
    centered = values - mean_row
    var_row = jnp.mean(centered * centered, -1, keepdims=True)
    inverse = lax.rsqrt(var_row + norm_eps)
    normed = centered * inverse
    return (normed * gain + shift, normed, inverse)


def layer_norm_back(grad_norm, normed, inverse, gain):
    scaled = grad_norm * gain
    return inverse * (
        scaled
        - jnp.mean(scaled, -1, keepdims=True)
        - normed * jnp.mean(scaled * normed, -1, keepdims=True)
    )


def gelu_tanh(values):
    inner = gelu_coef * (values + 0.044715 * values * values * values)
    return 0.5 * values * (1.0 + jnp.tanh(inner))


def gelu_slope(values):
    tangent = jnp.tanh(gelu_coef * (values + 0.044715 * values * values * values))
    return 0.5 * (1.0 + tangent) + 0.5 * values * (1.0 - tangent * tangent) * gelu_coef * (
        1.0 + 3.0 * 0.044715 * values * values
    )


def rows_by_rows(left, right):
    return lax.dot_general(left, right, (((1,), (1,)), ((), ())), preferred_element_type=f32)


def cols_by_cols(left, right):
    return lax.dot_general(left, right, (((0,), (0,)), ((), ())), preferred_element_type=f32)


def plain_dot(left, right):
    return jnp.dot(left, right, preferred_element_type=f32)


def vector_sizes():
    return [D, D, H * HD, HD, D, D, D, FF, D]


def swap(value, axis, step):
    count = lax.axis_size(axis)
    return lax.ppermute(value, axis, [(source, source ^ step) for source in range(count)])


def swap_core(value):
    return swap(value, "dp", 1)


def spread_directly(value):
    return [value] + [swap(value, "tp", m) for m in range(1, lax.axis_size("tp"))]


def cut(value):
    at = value.shape[-2] // 2
    return (value[..., :at, :], value[..., at:, :])


def spread(value):
    if lax.axis_size("tp") != 4:
        return spread_directly(value)
    first = swap(value, "tp", 1)
    second = swap(value, "tp", 2)
    far_top = swap(cut(first)[0], "tp", 2)
    far_low = swap(cut(second)[1], "tp", 1)
    return [value, first, second, far_top, far_low]


def deliver(pieces):
    return [pieces[0]] + [swap(pieces[m].astype(bf16), "tp", m) for m in range(1, len(pieces))]


def far_cuts(count, rows):
    return [rows] * count if count != 4 else [rows] + [rows // 2] * 6


def row_halves(value):
    at = value.shape[0] // 2
    return (slice(0, at), slice(at, 2 * at))


def deliver_halves(pieces):
    if len(pieces) != 7:
        own, *others = deliver(pieces)
        return (own, *([piece[part] for piece in others] for part in row_halves(own)))
    own, one_top, one_low, two_top, two_low, far_top, far_low = pieces
    for_two = swap(far_top, "tp", 1)
    for_one = swap(far_low, "tp", 2)
    got_one_top = swap(one_top, "tp", 1)
    got_two_low = swap(two_low, "tp", 2)
    got_one_low = swap((one_low.astype(f32) + for_one.astype(f32)).astype(bf16), "tp", 1)
    got_two_top = swap((two_top.astype(f32) + for_two.astype(f32)).astype(bf16), "tp", 2)
    return (own, [got_one_top, got_two_top], [got_one_low, got_two_low])


def total_of(pieces):
    total = pieces[0].astype(f32)
    for piece in pieces[1:]:
        total = total + piece.astype(f32)
    return total


def after(value, *others):
    return lax.optimization_barrier((value,) + others)[0]


def sum_everywhere(value):
    for axis in ("dp", "tp"):
        step = 1
        while step < lax.axis_size(axis):
            value = value + swap(value, axis, step)
            step *= 2
    return value


def attend_forward_kernel(bounds, q_ref, k_ref, vt_ref, bias_ref, out_ref, log_ref, keep_ref):
    rows = q_ref.shape[1]
    tile_heads = bias_ref.shape[2] // rows
    tiles = HEAD_GROUP // tile_heads
    width = HEAD_GROUP * rows
    batch = pl.program_id(0)
    first = bounds[batch, 0]
    last = bounds[batch, 1]
    queries = jnp.concatenate(
        [q_ref[0, :, h * HD : (h + 1) * HD] for h in range(HEAD_GROUP)], 0
    )

    def score_block(block, peak):
        start = pl.multiple_of(block * KEY_BLOCK, KEY_BLOCK)
        scores = rows_by_rows(k_ref[0, pl.ds(start, KEY_BLOCK), :], queries) * score_scale
        bias = bias_ref[0, pl.ds(start, KEY_BLOCK), :]
        scores = scores + jnp.concatenate([bias] * tiles, 1)
        keep_ref[pl.ds(start, KEY_BLOCK), :] = scores
        return jnp.maximum(peak, jnp.max(scores, 0, keepdims=True))

    peak = lax.fori_loop(first, last, score_block, jnp.full((1, width), masked_score, f32))

    def exp_block(block, total):
        start = pl.multiple_of(block * KEY_BLOCK, KEY_BLOCK)
        powers = jnp.exp(keep_ref[pl.ds(start, KEY_BLOCK), :] - peak)
        keep_ref[pl.ds(start, KEY_BLOCK), :] = powers
        return total + jnp.sum(powers, 0, keepdims=True)

    total = lax.fori_loop(first, last, exp_block, jnp.zeros((1, width), f32))
    share = 1.0 / total

    def value_block(block, acc):
        start = pl.multiple_of(block * KEY_BLOCK, KEY_BLOCK)
        probs = (keep_ref[pl.ds(start, KEY_BLOCK), :] * share).astype(bf16)
        return acc + plain_dot(vt_ref[0, :, pl.ds(start, KEY_BLOCK)], probs)

    acc = lax.fori_loop(first, last, value_block, jnp.zeros((HD, width), f32))
    for h in range(HEAD_GROUP):
        out_ref[0, :, h * HD : (h + 1) * HD] = acc[:, h * rows : (h + 1) * rows].T.astype(bf16)
    log_ref[0, 0] = peak + jnp.log(total)


def attend_backward_kernel(
    bounds,
    q_ref,
    g_ref,
    k_ref,
    kt_ref,
    v_ref,
    bias_ref,
    log_ref,
    dq_ref,
    dkv_ref,
    prob_ref,
    dprob_ref,
):
    rows = q_ref.shape[1]
    tile_heads = bias_ref.shape[2] // rows
    tiles = HEAD_GROUP // tile_heads
    width = HEAD_GROUP * rows
    batch = pl.program_id(0)
    first = bounds[batch, 0]
    last = bounds[batch, 1]

    @pl.when(pl.program_id(1) == 0)
    def _():
        dkv_ref[...] = jnp.zeros_like(dkv_ref)

    queries = jnp.concatenate(
        [q_ref[0, :, h * HD : (h + 1) * HD] for h in range(HEAD_GROUP)], 0
    )
    grads = jnp.concatenate([g_ref[0, :, h * HD : (h + 1) * HD] for h in range(HEAD_GROUP)], 0)
    log_row = log_ref[0, 0]

    def prob_block(block, delta):
        start = pl.multiple_of(block * KEY_BLOCK, KEY_BLOCK)
        scores = rows_by_rows(k_ref[0, pl.ds(start, KEY_BLOCK), :], queries) * score_scale
        bias = bias_ref[0, pl.ds(start, KEY_BLOCK), :]
        probs = jnp.exp(scores + jnp.concatenate([bias] * tiles, 1) - log_row)
        dprobs = rows_by_rows(v_ref[0, pl.ds(start, KEY_BLOCK), :], grads)
        prob_ref[pl.ds(start, KEY_BLOCK), :] = probs
        dprob_ref[pl.ds(start, KEY_BLOCK), :] = dprobs
        return delta + jnp.sum(probs * dprobs, 0, keepdims=True)

    delta = lax.fori_loop(first, last, prob_block, jnp.zeros((1, width), f32))

    def grad_block(block, acc):
        start = pl.multiple_of(block * KEY_BLOCK, KEY_BLOCK)
        probs = prob_ref[pl.ds(start, KEY_BLOCK), :]
        grad_scores = (probs * (dprob_ref[pl.ds(start, KEY_BLOCK), :] - delta)).astype(bf16)
        at = pl.ds(start, KEY_BLOCK)
        dkv_ref[0, at, :HD] += plain_dot(grad_scores, queries) * score_scale
        dkv_ref[0, at, HD:] += plain_dot(probs.astype(bf16), grads)
        return acc + plain_dot(kt_ref[0, :, pl.ds(start, KEY_BLOCK)], grad_scores)

    acc = lax.fori_loop(first, last, grad_block, jnp.zeros((HD, width), f32)) * score_scale
    for h in range(HEAD_GROUP):
        dq_ref[0, :, h * HD : (h + 1) * HD] = acc[:, h * rows : (h + 1) * rows].T.astype(bf16)


def attend_forward(queries, keys, vals_t, bias, bounds):
    batches, rows, cols = queries.shape
    groups = cols // (HEAD_GROUP * HD)
    width = HEAD_GROUP * rows
    row_spec = pl.BlockSpec((1, rows, HEAD_GROUP * HD), lambda b, g, *_: (b, 0, g))
    return pl.pallas_call(
        attend_forward_kernel,
        name="attend_forward",
        grid_spec=pltpu.PrefetchScalarGridSpec(
            num_scalar_prefetch=1,
            grid=(batches, groups),
            in_specs=[
                row_spec,
                pl.BlockSpec((1, KEY_ROWS, HD), lambda b, g, *_: (b, 0, 0)),
                pl.BlockSpec((1, HD, KEY_ROWS), lambda b, g, *_: (b, 0, 0)),
                pl.BlockSpec((1, KEY_ROWS, bias.shape[2]), lambda b, g, *_: (b, 0, 0)),
            ],
            out_specs=[
                row_spec,
                pl.BlockSpec((1, 1, 1, width), lambda b, g, *_: (b, g, 0, 0)),
            ],
            scratch_shapes=[pltpu.VMEM((KEY_ROWS, width), f32)],
        ),
        out_shape=[
            jax.ShapeDtypeStruct(queries.shape, bf16),
            jax.ShapeDtypeStruct((batches, groups, 1, width), f32),
        ],
        compiler_params=pltpu.CompilerParams(
            dimension_semantics=("arbitrary", "arbitrary"), vmem_limit_bytes=32 << 20
        ),
        cost_estimate=cheap,
    )(bounds, queries, keys, vals_t, bias)


def attend_backward(queries, grads, keys, keys_t, vals, bias, log_sums, bounds):
    batches, rows, cols = queries.shape
    groups = cols // (HEAD_GROUP * HD)
    width = HEAD_GROUP * rows
    row_spec = pl.BlockSpec((1, rows, HEAD_GROUP * HD), lambda b, g, *_: (b, 0, g))
    key_spec = pl.BlockSpec((1, KEY_ROWS, HD), lambda b, g, *_: (b, 0, 0))
    return pl.pallas_call(
        attend_backward_kernel,
        name="attend_backward",
        grid_spec=pltpu.PrefetchScalarGridSpec(
            num_scalar_prefetch=1,
            grid=(batches, groups),
            in_specs=[
                row_spec,
                row_spec,
                key_spec,
                pl.BlockSpec((1, HD, KEY_ROWS), lambda b, g, *_: (b, 0, 0)),
                key_spec,
                pl.BlockSpec((1, KEY_ROWS, bias.shape[2]), lambda b, g, *_: (b, 0, 0)),
                pl.BlockSpec((1, 1, 1, width), lambda b, g, *_: (b, g, 0, 0)),
            ],
            out_specs=[
                row_spec,
                pl.BlockSpec((1, KEY_ROWS, 2 * HD), lambda b, g, *_: (b, 0, 0)),
            ],
            scratch_shapes=[
                pltpu.VMEM((KEY_ROWS, width), f32),
                pltpu.VMEM((KEY_ROWS, width), f32),
            ],
        ),
        out_shape=[
            jax.ShapeDtypeStruct(queries.shape, bf16),
            jax.ShapeDtypeStruct((batches, KEY_ROWS, 2 * HD), f32),
        ],
        compiler_params=pltpu.CompilerParams(
            dimension_semantics=("arbitrary", "arbitrary"), vmem_limit_bytes=40 << 20
        ),
        cost_estimate=cheap,
    )(bounds, queries, grads, keys, keys_t, vals, bias, log_sums)


def gelu_parts(values):
    square = values * values
    return jnp.tanh(values * (gelu_coef + (gelu_coef * 0.044715) * square)), square


def rows_at(refs, at, rows):
    for ref in refs:
        if at < ref.shape[0]:
            return ref[pl.ds(at, rows), :]
        at -= ref.shape[0]


def spans(refs):
    at = 0
    for ref in refs:
        yield ref, at, ref.shape[0]
        at += ref.shape[0]


def ffn_up_kernel(*refs):
    hidden_refs, (weight_ref, bias_ref, pre_ref, act_ref) = refs[:-4], refs[-4:]
    for hidden_ref, at, rows in spans(hidden_refs):
        values = rows_by_rows(hidden_ref[...], weight_ref[...]) + bias_ref[...]
        pre_ref[pl.ds(at, rows), :] = values
        tangent, _ = gelu_parts(values)
        act_ref[pl.ds(at, rows), :] = (0.5 * values * (1.0 + tangent)).astype(bf16)


def ffn_back_kernel(*refs, count):
    cot_refs, weight_ref = refs[:count], refs[count]
    pre_refs, (grad_ref, sum_ref) = refs[count + 1 : -2], refs[-2:]
    total = jnp.zeros(sum_ref.shape, f32)
    for cot_ref, at, rows in spans(cot_refs):
        values = rows_at(pre_refs, at, rows)
        tangent, square = gelu_parts(values)
        slope = 0.5 * (1.0 + tangent) + (0.5 * gelu_coef) * values * (1.0 - tangent * tangent) * (
            1.0 + (3.0 * 0.044715) * square
        )
        grad = (rows_by_rows(cot_ref[...], weight_ref[...]) * slope).astype(bf16)
        grad_ref[pl.ds(at, rows), :] = grad
        total = total + jnp.sum(grad.astype(f32), 0, keepdims=True)
    sum_ref[...] = total


def ffn_product_kernel(*refs, lefts):
    right_ref, out_refs = refs[lefts], refs[lefts + 1 :]
    for out_ref, at, rows in spans(out_refs):
        left = rows_at(refs[:lefts], at, rows)
        out_ref[...] = plain_dot(left, right_ref[...]).astype(bf16)


def ffn_weight_kernel(*refs, lefts):
    right_refs, out_ref = refs[lefts:-1], refs[-1]
    total = None
    for right_ref, at, rows in spans(right_refs):
        part = cols_by_cols(rows_at(refs[:lefts], at, rows), right_ref[...])
        total = part if total is None else total + part
    out_ref[...] = total.astype(bf16)


def ffn_params():
    return pltpu.CompilerParams(
        dimension_semantics=("arbitrary",), vmem_limit_bytes=56 << 20
    )


def whole_specs(pieces):
    return [pl.BlockSpec(piece.shape, lambda i: (0, 0)) for piece in pieces]


def ffn_up(pieces, weights, bias, tile=256):
    units, width = weights.shape
    rows = sum(piece.shape[0] for piece in pieces)
    out_spec = pl.BlockSpec((rows, tile), lambda i: (0, i))
    return pl.pallas_call(
        ffn_up_kernel,
        name="ffn_up",
        grid=(units // tile,),
        in_specs=whole_specs(pieces)
        + [
            pl.BlockSpec((tile, width), lambda i: (i, 0)),
            pl.BlockSpec((1, tile), lambda i: (0, i)),
        ],
        out_specs=[out_spec, out_spec],
        out_shape=[
            jax.ShapeDtypeStruct((rows, units), f32),
            jax.ShapeDtypeStruct((rows, units), bf16),
        ],
        compiler_params=ffn_params(),
        cost_estimate=cheap,
    )(*pieces, weights, bias.reshape(1, units))


def ffn_back(pieces, weights, pre_acts, tile=256):
    units, width = weights.shape
    rows = sum(piece.shape[0] for piece in pieces)
    out_spec = pl.BlockSpec((rows, tile), lambda i: (0, i))
    sum_spec = pl.BlockSpec((1, tile), lambda i: (0, i))
    return pl.pallas_call(
        functools.partial(ffn_back_kernel, count=len(pieces)),
        name="ffn_back",
        grid=(units // tile,),
        in_specs=whole_specs(pieces)
        + [pl.BlockSpec((tile, width), lambda i: (i, 0))]
        + [pl.BlockSpec((part.shape[0], tile), lambda i: (0, i)) for part in pre_acts],
        out_specs=[out_spec, sum_spec],
        out_shape=[
            jax.ShapeDtypeStruct((rows, units), bf16),
            jax.ShapeDtypeStruct((1, units), f32),
        ],
        compiler_params=ffn_params(),
        cost_estimate=cheap,
    )(*pieces, weights, *pre_acts)


def ffn_product(lefts, right, sizes, tile=256):
    units, width = right.shape
    return pl.pallas_call(
        functools.partial(ffn_product_kernel, lefts=len(lefts)),
        name="ffn_product",
        grid=(width // tile,),
        in_specs=whole_specs(lefts) + [pl.BlockSpec((units, tile), lambda i: (0, i))],
        out_specs=[pl.BlockSpec((size, tile), lambda i: (0, i)) for size in sizes],
        out_shape=[jax.ShapeDtypeStruct((size, width), bf16) for size in sizes],
        compiler_params=ffn_params(),
        cost_estimate=cheap,
    )(*lefts, right)


def ffn_weight(lefts, pieces, tile=256, first=0):
    units = lefts[0].shape[1] - first
    skip = first // tile
    width = pieces[0].shape[1]
    return pl.pallas_call(
        functools.partial(ffn_weight_kernel, lefts=len(lefts)),
        name="ffn_weight",
        grid=(units // tile,),
        in_specs=[pl.BlockSpec((left.shape[0], tile), lambda i: (0, i + skip)) for left in lefts]
        + whole_specs(pieces),
        out_specs=pl.BlockSpec((tile, width), lambda i: (i, 0)),
        out_shape=jax.ShapeDtypeStruct((units, width), bf16),
        compiler_params=ffn_params(),
        cost_estimate=cheap,
    )(*lefts, *pieces)


def weight_pieces_kernel(left_ref, right_ref, add_ref, *out_refs):
    total = cols_by_cols(left_ref[...], right_ref[...]) + add_ref[...].astype(f32)
    for m, out_ref in enumerate(out_refs):

        @pl.when(pl.program_id(0) == m)
        def _():
            out_ref[...] = total.astype(bf16)


def weight_pieces(left, right, addend, count):
    rows, width = right.shape
    tile = addend.shape[0] // count
    return pl.pallas_call(
        weight_pieces_kernel,
        name="weight_pieces",
        grid=(count,),
        in_specs=[pl.BlockSpec((rows, tile), lambda i: (0, i))]
        + whole_specs([right])
        + [pl.BlockSpec((tile, width), lambda i: (i, 0))],
        out_specs=[pl.BlockSpec((tile, width), lambda i: (0, 0))] * count,
        out_shape=[jax.ShapeDtypeStruct((tile, width), bf16)] * count,
        compiler_params=ffn_params(),
        cost_estimate=cheap,
    )(left, right, addend)


def onto_rows_kernel(*refs, group):
    left_ref, bias_ref, piece_refs, out_ref = refs[0], refs[1], refs[2:-1], refs[-1]
    tile = piece_refs[0].shape[0]
    for first in range(0, len(piece_refs), group):

        @pl.when(pl.program_id(0) == first // group)
        def _():
            for m, piece_ref in enumerate(piece_refs[first : first + group]):
                at = slice(m * tile, (m + 1) * tile)
                product = rows_by_rows(left_ref[...], piece_ref[...])
                out_ref[:, at] = (product + bias_ref[:, at]).astype(bf16)


def onto_rows(left, pieces, bias, group=4):
    tile = pieces[0].shape[0] * group
    width = pieces[0].shape[0] * len(pieces)
    return pl.pallas_call(
        functools.partial(onto_rows_kernel, group=group),
        name="onto_rows",
        grid=(len(pieces) // group,),
        in_specs=whole_specs([left])
        + [pl.BlockSpec((1, tile), lambda i: (0, i))]
        + whole_specs(pieces),
        out_specs=pl.BlockSpec((left.shape[0], tile), lambda i: (0, i)),
        out_shape=jax.ShapeDtypeStruct((left.shape[0], width), bf16),
        compiler_params=ffn_params(),
        cost_estimate=cheap,
    )(left, bias.reshape(1, width), *pieces)


def onto_columns_kernel(*refs, lefts):
    piece_refs, out_ref = refs[lefts:-1], refs[-1]
    total = None
    at, index = 0, 0
    for piece_ref in piece_refs:
        size = piece_ref.shape[0]
        if at == refs[index].shape[1]:
            at, index = 0, index + 1
        part = plain_dot(refs[index][:, at : at + size], piece_ref[...])
        total = part if total is None else total + part
        at += size
    out_ref[...] = total


def onto_columns(lefts, pieces, tile=512):
    rows, width = lefts[0].shape[0], pieces[0].shape[1]
    return pl.pallas_call(
        functools.partial(onto_columns_kernel, lefts=len(lefts)),
        name="onto_columns",
        grid=(width // tile,),
        in_specs=whole_specs(lefts)
        + [pl.BlockSpec((piece.shape[0], tile), lambda i: (0, i)) for piece in pieces],
        out_specs=pl.BlockSpec((rows, tile), lambda i: (0, i)),
        out_shape=jax.ShapeDtypeStruct((rows, width), f32),
        compiler_params=ffn_params(),
        cost_estimate=cheap,
    )(*lefts, *pieces)


def place_keys_kernel(starts, *refs):
    piece_refs, (key_ref, key_t_ref, val_ref, val_t_ref) = refs[:-4], refs[-4:]
    rows = piece_refs[0].shape[2]
    for index, piece_ref in enumerate(piece_refs):
        for which in range(2):
            at = pl.ds(pl.multiple_of(which * CHIP_ROWS + starts[index], rows), rows)
            key_ref[0, at, :] = piece_ref[which, 0, :, :HD]
            val_ref[0, at, :] = piece_ref[which, 0, :, HD:]
    for first in range(0, KEY_ROWS, 128):
        at = slice(first, first + 128)
        key_t_ref[0, :, at] = key_ref[0, at, :].T
        val_t_ref[0, :, at] = val_ref[0, at, :].T


def place_keys(starts, pieces):
    batches, rows = pieces[0].shape[1:3]
    tall = pl.BlockSpec((1, KEY_ROWS, HD), lambda b, *_: (b, 0, 0))
    wide = pl.BlockSpec((1, HD, KEY_ROWS), lambda b, *_: (b, 0, 0))
    return pl.pallas_call(
        place_keys_kernel,
        name="place_keys",
        grid_spec=pltpu.PrefetchScalarGridSpec(
            num_scalar_prefetch=1,
            grid=(batches,),
            in_specs=[pl.BlockSpec((2, 1, rows, 2 * HD), lambda b, *_: (0, b, 0, 0))] * len(pieces),
            out_specs=[tall, wide, tall, wide],
        ),
        out_shape=[
            jax.ShapeDtypeStruct((batches, KEY_ROWS, HD), bf16),
            jax.ShapeDtypeStruct((batches, HD, KEY_ROWS), bf16),
        ]
        * 2,
        compiler_params=ffn_params(),
        cost_estimate=cheap,
    )(starts, *pieces)


def norm_back_kernel(*refs, count):
    own_ref, cot_ref, normed_ref, inverse_ref, gain_ref = refs[:5]
    top_refs, low_refs = refs[5 : 5 + count], refs[5 + count : 5 + 2 * count]
    resid_ref, low_resid_ref, sum_ref = refs[5 + 2 * count :]
    is_top = pl.program_id(0) < 2
    grad = own_ref[...].astype(f32)
    for top_ref, low_ref in zip(top_refs, low_refs):
        grad = grad + jnp.where(is_top, top_ref[...], low_ref[...]).astype(f32)
    normed = normed_ref[...]
    resid = cot_ref[...].astype(f32) + layer_norm_back(
        grad, normed, inverse_ref[...], gain_ref[...]
    )
    resid_ref[...] = resid
    low_resid_ref[...] = resid.astype(bf16)
    sums = [jnp.sum(part, 0, keepdims=True) for part in (grad * normed, grad, resid)]

    @pl.when(pl.program_id(0) == 0)
    def _():
        sum_ref[...] = jnp.zeros_like(sum_ref)

    for index, part in enumerate(sums):
        sum_ref[index : index + 1, :] += part


def norm_back(own, tops, lows, cot, normed, inverse, gain):
    rows, width = own.shape
    block = rows // 4
    by_block = pl.BlockSpec((block, width), lambda i: (i, 0))
    return pl.pallas_call(
        functools.partial(norm_back_kernel, count=len(tops)),
        name="norm_back",
        grid=(4,),
        in_specs=[
            by_block,
            by_block,
            by_block,
            pl.BlockSpec((block, 1), lambda i: (i, 0)),
            pl.BlockSpec((1, width), lambda i: (0, 0)),
        ]
        + [pl.BlockSpec((block, width), lambda i: (jnp.minimum(i, 1), 0))] * len(tops)
        + [pl.BlockSpec((block, width), lambda i: (jnp.maximum(i - 2, 0), 0))] * len(lows),
        out_specs=[by_block, by_block, pl.BlockSpec((8, width), lambda i: (0, 0))],
        out_shape=[
            jax.ShapeDtypeStruct((rows, width), f32),
            jax.ShapeDtypeStruct((rows, width), bf16),
            jax.ShapeDtypeStruct((8, width), f32),
        ],
        compiler_params=ffn_params(),
        cost_estimate=cheap,
    )(own, cot, normed, inverse, gain.reshape(1, width), *tops, *lows)


def adam_step(weights, grads, first, second, step_count, learning_rate):
    steps_float = step_count[0].astype(f32)
    first_new = beta_one * first + (1.0 - beta_one) * grads
    second_new = beta_two * second + (1.0 - beta_two) * grads * grads
    corr_one = 1.0 - jnp.power(beta_one, steps_float)
    corr_two = 1.0 - jnp.power(beta_two, steps_float)
    update = first_new / corr_one / (jnp.sqrt(second_new / corr_two) + adam_eps)
    return (weights - learning_rate[0] * (update + decay_rate * weights), first_new, second_new)


def adam_kernel(scalars, weights, grads, first, second, *refs):
    new_weights, new_first, new_second = refs[-3:]
    rate = scalars[0]
    grad = grads[...].astype(f32)
    first_new = beta_one * first[...] + (1.0 - beta_one) * grad
    second_new = beta_two * second[...] + (1.0 - beta_two) * grad * grad
    update = first_new / scalars[1] / (jnp.sqrt(second_new / scalars[2]) + adam_eps)
    new_weights[...] = weights[...] - rate * (update + decay_rate * weights[...])
    new_first[...] = first_new
    new_second[...] = second_new


def adam_rows(scalars, weights, grads, first, second, start, block, filled):
    count, width = grads.shape

    def placed(i, *_):
        return (pl.multiple_of(start + i * block, 8), 0)

    whole = pl.BlockSpec((pl.Element(block), pl.Element(width)), placed)
    piece = pl.BlockSpec((block, width), lambda i, *_: (i, 0))
    return pl.pallas_call(
        adam_kernel,
        name="adam_rows",
        grid_spec=pltpu.PrefetchScalarGridSpec(
            num_scalar_prefetch=1,
            grid=(count // block,),
            in_specs=[whole, piece, whole, whole]
            + [pl.BlockSpec(memory_space=pl.ANY)] * len(filled),
            out_specs=[whole] * 3,
        ),
        out_shape=[jax.ShapeDtypeStruct(weights.shape, f32)] * 3,
        input_output_aliases={5 + i: i for i in range(len(filled))},
        compiler_params=pltpu.CompilerParams(
            dimension_semantics=("arbitrary",), vmem_limit_bytes=56 << 20
        ),
        cost_estimate=cheap,
    )(scalars, weights, grads, first, second, *filled)


def body(
    block_in,
    cotangent,
    segments,
    master,
    moment_one,
    moment_two,
    vectors,
    vec_one,
    vec_two,
    step_count,
    learning_rate,
):
    tp_size = lax.axis_size("tp")
    dp_size = lax.axis_size("dp")
    tp_index = lax.axis_index("tp")
    dp_index = lax.axis_index("dp")
    core = dp_index % 2
    chip = dp_index // 2
    batches, rows, _ = block_in.shape
    stretch = rows * tp_size
    query_rows = H * HD // tp_size
    kv_share = 2 * HD // tp_size
    ff_rows = FF // tp_size
    half = query_rows // 2
    kv_half = kv_share // 2
    row_starts = [0]
    for length in [query_rows, kv_share, query_rows, ff_rows, ff_rows]:
        row_starts.append(row_starts[-1] + length)
    parity = [[2 * i + c for i in range(dp_size // 2)] for c in range(2)]

    vec_pieces = []
    cursor = 0
    for length in vector_sizes():
        vec_pieces.append(vectors[cursor : cursor + length])
        cursor += length
    (
        gain_one,
        shift_one,
        bias_query_all,
        bias_value,
        bias_out,
        gain_two,
        shift_two,
        bias_up_all,
        bias_down,
    ) = vec_pieces
    bias_up = lax.dynamic_slice_in_dim(bias_up_all, tp_index * ff_rows, ff_rows)
    keyval_bias = jnp.concatenate([jnp.zeros((HD,), f32), bias_value])

    sides = [core, 1 - core]
    block_of = [tp_index ^ m for m in range(tp_size)]
    query_starts = [
        block_of[m] * query_rows + side * half for side in sides for m in range(tp_size)
    ]
    kv_starts = [
        block_of[m] * kv_share + side * kv_half for side in sides for m in range(tp_size)
    ]
    bias_query = jnp.concatenate(
        [lax.dynamic_slice_in_dim(bias_query_all, start, half) for start in query_starts]
    )

    def shard(first, last):
        return master[row_starts[first] : row_starts[last]].astype(bf16)

    def gather_columns(piece):
        return lax.all_gather(piece, "dp", axis=1, tiled=True)

    kv_rows = gather_columns(shard(1, 2))
    query_rows_all = gather_columns(shard(0, 1))
    out_rows = gather_columns(shard(2, 3))
    w_up = gather_columns(shard(3, 4))
    w_down = gather_columns(shard(4, 5))
    def split_sides(block):
        size = block.shape[0] // 2
        return [lax.dynamic_slice_in_dim(block, side * size, size) for side in sides]

    def widen_rows(received, other):
        return received + [other] + [swap_core(piece) for piece in received[1:]]

    w_keyval = jnp.zeros((2 * HD, D), bf16)
    for m, piece in enumerate(spread_directly(kv_rows)):
        w_keyval = lax.dynamic_update_slice_in_dim(w_keyval, piece, block_of[m] * kv_share, 0)
    query_own, query_other = split_sides(query_rows_all)
    query_got = spread_directly(query_own)
    w_query = widen_rows(query_got, query_other)

    block_rows = block_in.astype(f32).reshape(batches * rows, D)
    ln_one, normed_one, inverse_one = layer_norm_fwd(block_rows, gain_one, shift_one)
    hidden_one = ln_one.astype(bf16)
    kv_local = (rows_by_rows(hidden_one, w_keyval) + keyval_bias).astype(bf16)
    kv_local = kv_local.reshape(1, batches, rows, 2 * HD)
    to_next = [(d, d + 2) for d in range(dp_size - 2) if (d // 2) % 2 == 1]
    to_last = [(target, source) for source, target in to_next]
    kv_pair = jnp.concatenate([lax.ppermute(kv_local, "dp", to_next), kv_local], 0)
    kv_pieces = spread_directly(after(kv_pair, *query_got))
    out_own, out_other = split_sides(out_rows)
    out_got = spread_directly(after(out_own, *kv_pieces))
    key_starts = jnp.stack([side * stretch + at * rows for side in sides for at in block_of])
    keys, keys_t, vals, vals_t = place_keys(
        key_starts.astype(jnp.int32), kv_pieces + [swap_core(piece) for piece in kv_pieces]
    )

    own_first = dp_index * stretch + tp_index * rows
    seg_own = lax.dynamic_slice_in_dim(segments, own_first, rows, 1)
    seg_padded = jnp.pad(segments, ((0, 0), (CHIP_ROWS, 0)), constant_values=-1)
    seg_keys = lax.dynamic_slice_in_dim(seg_padded, chip * CHIP_ROWS, KEY_ROWS, 1)
    key_base = (chip - 1) * CHIP_ROWS
    key_place = key_base + jnp.arange(KEY_ROWS)
    tile_heads = max(1, 128 // rows)
    own_place = own_first + jnp.arange(rows)
    allowed = (seg_keys[:, :, None] == seg_own[:, None, :]) & (
        key_place[None, :, None] <= own_place[None, None, :]
    )
    bias = jnp.where(jnp.tile(allowed, (1, 1, tile_heads)), 0.0, masked_score).astype(f32)
    last_block = jnp.broadcast_to(
        (own_first - key_base + rows + KEY_BLOCK - 1) // KEY_BLOCK, (batches,)
    )
    first_block = jnp.maximum(seg_own[:, 0] - key_base, 0) // KEY_BLOCK
    bounds = jnp.stack([first_block, last_block], 1).astype(jnp.int32)

    queries = onto_rows(hidden_one, w_query, bias_query)
    queries = queries.reshape(batches, rows, H * HD)
    attended, log_sums = attend_forward(queries, keys, vals_t, bias, bounds)
    attended = attended.reshape(batches * rows, H * HD)
    w_out = widen_rows(after(out_got, attended), out_other)
    residual = block_rows + onto_columns([attended], w_out) + bias_out
    ln_two, normed_two, inverse_two = layer_norm_fwd(residual, gain_two, shift_two)
    hidden_two = ln_two.astype(bf16)

    hidden_got = spread(hidden_two)
    cot_got = spread_directly(after(cotangent.reshape(batches * rows, D), *hidden_got))

    def scatter_columns(full):
        return lax.psum_scatter(full, "dp", scatter_dimension=1, tiled=True)

    pre_act, activated = ffn_up(hidden_got, w_up, bias_up)
    product = ffn_product([activated], w_down, [batches * rows] * tp_size)
    received = deliver(product)
    cot_got = after(cot_got, product)
    grad_down = ffn_weight([activated], cot_got)
    grad_pre, grad_bias_up = ffn_back(after(cot_got, grad_down), w_down, [pre_act])
    grad_bias_up = grad_bias_up[0]
    grad_hidden = ffn_product([grad_pre], w_up, far_cuts(tp_size, batches * rows))
    shard_down = scatter_columns(after(grad_down, *grad_hidden, *received))
    grad_two_own, grad_two_tops, grad_two_lows = deliver_halves(grad_hidden)
    grad_up = ffn_weight([after(grad_pre, *grad_hidden)], hidden_got)
    shard_up = scatter_columns(after(grad_up, *grad_two_tops, *grad_two_lows))

    cot_rows = cotangent.reshape(batches * rows, D)
    grad_bias_down = jnp.sum(cot_rows.astype(f32), 0)
    grad_resid, grad_att, norm_sums = norm_back(
        after(grad_two_own, grad_up),
        grad_two_tops,
        grad_two_lows,
        cot_rows,
        normed_two,
        inverse_two,
        gain_two,
    )
    grad_gain_two, grad_shift_two, grad_bias_out = norm_sums[0], norm_sums[1], norm_sums[2]
    cols_half = H * HD // 2

    def halves_of(left, right):
        return (cols_by_cols(left[:, :cols_half], right), cols_by_cols(left[:, cols_half:], right))

    def reduce_core(own, other):
        own = (own + other.astype(f32)).astype(bf16)
        size = own.shape[0] // tp_size
        return [own[m * size : (m + 1) * size] for m in range(tp_size)]

    out_grad_own, out_grad_other = halves_of(attended, grad_att)
    out_grad_other = out_grad_other.astype(bf16)
    result = residual + total_of(after(received, out_grad_other)) + bias_down
    outputs = result.astype(bf16).reshape(batches, rows, D)
    out_pieces = reduce_core(out_grad_own, after(swap_core(out_grad_other), outputs))
    grad_heads = onto_rows(after(grad_att, *out_pieces), w_out, jnp.zeros((H * HD,), f32))
    grad_heads = grad_heads.reshape(batches, rows, H * HD)
    out_pieces = deliver(out_pieces)
    grad_query, kv_grads = attend_backward(
        queries, grad_heads, keys, keys_t, vals, bias, log_sums, bounds
    )
    grad_query = grad_query.reshape(batches * rows, H * HD)

    query_grad_other = ffn_weight([after(grad_query, *out_pieces)], [hidden_one], first=cols_half)
    query_pieces = weight_pieces(grad_query, hidden_one, swap_core(query_grad_other), tp_size)
    part_out = part_out_sum = total_of(after(out_pieces, *query_pieces)).astype(bf16)

    def scatter_chips(part):
        return lax.psum_scatter(
            part, "dp", scatter_dimension=1, axis_index_groups=parity, tiled=True
        )

    query_got = deliver(query_pieces)
    grad_query = after(grad_query, *query_pieces)
    grad_bias_query = jnp.sum(grad_query.astype(f32), 0)

    kv_grads = kv_grads.reshape(batches, 2, 2, stretch, 2 * HD)
    kv_kept = lax.dynamic_slice_in_dim(kv_grads, core, 1, 2)
    kv_sent = lax.dynamic_slice_in_dim(kv_grads, 1 - core, 1, 2).astype(bf16)
    kv_kept = kv_kept + swap_core(kv_sent).astype(f32)
    kv_kept = after(kv_kept, *out_pieces, query_grad_other)
    kv_kept = kv_kept.reshape(batches, 2, tp_size, rows, 2 * HD)
    kv_got = deliver([lax.dynamic_slice_in_dim(kv_kept, at, 1, 2) for at in block_of])
    kv_total = total_of(after(kv_got, *query_pieces))
    steps_float = step_count[0].astype(f32)
    scalars = jnp.stack(
        [
            learning_rate[0],
            1.0 - jnp.power(beta_one, steps_float),
            1.0 - jnp.power(beta_two, steps_float),
        ]
    )

    def update_rows(grads, start, filled):
        block = grads.shape[0] // 2
        return adam_rows(scalars, master, grads, moment_one, moment_two, start, block, filled)

    state = update_rows(after(shard_down, *query_pieces), row_starts[4], ())
    part_out, shard_up, kv_total, _, _ = lax.optimization_barrier(
        (part_out, shard_up, kv_total, query_pieces, state)
    )
    part_out = scatter_chips(part_out)
    grad_kv = kv_total[:, 1] + lax.ppermute(
        kv_total[:, 0].astype(bf16), "dp", to_last
    ).astype(f32)
    grad_kv = grad_kv.astype(bf16).reshape(batches * rows, 2 * HD)
    grad_bias_value = jnp.sum(grad_kv[:, HD:].astype(f32), 0)

    grad_w_keyval = cols_by_cols(after(grad_kv, part_out_sum), hidden_one)
    kv_rows = [lax.dynamic_slice_in_dim(grad_w_keyval, start, kv_half) for start in kv_starts]
    kv_parts = reduce_core(
        jnp.concatenate(kv_rows[:tp_size], 0),
        swap_core(jnp.concatenate(kv_rows[tp_size:], 0).astype(bf16)),
    )
    grad_kv = after(grad_kv, *kv_parts)
    kv_parts = deliver(kv_parts)
    grad_hidden_one = onto_columns([grad_query, grad_kv], w_query + [w_keyval])
    grad_rows = grad_resid + layer_norm_back(grad_hidden_one, normed_one, inverse_one, gain_one)
    grad_gain_one = jnp.sum(grad_hidden_one * normed_one, 0)
    grad_shift_one = jnp.sum(grad_hidden_one, 0)
    input_grads = grad_rows.astype(bf16).reshape(batches, rows, D)

    query_got = after(query_got, grad_hidden_one)
    part_keyval = total_of(after(kv_parts, *query_got))
    part_query = total_of(query_got)
    part_all = jnp.concatenate([part_query, part_keyval], 0).astype(bf16)
    state = update_rows(after(shard_up, part_all), row_starts[3], state)
    part_all = after(scatter_chips(after(part_all, part_out)), *state)
    part_all = jnp.concatenate([part_all, part_out], 0)
    width = part_all.shape[1] // 2
    mine = lax.dynamic_slice_in_dim(part_all, core * width, width, 1)
    theirs = swap_core(lax.dynamic_slice_in_dim(part_all, (1 - core) * width, width, 1))
    low_half = jnp.where(core == 0, mine, theirs)
    high_half = jnp.where(core == 0, theirs, mine)
    pieces = []
    at = 0
    for size in (half, kv_half, half):
        pieces += [low_half[at : at + size], high_half[at : at + size]]
        at += size
    shard_attention = jnp.concatenate(pieces, 0)

    whole_bias_query = jnp.zeros((H * HD,), f32)
    for index, start in enumerate(query_starts):
        whole_bias_query = lax.dynamic_update_slice_in_dim(
            whole_bias_query, grad_bias_query[index * half : (index + 1) * half], start, 0
        )
    whole_bias_up = lax.dynamic_update_slice_in_dim(
        jnp.zeros((FF,), f32), grad_bias_up, tp_index * ff_rows, 0
    )
    vec_grads = jnp.concatenate(
        [
            grad_gain_one,
            grad_shift_one,
            whole_bias_query,
            grad_bias_value,
            grad_bias_out,
            grad_gain_two,
            grad_shift_two,
            whole_bias_up,
            grad_bias_down,
        ]
    )
    vec_total = sum_everywhere(vec_grads.reshape(-1, 128)).reshape(-1)
    new_vectors, new_vec_one, new_vec_two = adam_step(
        vectors, vec_total, vec_one, vec_two, step_count, learning_rate
    )
    new_state = update_rows(shard_attention, 0, state)
    new_master, new_moment_one, new_moment_two = new_state
    return (
        outputs,
        input_grads,
        new_master,
        new_moment_one,
        new_moment_two,
        new_vectors,
        new_vec_one,
        new_vec_two,
    )


def solution(mesh):
    in_specs = (
        P(None, ("dp", "tp"), None),
        P(None, ("dp", "tp"), None),
        P(),
        P("tp", "dp"),
        P("tp", "dp"),
        P("tp", "dp"),
        P(),
        P(),
        P(),
        P(),
        P(),
    )
    out_specs = (
        P(None, ("dp", "tp"), None),
        P(None, ("dp", "tp"), None),
        P("tp", "dp"),
        P("tp", "dp"),
        P("tp", "dp"),
        P(),
        P(),
        P(),
    )
    return jax.shard_map(body, mesh=mesh, in_specs=in_specs, out_specs=out_specs, check_vma=False)
```
